256 devices in a mesh: seq: 32 (over x, z), head: 8 (over y, core).
Axes of the slice: x: 4, y: 4, z: 8, core: 2. Of those that a mesh axis runs over, the one named last changes fastest.
Arguments:
- tokens: bfloat16 [32768, 3072], P(('seq', 'head')), may hold values from -150 to 150
- norm_gain: float32 [3072], replicated, may hold values from 0.1 to 1.9
- w_query: bfloat16 [3072, 3072], P(None, 'head'), may hold values from -0.15625 to 0.15625
- w_key: bfloat16 [3072, 1024], P(None, 'head'), may hold values from -0.15625 to 0.15625
- w_value: bfloat16 [3072, 1024], P(None, 'head'), may hold values from -0.109375 to 0.109375
- w_out: bfloat16 [3072, 3072], P('head'), may hold values from -1.5 to 1.5
- long_cache: bfloat16 [2, 32768, 1024], P(None, 'seq', 'head'), may hold values from -244 to 244
- short_cache: bfloat16 [2, 8192, 1024], P(None, 'seq', 'head'), may hold values from -244 to 244
- slot_owner: int32 [8192], P('seq'), may hold values from -1 to 63, as said below
- new_len: int32 [64], replicated, may hold values from 2 to 1024, as said below
- cache_len: int32 [64], replicated, may hold values from 32 to 85, as said below
Outputs:
- layer_out: bfloat16 [32768, 3072], P(('seq', 'head'))
The draws below stay inside these ranges and needn't reach their ends.
Inputs may be any that keep to these rules, and one draw needn't show every extreme that they name: `new_len`: lengths in order after the lead request's 64 tokens; they sum to 32704, and one request has exactly 1024 new tokens. `cache_len`: equals the number of short-cache slots that the request owns; one request has exactly 85. `slot_owner`: A request's slots are contiguous and lie in the block of 256 slots whose index equals that of the block of 1024 tokens holding the request's first new token.
All inputs are finite; a program needn't handle non-finite values.
Results may differ from the reference program's by a relative error of at most 0.02.
The reference program's roundings to bfloat16 on the way count: a program that leaves them out, or rounds other values in their place, can miss the bound.
Values may be sent and summed in bfloat16 or wider, within the bound.
A program may use at most 128 MiB of HBM per device.

```python
import math
import jax
import jax.numpy as jnp
from jax import lax

D = 3072
QH = 24
KVH = 8
HD = 128
TOK_DEV = 1024
SHORT_DEV = 256
TOKENS = 32768
LONG = 32768
SHORT = 8192
LEAD = 64
NREQ = 64
N_SEQ = 32
N_HEAD = 8


def request_layout(key):
    base = jax.random.fold_in(key, 7)
    half = TOK_DEV // 2
    spread = half // 2 - 2
    cut_number = jnp.arange(1, NREQ, dtype=jnp.int32)
    jitter = jax.random.randint(jax.random.fold_in(base, 1), (NREQ - 1,), -spread, spread + 1, dtype=jnp.int32)
    forced = jax.random.randint(jax.random.fold_in(base, 2), (), 2, NREQ, dtype=jnp.int32)
    jitter = jnp.where(cut_number == forced, half // 2, jitter)
    jitter = jnp.where(cut_number == forced - 1, -(half // 2), jitter)
    cuts = LEAD + cut_number * half + jitter
    bounds = jnp.concatenate([jnp.array([LEAD], dtype=jnp.int32), cuts.astype(jnp.int32), jnp.array([TOKENS], dtype=jnp.int32)])
    counts = (bounds[1:] - bounds[:-1]).astype(jnp.int32)
    lowest = SHORT_DEV // 8
    highest = SHORT_DEV // 3
    numbers = jnp.arange(NREQ, dtype=jnp.int32)
    lengths = jax.random.randint(jax.random.fold_in(base, 3), (NREQ,), lowest, highest + 1, dtype=jnp.int32)
    chosen = jax.random.randint(jax.random.fold_in(base, 4), (), 0, NREQ, dtype=jnp.int32)
    lengths = jnp.where(numbers == chosen, highest, lengths).astype(jnp.int32)
    owner_block = bounds[:-1] // TOK_DEV
    earlier = (owner_block[None, :] == owner_block[:, None]) & (numbers[None, :] < numbers[:, None])
    offsets = owner_block * SHORT_DEV + jnp.sum(jnp.where(earlier, lengths[None, :], 0), axis=1)
    slot_index = jnp.arange(SHORT, dtype=jnp.int32)
    inside = (slot_index[:, None] >= offsets[None, :]) & (slot_index[:, None] < (offsets + lengths)[None, :])
    owner = jnp.sum(jnp.where(inside, numbers[None, :] + 1, 0), axis=1) - 1
    return (counts, lengths, owner.astype(jnp.int32))


def draw_new_len(key, part):
    return request_layout(key)[0]


def draw_cache_len(key, part):
    return request_layout(key)[1]


def draw_slot_owner(key, part):
    return request_layout(key)[2]


def cache_pair(key, amount):
    width = KVH * HD
    keys = 3.0 * jax.random.truncated_normal(jax.random.fold_in(key, 11), -5.0, 5.0, (amount, width), jnp.float32)
    values = jax.random.truncated_normal(jax.random.fold_in(key, 13), -5.0, 5.0, (amount, width), jnp.float32)
    return jnp.stack([keys, values]).astype(jnp.bfloat16)


def draw_long_cache(key, part):
    return cache_pair(jax.random.fold_in(key, 21), LONG)


def draw_short_cache(key, part):
    return cache_pair(jax.random.fold_in(key, 22), SHORT)


def draw_tokens(key, part):
    row_scale = jnp.exp(jax.random.uniform(jax.random.fold_in(key, 1), (TOKENS, 1), jnp.float32, 0.0, math.log(10.0)))
    column_scale = jnp.exp(jax.random.uniform(jax.random.fold_in(key, 2), (1, D), jnp.float32, math.log(0.3), math.log(3.0)))
    noise = jax.random.truncated_normal(jax.random.fold_in(key, 4), -5.0, 5.0, (TOKENS, D), jnp.float32)
    return (noise * row_scale * column_scale).astype(jnp.bfloat16)


def levels(stream_key, extent, pieces, smallest, largest):
    level = 1.0
    for axis_at, shards_of in pieces:
        steps = jax.random.uniform(jax.random.fold_in(jax.random.fold_in(stream_key, 6), axis_at), (shards_of,), jnp.float32, smallest / len(pieces), largest / len(pieces))
        level = level * jnp.repeat(jnp.exp(steps), extent[axis_at] // shards_of).reshape((-1,) + (1,) * (len(extent) - 1 - axis_at))
    return level


def centred(stream_key, extent, scale, most, split=(), kind=jnp.bfloat16):
    drawn = scale * jax.random.normal(stream_key, extent, jnp.float32)
    if split:
        drawn = drawn * levels(stream_key, extent, split, -0.22, 0.18)
    return jnp.clip(drawn, -most, most).astype(kind)


def setup_inputs(seed: int = 0) -> dict:
    streams_of = jax.random.split(jax.random.key(seed), 12)
    return {
        "tokens": draw_tokens(jax.random.fold_in(streams_of[11], 71), 0),
        "norm_gain": jnp.clip(1.0 + 0.18 * jax.random.normal(streams_of[1], (D,), jnp.float32), 0.1, 1.9),
        "w_query": centred(streams_of[2], (D, QH * HD), (D // 2) ** -0.5, 0.15625, ((1, 8),)),
        "w_key": centred(streams_of[3], (D, KVH * HD), (D // 2) ** -0.5, 0.15625, ((1, 8),)),
        "w_value": centred(streams_of[4], (D, KVH * HD), D ** -0.5, 0.109375, ((1, 8),)),
        "w_out": centred(streams_of[5], (QH * HD, D), 16 ** -0.5, 1.5, ((0, 8),)),
        "long_cache": draw_long_cache(jax.random.fold_in(streams_of[11], 71), 0),
        "short_cache": draw_short_cache(jax.random.fold_in(streams_of[11], 71), 0),
        "slot_owner": draw_slot_owner(jax.random.fold_in(streams_of[11], 71), 0),
        "new_len": draw_new_len(jax.random.fold_in(streams_of[11], 71), 0),
        "cache_len": draw_cache_len(jax.random.fold_in(streams_of[11], 71), 0),
    }


THETA_LOG = math.log(500000.0)

def rotate(field, position):
    half = field.shape[-1] // 2
    frequency = jnp.exp(jnp.arange(half, dtype=jnp.float32) * (-2.0 * THETA_LOG / field.shape[-1]))
    angle = position.astype(jnp.float32)[:, None] * frequency[None, :]
    cosine = jnp.cos(angle)[:, None, :]
    sine_part = jnp.sin(angle)[:, None, :]
    first_half = field[..., :half]
    second_half = field[..., half:]
    return jnp.concatenate([first_half * cosine - second_half * sine_part, second_half * cosine + first_half * sine_part], axis=-1)

def request_starts(new_len):
    return (LEAD + jnp.cumsum(new_len).astype(jnp.int32) - new_len).astype(jnp.int32)

def request_of(position_index, starts):
    passed = (starts[None, :] <= position_index[:, None]).astype(jnp.int32)
    request = lax.optimization_barrier(jnp.sum(passed, axis=1)).astype(jnp.int32) - 1
    return jnp.where(request < 0, starts.shape[0], request).astype(jnp.int32)

def position_of(position_index, request, starts, cache_len, long_len):
    number = starts.shape[0]
    select = jnp.arange(number, dtype=jnp.int32)[None, :] == request[:, None]
    begin = lax.optimization_barrier(jnp.sum(jnp.where(select, starts[None, :], 0), axis=1)).astype(jnp.int32)
    cached = lax.optimization_barrier(jnp.sum(jnp.where(select, cache_len[None, :], 0), axis=1)).astype(jnp.int32)
    return jnp.where(request == number, position_index + long_len, position_index - begin + cached).astype(jnp.int32)

def normalize(tokens, norm_gain):
    values = tokens.astype(jnp.float32)
    mean_square = lax.optimization_barrier(jnp.mean(values * values, axis=-1, keepdims=True))
    return (values * lax.rsqrt(mean_square + 1e-05) * norm_gain).astype(jnp.bfloat16)

def attend(queries, keys, values, valid):
    scores = jnp.einsum('bgph,ngh->bgpn', queries.astype(jnp.float32), keys.astype(jnp.float32)) * (1.0 / math.sqrt(keys.shape[-1]))
    scores = jnp.where(valid[:, None, None, :], scores, -jnp.inf)
    highest = lax.optimization_barrier(jnp.max(scores, axis=-1, keepdims=True))
    weights = jnp.exp(scores - highest)
    summed = lax.optimization_barrier(jnp.sum(weights, axis=-1))
    rounded = lax.optimization_barrier(weights.astype(jnp.bfloat16))
    mixture = jnp.einsum('bgpn,ngh->bgph', rounded.astype(jnp.float32), values.astype(jnp.float32))
    return (mixture / summed[..., None]).astype(jnp.bfloat16)

def take_rows(array, begin, amount):
    return lax.dynamic_slice_in_dim(array, begin, amount, 0)

def reference(tokens, norm_gain, w_query, w_key, w_value, w_out, long_cache, short_cache, slot_owner, new_len, cache_len):
    per_kv = QH // KVH
    starts = request_starts(new_len)
    token_index = jnp.arange(TOKENS, dtype=jnp.int32)
    request = request_of(token_index, starts)
    position = position_of(token_index, request, starts, cache_len, LONG)
    normed = normalize(tokens, norm_gain)
    queries = rotate(jnp.dot(normed, w_query, preferred_element_type=jnp.float32).reshape(TOKENS, QH, HD), position).astype(jnp.bfloat16)
    queries = queries.reshape(TOKENS, KVH, per_kv, HD)
    keys = rotate(jnp.dot(normed, w_key, preferred_element_type=jnp.float32).reshape(TOKENS, KVH, HD), position).astype(jnp.bfloat16)
    values = jnp.dot(normed, w_value, preferred_element_type=jnp.float32).astype(jnp.bfloat16).reshape(TOKENS, KVH, HD)
    cache_keys = short_cache[0].reshape(SHORT, KVH, HD)
    cache_values = short_cache[1].reshape(SHORT, KVH, HD)
    cache_index = jnp.full((2 * SHORT_DEV,), -1, jnp.int32)

    def local_keys(block):
        here = (block * TOK_DEV).astype(jnp.int32)
        before = (jnp.maximum(block - 1, 0) * TOK_DEV).astype(jnp.int32)
        slot_here = (block * SHORT_DEV).astype(jnp.int32)
        slot_before = (jnp.maximum(block - 1, 0) * SHORT_DEV).astype(jnp.int32)
        has_before = block > 0
        key_rows = jnp.concatenate([take_rows(keys, before, TOK_DEV), take_rows(keys, here, TOK_DEV), take_rows(cache_keys, slot_before, SHORT_DEV), take_rows(cache_keys, slot_here, SHORT_DEV)], axis=0)
        value_rows = jnp.concatenate([take_rows(values, before, TOK_DEV), take_rows(values, here, TOK_DEV), take_rows(cache_values, slot_before, SHORT_DEV), take_rows(cache_values, slot_here, SHORT_DEV)], axis=0)
        key_request = jnp.concatenate([jnp.where(has_before, take_rows(request, before, TOK_DEV), -1), take_rows(request, here, TOK_DEV), jnp.where(has_before, take_rows(slot_owner, slot_before, SHORT_DEV), -1), take_rows(slot_owner, slot_here, SHORT_DEV)]).astype(jnp.int32)
        key_index = jnp.concatenate([take_rows(token_index, before, TOK_DEV), take_rows(token_index, here, TOK_DEV), cache_index]).astype(jnp.int32)
        return (key_rows, value_rows, key_request, key_index)

    def block_out(block):
        key_rows, value_rows, key_request, key_index = local_keys(block)
        here = (block * TOK_DEV).astype(jnp.int32)
        query_request = take_rows(request, here, TOK_DEV)
        query_index = take_rows(token_index, here, TOK_DEV)
        valid = (key_request[None, :] == query_request[:, None]) & (key_index[None, :] <= query_index[:, None])
        return attend(take_rows(queries, here, TOK_DEV), key_rows, value_rows, valid)
    attended = lax.map(block_out, jnp.arange(N_SEQ, dtype=jnp.int32)).reshape(TOKENS, KVH, per_kv, HD)
    key_rows, value_rows, key_request, key_index = local_keys(jnp.int32(0))
    lead_valid = (key_request[None, :] == request[:LEAD, None]) & (key_index[None, :] <= token_index[:LEAD, None])
    all_valid = jnp.concatenate([jnp.ones((LEAD, LONG), dtype=bool), lead_valid], axis=1)
    all_keys = jnp.concatenate([long_cache[0].reshape(LONG, KVH, HD), key_rows], axis=0)
    all_values = jnp.concatenate([long_cache[1].reshape(LONG, KVH, HD), value_rows], axis=0)
    lead_out = attend(queries[:LEAD], all_keys, all_values, all_valid)
    attended = attended.at[:LEAD].set(lead_out).reshape(TOKENS, QH * HD)
    width = QH * HD // N_HEAD
    summed = jnp.zeros((TOKENS, D), jnp.float32)
    for group in range(N_HEAD):
        partial_out = jnp.dot(attended[:, group * width:(group + 1) * width], w_out[group * width:(group + 1) * width], preferred_element_type=jnp.float32).astype(jnp.bfloat16)
        summed = summed + lax.optimization_barrier(partial_out).astype(jnp.float32)
    return summed.astype(jnp.bfloat16)
```

```python
import math

import jax
import jax.numpy as jnp
from jax import lax
from jax.experimental import pallas as pl
from jax.experimental.pallas import tpu as pltpu
from jax.sharding import PartitionSpec as P

HD = 128
LEAD = 64
THETA_LOG = math.log(500000.0)
SCALE = 1.0 / math.sqrt(HD)
LOW = -1e30
TILE = 256


def from_behind(block, axis, distance):
    devices = range(lax.axis_size(axis))
    route = [(i - distance, i) for i in devices if i - distance in devices]
    return lax.ppermute(block, axis, route)


def request_starts(new_len):
    return LEAD + jnp.cumsum(new_len) - new_len


def token_facts(token_index, starts, cache_len, long_len):
    number = starts.shape[0]
    passed = (starts[None, :] <= token_index[:, None]).astype(jnp.int32)
    request = jnp.sum(passed, axis=1) - 1
    select = jnp.arange(number, dtype=jnp.int32)[None, :] == request[:, None]
    begin = jnp.sum(jnp.where(select, starts[None, :], 0), axis=1)
    cached = jnp.sum(jnp.where(select, cache_len[None, :], 0), axis=1)
    lead = request < 0
    position = jnp.where(lead, token_index + long_len, token_index - begin + cached)
    return jnp.where(lead, number, request), begin, position


def normalize(tokens, norm_gain):
    values = tokens.astype(jnp.float32)
    mean_square = jnp.mean(values * values, axis=-1, keepdims=True)
    return (values * lax.rsqrt(mean_square + 1e-05) * norm_gain).astype(jnp.bfloat16)


def rotate_tables(position):
    half = HD // 2
    frequency = jnp.exp(jnp.arange(half, dtype=jnp.float32) * (-2.0 * THETA_LOG / HD))
    angle = position.astype(jnp.float32)[:, None] * frequency[None, :]
    cosine = jnp.cos(angle)
    sine = jnp.sin(angle)
    return (
        jnp.concatenate([cosine, cosine], axis=1),
        jnp.concatenate([-sine, sine], axis=1),
    )


def dot32(a, b):
    return jnp.dot(a, b, preferred_element_type=jnp.float32)


def dot_t(a, b):
    return lax.dot_general(a, b, (((1,), (1,)), ((), ())), preferred_element_type=jnp.float32)


def kv_kernel(x_ref, wk_ref, wv_ref, cos_ref, sin_ref, kv_ref):
    x = x_ref[...]
    key = dot32(x, wk_ref[...])
    kv_ref[0] = (key * cos_ref[...] + pltpu.roll(key, HD // 2, 1) * sin_ref[...]).astype(jnp.bfloat16)
    kv_ref[1] = dot32(x, wv_ref[...]).astype(jnp.bfloat16)


def q_kernel(x_ref, wq_ref, cos_ref, sin_ref, q_ref):
    product = dot32(x_ref[...], wq_ref[...])
    cosine = cos_ref[...]
    sine = sin_ref[...]
    for head in range(q_ref.shape[0]):
        query = product[:, head * HD : (head + 1) * HD]
        q_ref[head] = (query * cosine + pltpu.roll(query, HD // 2, 1) * sine).astype(jnp.bfloat16)


def project_kv(x, w_key, w_value, cosine, sine):
    rows, width = x.shape
    tile = TILE
    return pl.pallas_call(
        kv_kernel,
        grid=(rows // tile,),
        in_specs=[
            pl.BlockSpec((tile, width), lambda i: (i, 0)),
            pl.BlockSpec(w_key.shape, lambda i: (0, 0)),
            pl.BlockSpec(w_value.shape, lambda i: (0, 0)),
            pl.BlockSpec((tile, HD), lambda i: (i, 0)),
            pl.BlockSpec((tile, HD), lambda i: (i, 0)),
        ],
        out_specs=pl.BlockSpec((2, tile, HD), lambda i: (0, i, 0)),
        out_shape=jax.ShapeDtypeStruct((2, rows, HD), jnp.bfloat16),
        cost_estimate=pl.CostEstimate(
            flops=4 * rows * width * HD, bytes_accessed=rows * width * 2, transcendentals=0
        ),
        name="project_kv",
    )(x, w_key, w_value, cosine, sine)


def project_q(x, w_query, cosine, sine):
    rows, width = x.shape
    heads = w_query.shape[1] // HD
    tile = TILE
    return pl.pallas_call(
        q_kernel,
        grid=(rows // tile,),
        in_specs=[
            pl.BlockSpec((tile, width), lambda i: (i, 0)),
            pl.BlockSpec(w_query.shape, lambda i: (0, 0)),
            pl.BlockSpec((tile, HD), lambda i: (i, 0)),
            pl.BlockSpec((tile, HD), lambda i: (i, 0)),
        ],
        out_specs=pl.BlockSpec((heads, tile, HD), lambda i: (0, i, 0)),
        out_shape=jax.ShapeDtypeStruct((heads, rows, HD), jnp.bfloat16),
        cost_estimate=pl.CostEstimate(
            flops=2 * heads * rows * width * HD, bytes_accessed=rows * width * 2, transcendentals=0
        ),
        name="project_q",
    )(x, w_query, cosine, sine)


def local_kernel(
    first_ref,
    q_ref,
    before_ref,
    here_ref,
    slot_before_ref,
    slot_here_ref,
    owner_ref,
    facts_ref,
    out_ref,
    lead_mix_ref,
    lead_top_ref,
    lead_sum_ref,
    window,
    top_ref,
    sum_ref,
    mix_ref,
):
    step = pl.program_id(0)
    rows = here_ref.shape[1]
    slots = slot_here_ref.shape[1]
    heads, tile, _ = q_ref.shape

    @pl.when(step == 0)
    def _():
        window[:, pl.ds(0, rows)] = before_ref[...]
        window[:, pl.ds(rows, rows)] = here_ref[...]
        window[:, pl.ds(2 * rows, slots)] = slot_before_ref[...]
        window[:, pl.ds(2 * rows + slots, slots)] = slot_here_ref[...]

    request = facts_ref[:, 0:1]
    begin = facts_ref[:, 1:2]
    index = facts_ref[:, 2:3]

    def take(keys, values, valid, fresh):
        for head in range(heads):
            scores = jnp.where(valid, dot_t(q_ref[head], keys) * SCALE, LOW)
            top = jnp.max(scores, axis=1, keepdims=True)
            if not fresh:
                old = top_ref[head]
                top = jnp.maximum(top, old)
                keep = jnp.exp(old - top)
            weights = jnp.exp(scores - top)
            total = jnp.sum(weights, axis=1, keepdims=True)
            mixed = dot32(weights.astype(jnp.bfloat16), values)
            top_ref[head] = top
            if fresh:
                sum_ref[head] = total
                mix_ref[head] = mixed
            else:
                sum_ref[head] = sum_ref[head] * keep + total
                mix_ref[head] = mix_ref[head] * keep + mixed

    def new_chunk(number, fresh):
        at = pl.multiple_of(number * tile, tile)
        key_at = at + lax.broadcasted_iota(jnp.int32, (tile, tile), 1)
        valid = (key_at >= begin) & (key_at <= index)
        take(window[0, pl.ds(at, tile), :], window[1, pl.ds(at, tile), :], valid, fresh)

    last = rows // tile + step
    new_chunk(last, True)
    first = first_ref[step]

    @pl.loop(first, last)
    def _(number):
        new_chunk(number, False)

    valid = owner_ref[...] == request
    take(window[0, pl.ds(2 * rows, 2 * slots), :], window[1, pl.ds(2 * rows, 2 * slots), :], valid, False)
    for head in range(heads):
        out_ref[:, head * HD : (head + 1) * HD] = (mix_ref[head] / sum_ref[head]).astype(jnp.bfloat16)

    @pl.when(step == 0)
    def _():
        lead_mix_ref[...] = mix_ref[:, pl.ds(0, LEAD), :]
        lead_top_ref[...] = jnp.broadcast_to(top_ref[:, pl.ds(0, LEAD), :], lead_top_ref.shape)
        lead_sum_ref[...] = jnp.broadcast_to(sum_ref[:, pl.ds(0, LEAD), :], lead_sum_ref.shape)


def local_attention(first, queries, before, here, slot_before, slot_here, owner, facts):
    heads, rows, _ = queries.shape
    slots = slot_here.shape[1]
    tile = TILE

    def whole(array):
        return pl.BlockSpec(array.shape, lambda i, first: (0,) * array.ndim)

    lead_shape = jax.ShapeDtypeStruct((heads, LEAD, HD), jnp.float32)
    return pl.pallas_call(
        local_kernel,
        grid_spec=pltpu.PrefetchScalarGridSpec(
            num_scalar_prefetch=1,
            grid=(rows // tile,),
            in_specs=[
                pl.BlockSpec((heads, tile, HD), lambda i, first: (0, i, 0)),
                whole(before),
                whole(here),
                whole(slot_before),
                whole(slot_here),
                whole(owner),
                pl.BlockSpec((tile, facts.shape[1]), lambda i, first: (i, 0)),
            ],
            out_specs=[
                pl.BlockSpec((tile, heads * HD), lambda i, first: (i, 0)),
                whole(lead_shape),
                whole(lead_shape),
                whole(lead_shape),
            ],
            scratch_shapes=[
                pltpu.VMEM((2, 2 * rows + 2 * slots, HD), jnp.bfloat16),
                pltpu.VMEM((heads, tile, 1), jnp.float32),
                pltpu.VMEM((heads, tile, 1), jnp.float32),
                pltpu.VMEM((heads, tile, HD), jnp.float32),
            ],
        ),
        out_shape=[
            jax.ShapeDtypeStruct((rows, heads * HD), jnp.bfloat16),
            lead_shape,
            lead_shape,
            lead_shape,
        ],
        cost_estimate=pl.CostEstimate(
            flops=4 * heads * rows * (rows + 2 * slots) * HD,
            bytes_accessed=8 * rows * HD * heads,
            transcendentals=heads * rows * (rows + 2 * slots),
        ),
        name="local_attention",
    )(first, queries, before, here, slot_before, slot_here, owner, facts)


def long_kernel(q_ref, cache_ref, mix_ref, top_ref, sum_ref):
    for head in range(q_ref.shape[0]):
        scores = dot_t(q_ref[head], cache_ref[0]) * SCALE
        top = jnp.max(scores, axis=1, keepdims=True)
        weights = jnp.exp(scores - top)
        mix_ref[head] = dot32(weights.astype(jnp.bfloat16), cache_ref[1])
        top_ref[head] = jnp.broadcast_to(top, top_ref.shape[1:])
        sum_ref[head] = jnp.broadcast_to(jnp.sum(weights, axis=1, keepdims=True), sum_ref.shape[1:])


def long_part(lead_queries, cache):
    shape = jax.ShapeDtypeStruct(lead_queries.shape, jnp.float32)
    return pl.pallas_call(
        long_kernel,
        out_shape=[shape, shape, shape],
        cost_estimate=pl.CostEstimate(
            flops=4 * 192 * cache.shape[1] * HD, bytes_accessed=cache.size * 2, transcendentals=192 * 1024
        ),
        name="long_part",
    )(lead_queries, cache)


def on_device(
    tokens,
    norm_gain,
    w_query,
    w_key,
    w_value,
    w_out,
    long_cache,
    short_cache,
    slot_owner,
    new_len,
    cache_len,
):
    seq_index = lax.axis_index("seq")
    long_len = long_cache.shape[1] * lax.axis_size("seq")
    heads = w_query.shape[1] // HD
    earlier_slots, earlier_owner = from_behind((short_cache, slot_owner), "seq", 1)
    normed = normalize(tokens, norm_gain)
    piece = lax.all_gather(normed, "head", axis=0, tiled=True)
    rows = piece.shape[0]
    starts = request_starts(new_len)
    token_index = seq_index * rows + jnp.arange(rows, dtype=jnp.int32)
    request, begin, position = token_facts(token_index, starts, cache_len, long_len)
    cosine, sine = rotate_tables(position)
    here = project_kv(piece, w_key, w_value, cosine, sine)
    before = from_behind(here, "seq", 1)
    queries = project_q(piece, w_query, cosine, sine)

    lead_queries = queries[:, :LEAD]
    lead_queries = lax.psum(jnp.where(seq_index == 0, lead_queries, jnp.zeros_like(lead_queries)), "seq")
    long_mix, long_top, long_sum = long_part(lead_queries, long_cache)
    long_high = lax.pmax(long_top[:, :, 0], "seq")
    shrink = jnp.exp(long_top[:, :, 0] - long_high)
    packed = jnp.concatenate(
        [long_mix * shrink[..., None], jnp.tile((long_sum[:, :, 0] * shrink)[:, None, :], (1, 1, HD // LEAD))],
        axis=1,
    )
    packed = lax.psum(packed, "seq")
    long_mix = packed[:, :LEAD]
    long_sum = packed[:, LEAD, :LEAD]

    shift = (seq_index - 1) * rows
    window_begin = jnp.maximum(begin - shift, 0)
    window_index = token_index - shift
    window_begin = jnp.where(request == starts.shape[0], -shift, window_begin)
    facts = jnp.stack([request, window_begin, window_index] + [window_index] * 5, axis=1)
    owner = jnp.concatenate([jnp.where(seq_index > 0, earlier_owner, -1), slot_owner])[None, :]
    first = window_begin[::TILE] // TILE
    attended, lead_mix, lead_top, lead_sum = local_attention(
        first, queries, before, here, earlier_slots, short_cache, owner, facts
    )
    lead_top = lead_top[:, :, 0]
    lead_sum = lead_sum[:, :, 0]
    highest = jnp.maximum(lead_top, long_high)
    scale_near = jnp.exp(lead_top - highest)
    scale_long = jnp.exp(long_high - highest)
    total = lead_sum * scale_near + long_sum * scale_long
    mixture = lead_mix * scale_near[..., None] + long_mix * scale_long[..., None]
    lead_out = (mixture / total[..., None]).astype(jnp.bfloat16)
    lead_out = jnp.transpose(lead_out, (1, 0, 2)).reshape(LEAD, heads * HD)
    lead_out = jnp.where(seq_index == 0, lead_out, attended[:LEAD])
    attended = lax.dynamic_update_slice(attended, lead_out, (0, 0))
    return lax.psum_scatter(
        dot32(attended, w_out).astype(jnp.bfloat16), "head", scatter_dimension=0, tiled=True
    )


def solution(mesh):
    placed = (
        P(("seq", "head"), None),
        P(),
        P(None, "head"),
        P(None, "head"),
        P(None, "head"),
        P("head", None),
        P(None, "seq", "head"),
        P(None, "seq", "head"),
        P("seq"),
        P(),
        P(),
    )
    return jax.shard_map(
        on_device, mesh=mesh, in_specs=placed, out_specs=P(("seq", "head"), None), check_vma=False
    )
```

```python
import math

import jax
import jax.numpy as jnp
from jax import lax
from jax.experimental import pallas as pl
from jax.experimental.pallas import tpu as pltpu
from jax.sharding import PartitionSpec as P

HD = 128
LEAD = 64
THETA_LOG = math.log(500000.0)
SCALE = 1.0 / math.sqrt(HD)
LOW = -1e30
TILE = 256


def from_behind(block, axis, distance):
    devices = range(lax.axis_size(axis))
    route = [(i - distance, i) for i in devices if i - distance in devices]
    return lax.ppermute(block, axis, route)


def request_starts(new_len):
    return LEAD + jnp.cumsum(new_len) - new_len


def token_facts(token_index, starts, cache_len, long_len):
    number = starts.shape[0]
    passed = (starts[None, :] <= token_index[:, None]).astype(jnp.int32)
    request = jnp.sum(passed, axis=1) - 1
    select = jnp.arange(number, dtype=jnp.int32)[None, :] == request[:, None]
    begin = jnp.sum(jnp.where(select, starts[None, :], 0), axis=1)
    cached = jnp.sum(jnp.where(select, cache_len[None, :], 0), axis=1)
    lead = request < 0
    position = jnp.where(lead, token_index + long_len, token_index - begin + cached)
    return jnp.where(lead, number, request), begin, position


def normalize(tokens, norm_gain):
    values = tokens.astype(jnp.float32)
    mean_square = jnp.mean(values * values, axis=-1, keepdims=True)
    return (values * lax.rsqrt(mean_square + 1e-05) * norm_gain).astype(jnp.bfloat16)


def rotate_tables(position):
    half = HD // 2
    frequency = jnp.exp(jnp.arange(half, dtype=jnp.float32) * (-2.0 * THETA_LOG / HD))
    angle = position.astype(jnp.float32)[:, None] * frequency[None, :]
    cosine = jnp.cos(angle)
    sine = jnp.sin(angle)
    return (
        jnp.concatenate([cosine, cosine], axis=1),
        jnp.concatenate([-sine, sine], axis=1),
    )


def dot32(a, b):
    return jnp.dot(a, b, preferred_element_type=jnp.float32)


def dot_t(a, b):
    return lax.dot_general(a, b, (((1,), (1,)), ((), ())), preferred_element_type=jnp.float32)


MESH = pl.DeviceIdType.MESH
LIMIT = 60 * 1024 * 1024
Z = 8
Y = 4
UNITS = [(0, 0), (0, 1), (1, 0), (3, 0), (1, 1), (2, 0), (2, 1), (3, 1)]
SLOT = {unit: number for number, unit in enumerate(UNITS)}


def place():
    seq = lax.axis_index("seq")
    head = lax.axis_index("head")
    return seq, head, head // 2, lax.rem(head, 2)


def pick(number, table):
    value = jnp.int32(table[0])
    for at, entry in enumerate(table):
        value = jnp.where(number == at, jnp.int32(entry), value)
    return value


def greet(device):
    pl.semaphore_signal(
        pltpu.get_barrier_semaphore(), inc=1, device_id=device, device_id_type=MESH
    )


def gather_kernel(
    normed_ref,
    wq_ref,
    wk_ref,
    wv_ref,
    cos_ref,
    sin_ref,
    slots_ref,
    owner_ref,
    q_ref,
    kv_ref,
    before_ref,
    slots_before_ref,
    owner_before_ref,
    lead_ref,
    held,
    ring_send,
    ring_recv,
    pair_send,
    pair_recv,
    kv_send,
    kv_recv,
    slot_send,
    slot_recv,
    lead_send,
    lead_recv,
):
    seq, head, y, core = place()
    n_seq = lax.axis_size("seq")
    x, z = seq // Z, lax.rem(seq, Z)
    way = 1 - 2 * core
    right = (seq, lax.rem(y + way + Y, Y) * 2 + core)
    left = (seq, lax.rem(y - way + Y, Y) * 2 + core)
    pair = (seq, head + way)
    following = (lax.rem(seq + 1, n_seq), head)
    previous = (lax.rem(seq + n_seq - 1, n_seq), head)
    heads = q_ref.shape[0]
    half = held.shape[2]

    for device in (right, left, pair, following, previous):
        greet(device)

    @pl.when(seq == 0)
    def _():
        for to in range(1, Z):
            greet((to, head))

    @pl.when(x == 0)
    def _():
        for to in range(1, n_seq // Z):
            greet((to * Z + z, head))

    @pl.when((x == 0) & (z > 0))
    def _():
        greet((0, head))

    @pl.when(x > 0)
    def _():
        greet((z, head))

    barrier = pltpu.get_barrier_semaphore()
    others = n_seq // Z - 1

    @pl.when(seq == 0)
    def _():
        pl.semaphore_wait(barrier, 5 + Z - 1 + others)

    @pl.when((x == 0) & (z > 0))
    def _():
        pl.semaphore_wait(barrier, 5 + 1 + others)

    @pl.when(x > 0)
    def _():
        pl.semaphore_wait(barrier, 5 + 1)

    def ring(number, source, to, unit):
        slot = SLOT[unit]
        return pltpu.make_async_remote_copy(
            src_ref=source,
            dst_ref=held.at[slot, core],
            send_sem=ring_send.at[number],
            recv_sem=ring_recv.at[slot],
            device_id=to,
            device_id_type=MESH,
        )

    def mine(unit):
        return held.at[SLOT[unit], core]

    def to_pair(unit):
        slot = SLOT[unit]
        return pltpu.make_async_remote_copy(
            src_ref=normed_ref.at[unit[1]] if unit[0] == 0 else mine(unit),
            dst_ref=held.at[slot, core],
            send_sem=pair_send.at[slot],
            recv_sem=pair_recv.at[slot],
            device_id=pair,
            device_id_type=MESH,
        )

    rings = [
        ring(0, normed_ref.at[0], right, (1, 0)),
        ring(1, normed_ref.at[0], left, (3, 0)),
        ring(2, normed_ref.at[1], right, (1, 1)),
        ring(3, mine((1, 0)), right, (2, 0)),
        ring(4, mine((1, 1)), right, (2, 1)),
        ring(5, mine((2, 1)), right, (3, 1)),
    ]
    pairs = {unit: to_pair(unit) for unit in UNITS}
    side = [
        pltpu.make_async_remote_copy(
            src_ref=source,
            dst_ref=target,
            send_sem=slot_send.at[number],
            recv_sem=slot_recv.at[number],
            device_id=following,
            device_id_type=MESH,
        )
        for number, (source, target) in enumerate(
            [(slots_ref, slots_before_ref), (owner_ref, owner_before_ref)]
        )
    ]

    def lead_copy(number, to):
        return pltpu.make_async_remote_copy(
            src_ref=lead_ref,
            dst_ref=lead_ref,
            send_sem=lead_send.at[number],
            recv_sem=lead_recv,
            device_id=(to, head),
            device_id_type=MESH,
        )

    along_z = [lead_copy(to - 1, jnp.int32(to)) for to in range(1, Z)]
    along_x = [lead_copy(Z - 2 + to, to * Z + z) for to in range(1, n_seq // Z)]

    def row_starts(number):
        distance = pick(number, [unit[0] for unit in UNITS])
        later = pick(number, [unit[1] for unit in UNITS])
        first = lax.rem(y - distance + Y, Y) * (4 * half) + later * half
        second = lax.rem(y + distance, Y) * (4 * half) + 2 * half + later * half
        return pl.multiple_of(first, half), pl.multiple_of(second, half)

    def kv_copies(number):
        return [
            pltpu.make_async_remote_copy(
                src_ref=kv_ref.at[:, pl.ds(start, half), :],
                dst_ref=before_ref.at[:, pl.ds(start, half), :],
                send_sem=kv_send.at[2 * number + part],
                recv_sem=kv_recv.at[2 * number + part],
                device_id=following,
                device_id_type=MESH,
            )
            for part, start in enumerate(row_starts(number))
        ]

    rings[0].start()
    pairs[(0, 0)].start()
    rings[1].start()
    rings[2].start()
    pairs[(0, 1)].start()
    for copy in side:
        copy.start()
    for later in range(2):
        held[SLOT[(0, later)], core] = normed_ref[later]

    def event_0():
        pairs[(0, 0)].wait_recv()

    def event_1():
        pairs[(0, 1)].wait_recv()

    def event_2():
        rings[0].wait_recv()
        rings[3].start()
        pairs[(1, 0)].start()
        pairs[(1, 0)].wait_recv()

    def event_3():
        rings[1].wait_recv()
        pairs[(3, 0)].start()
        rings[2].wait_recv()
        rings[4].start()
        pairs[(1, 1)].start()
        pairs[(3, 0)].wait_recv()

    def event_4():
        pairs[(1, 1)].wait_recv()

    def event_5():
        rings[3].wait_recv()
        pairs[(2, 0)].start()
        pairs[(2, 0)].wait_recv()

    def event_6():
        @pl.when(seq == 0)
        def _():
            lead_ref[...] = q_ref[:, pl.ds(0, LEAD), :]
            for copy in along_z:
                copy.start()
            for copy in along_x:
                copy.start()

        rings[4].wait_recv()
        rings[5].start()
        pairs[(2, 1)].start()
        pairs[(2, 1)].wait_recv()

    def event_7():
        rings[5].wait_recv()
        pairs[(3, 1)].start()

        @pl.when((x == 0) & (z > 0))
        def _():
            along_z[0].wait_recv()
            for copy in along_x:
                copy.start()

        pairs[(3, 1)].wait_recv()

    events = [event_0, event_1, event_2, event_3, event_4, event_5, event_6, event_7]

    @pl.loop(0, len(UNITS))
    def _(number):
        for at, event in enumerate(events):
            pl.when(number == at)(event)
        block = held[number].reshape(2 * half, held.shape[3])
        starts = row_starts(number)
        cosine = jnp.concatenate([cos_ref[pl.ds(start, half), :] for start in starts], axis=0)
        sine = jnp.concatenate([sin_ref[pl.ds(start, half), :] for start in starts], axis=0)

        def turned(product):
            return (product * cosine + pltpu.roll(product, HD // 2, 1) * sine).astype(jnp.bfloat16)

        def put(ref, at, rows):
            for part, start in enumerate(starts):
                ref[at, pl.ds(start, half), :] = rows[part * half : (part + 1) * half]

        both = dot32(block, jnp.concatenate([wk_ref[...], wv_ref[...]], axis=1))
        put(kv_ref, 0, turned(both[:, :HD]))
        put(kv_ref, 1, both[:, HD:].astype(jnp.bfloat16))
        product = dot32(block, wq_ref[...])
        for at in range(heads):
            put(q_ref, at, turned(product[:, at * HD : (at + 1) * HD]))
        for copy in kv_copies(number):
            copy.start()

    @pl.loop(0, len(UNITS))
    def _(number):
        for copy in kv_copies(number):
            copy.wait_recv()
            copy.wait_send()

    for copy in rings:
        copy.wait_send()
    for unit in UNITS:
        pairs[unit].wait_send()
    for copy in side:
        copy.wait_recv()
        copy.wait_send()

    @pl.when(seq == 0)
    def _():
        for copy in along_z:
            copy.wait_send()

    @pl.when(x == 0)
    def _():
        for copy in along_x:
            copy.wait_send()

    @pl.when(x > 0)
    def _():
        along_x[0].wait_recv()


def gather_project(normed, w_query, w_key, w_value, cosine, sine, slots, owner):
    rows, width = cosine.shape[0], normed.shape[-1]
    heads = w_query.shape[1] // HD
    half = normed.shape[1]
    vmem = pl.BlockSpec(memory_space=pltpu.VMEM)
    dma = pltpu.SemaphoreType.DMA
    shape = jax.ShapeDtypeStruct
    return pl.pallas_call(
        gather_kernel,
        in_specs=[vmem] * 8,
        out_specs=[vmem] * 6,
        out_shape=[
            shape((heads, rows, HD), jnp.bfloat16),
            shape((2, rows, HD), jnp.bfloat16),
            shape((2, rows, HD), jnp.bfloat16),
            shape(slots.shape, jnp.bfloat16),
            shape(owner.shape, jnp.int32),
            shape((heads, LEAD, HD), jnp.bfloat16),
        ],
        scratch_shapes=[
            pltpu.VMEM((len(UNITS), 2, half, width), jnp.bfloat16),
            dma((6,)),
            dma((len(UNITS),)),
            dma((len(UNITS),)),
            dma((len(UNITS),)),
            dma((2 * len(UNITS),)),
            dma((2 * len(UNITS),)),
            dma((2,)),
            dma((2,)),
            dma((Z + 2,)),
            dma,
        ],
        compiler_params=pltpu.CompilerParams(
            collective_id=0, has_side_effects=True, vmem_limit_bytes=LIMIT
        ),
        name="gather_project",
    )(normed, w_query, w_key, w_value, cosine, sine, slots, owner)


def local_kernel(
    first_ref,
    q_ref,
    before_ref,
    here_ref,
    slot_before_ref,
    slot_here_ref,
    owner_ref,
    facts_ref,
    out_ref,
    lead_mix_ref,
    lead_top_ref,
    lead_sum_ref,
    window,
    top_ref,
    sum_ref,
    mix_ref,
):
    step = pl.program_id(0)
    rows = here_ref.shape[1]
    slots = slot_here_ref.shape[1]
    heads, tile, _ = q_ref.shape

    @pl.when(step == 0)
    def _():
        window[:, pl.ds(0, rows)] = before_ref[...]
        window[:, pl.ds(rows, rows)] = here_ref[...]
        window[:, pl.ds(2 * rows, slots)] = slot_before_ref[...]
        window[:, pl.ds(2 * rows + slots, slots)] = slot_here_ref[...]

    request = facts_ref[:, 0:1]
    begin = facts_ref[:, 1:2]
    index = facts_ref[:, 2:3]

    def take(keys, values, valid, fresh):
        for head in range(heads):
            scores = jnp.where(valid, dot_t(q_ref[head], keys) * SCALE, LOW)
            top = jnp.max(scores, axis=1, keepdims=True)
            if not fresh:
                old = top_ref[head]
                top = jnp.maximum(top, old)
                keep = jnp.exp(old - top)
            weights = jnp.exp(scores - top)
            total = jnp.sum(weights, axis=1, keepdims=True)
            mixed = dot32(weights.astype(jnp.bfloat16), values)
            top_ref[head] = top
            if fresh:
                sum_ref[head] = total
                mix_ref[head] = mixed
            else:
                sum_ref[head] = sum_ref[head] * keep + total
                mix_ref[head] = mix_ref[head] * keep + mixed

    def new_chunk(number, fresh):
        at = pl.multiple_of(number * tile, tile)
        key_at = at + lax.broadcasted_iota(jnp.int32, (tile, tile), 1)
        valid = (key_at >= begin) & (key_at <= index)
        take(window[0, pl.ds(at, tile), :], window[1, pl.ds(at, tile), :], valid, fresh)

    last = rows // tile + step
    new_chunk(last, True)
    first = first_ref[step]

    @pl.loop(first, last)
    def _(number):
        new_chunk(number, False)

    valid = owner_ref[...] == request
    take(window[0, pl.ds(2 * rows, 2 * slots), :], window[1, pl.ds(2 * rows, 2 * slots), :], valid, False)
    for head in range(heads):
        out_ref[:, head * HD : (head + 1) * HD] = (mix_ref[head] / sum_ref[head]).astype(jnp.bfloat16)

    @pl.when(step == 0)
    def _():
        lead_mix_ref[...] = mix_ref[:, pl.ds(0, LEAD), :]
        lead_top_ref[...] = jnp.broadcast_to(top_ref[:, pl.ds(0, LEAD), :], lead_top_ref.shape)
        lead_sum_ref[...] = jnp.broadcast_to(sum_ref[:, pl.ds(0, LEAD), :], lead_sum_ref.shape)


def local_attention(first, queries, before, here, slot_before, slot_here, owner, facts):
    heads, rows, _ = queries.shape
    slots = slot_here.shape[1]
    tile = TILE

    def whole(array):
        return pl.BlockSpec(array.shape, lambda i, first: (0,) * array.ndim)

    lead_shape = jax.ShapeDtypeStruct((heads, LEAD, HD), jnp.float32)
    return pl.pallas_call(
        local_kernel,
        grid_spec=pltpu.PrefetchScalarGridSpec(
            num_scalar_prefetch=1,
            grid=(rows // tile,),
            in_specs=[
                pl.BlockSpec((heads, tile, HD), lambda i, first: (0, i, 0)),
                whole(before),
                whole(here),
                whole(slot_before),
                whole(slot_here),
                whole(owner),
                pl.BlockSpec((tile, facts.shape[1]), lambda i, first: (i, 0)),
            ],
            out_specs=[
                pl.BlockSpec((tile, heads * HD), lambda i, first: (i, 0)),
                whole(lead_shape),
                whole(lead_shape),
                whole(lead_shape),
            ],
            scratch_shapes=[
                pltpu.VMEM((2, 2 * rows + 2 * slots, HD), jnp.bfloat16),
                pltpu.VMEM((heads, tile, 1), jnp.float32),
                pltpu.VMEM((heads, tile, 1), jnp.float32),
                pltpu.VMEM((heads, tile, HD), jnp.float32),
            ],
        ),
        out_shape=[
            jax.ShapeDtypeStruct((rows, heads * HD), jnp.bfloat16),
            lead_shape,
            lead_shape,
            lead_shape,
        ],
        cost_estimate=pl.CostEstimate(
            flops=4 * heads * rows * (rows + 2 * slots) * HD,
            bytes_accessed=8 * rows * HD * heads,
            transcendentals=heads * rows * (rows + 2 * slots),
        ),
        name="local_attention",
    )(first, queries, before, here, slot_before, slot_here, owner, facts)


def merge(into, top, total, part, part_top, part_total):
    highest = jnp.maximum(top, part_top)
    keep, add = jnp.exp(top - highest), jnp.exp(part_top - highest)
    return into * keep + part * add, highest, total * keep + part_total * add


def long_kernel(q_ref, cache_ref, mix_ref, stat_ref, mix_out, stat_out, mix_in, stat_in, sends, recvs):
    seq, head, _, _ = place()
    n_x = lax.axis_size("seq") // Z
    x, z = seq // Z, lax.rem(seq, Z)
    barrier = pltpu.get_barrier_semaphore()

    @pl.when(z > 0)
    def _():
        greet((x * Z, head))
        pl.semaphore_wait(barrier, 1)

    @pl.when((z == 0) & (x > 0))
    def _():
        for at in range(1, Z):
            greet((x * Z + at, head))
        greet((0, head))
        pl.semaphore_wait(barrier, Z)

    @pl.when(seq == 0)
    def _():
        for at in range(1, Z):
            greet((at, head))
        for at in range(1, n_x):
            greet((at * Z, head))
        pl.semaphore_wait(barrier, Z - 1 + n_x - 1)

    scores = dot_t(cache_ref[0], q_ref[...]) * SCALE
    top = jnp.max(scores, axis=0, keepdims=True)
    weights = jnp.exp(scores - top)
    total = jnp.sum(weights, axis=0, keepdims=True)
    mixed = lax.dot_general(
        cache_ref[1],
        weights.astype(jnp.bfloat16),
        (((0,), (0,)), ((), ())),
        preferred_element_type=jnp.float32,
    )

    def keep_state(mixed, top, total):
        mix_out[...] = mixed.astype(jnp.bfloat16)
        stat_out[0:1, :] = top
        stat_out[1:2, :] = total

    def copies(slot, to):
        return [
            pltpu.make_async_remote_copy(
                src_ref=source,
                dst_ref=target.at[slot],
                send_sem=sends.at[number],
                recv_sem=recvs.at[number, slot],
                device_id=(to, head),
                device_id_type=MESH,
            )
            for number, (source, target) in enumerate([(mix_out, mix_in), (stat_out, stat_in)])
        ]

    def collect(slots, mixed, top, total):
        for slot in slots:
            for copy in copies(slot, jnp.int32(0)):
                copy.wait_recv()
            mixed, top, total = merge(
                mixed,
                top,
                total,
                mix_in[slot].astype(jnp.float32),
                stat_in[slot, 0:1, :],
                stat_in[slot, 1:2, :],
            )
        return mixed, top, total

    stat_out[...] = jnp.zeros_like(stat_out)
    keep_state(mixed, top, total)
    mix_ref[...] = mixed
    stat_ref[0:1, :] = top
    stat_ref[1:2, :] = total

    for at in range(1, Z):
        @pl.when(z == at)
        def _():
            for copy in copies(at - 1, x * Z):
                copy.start()
            for copy in copies(at - 1, x * Z):
                copy.wait_send()

    @pl.when(z == 0)
    def _():
        state = collect(range(Z - 1), mix_ref[...], stat_ref[0:1, :], stat_ref[1:2, :])

        @pl.when(x > 0)
        def _():
            keep_state(*state)

        mix_ref[...] = state[0]
        stat_ref[0:1, :] = state[1]
        stat_ref[1:2, :] = state[2]

    for at in range(1, n_x):
        @pl.when((z == 0) & (x == at))
        def _():
            for copy in copies(Z - 2 + at, jnp.int32(0)):
                copy.start()
            for copy in copies(Z - 2 + at, jnp.int32(0)):
                copy.wait_send()

    @pl.when(seq == 0)
    def _():
        state = collect(
            range(Z - 1, Z + n_x - 2), mix_ref[...], stat_ref[0:1, :], stat_ref[1:2, :]
        )
        mix_ref[...] = state[0]
        stat_ref[0:1, :] = state[1]
        stat_ref[1:2, :] = state[2]


def long_part(lead_queries, cache):
    queries = lead_queries.shape[0]
    slots = Z - 1 + 3
    shape = jax.ShapeDtypeStruct
    dma = pltpu.SemaphoreType.DMA
    return pl.pallas_call(
        long_kernel,
        in_specs=[pl.BlockSpec(memory_space=pltpu.VMEM)] * 2,
        out_specs=[pl.BlockSpec(memory_space=pltpu.VMEM)] * 2,
        out_shape=[shape((HD, queries), jnp.float32), shape((8, queries), jnp.float32)],
        scratch_shapes=[
            pltpu.VMEM((HD, queries), jnp.bfloat16),
            pltpu.VMEM((8, queries), jnp.float32),
            pltpu.VMEM((slots, HD, queries), jnp.bfloat16),
            pltpu.VMEM((slots, 8, queries), jnp.float32),
            dma((2,)),
            dma((2, slots)),
        ],
        compiler_params=pltpu.CompilerParams(
            collective_id=1, has_side_effects=True, vmem_limit_bytes=LIMIT
        ),
        name="long_part",
    )(lead_queries, cache)


def on_device(
    tokens,
    norm_gain,
    w_query,
    w_key,
    w_value,
    w_out,
    long_cache,
    short_cache,
    slot_owner,
    new_len,
    cache_len,
):
    seq_index = lax.axis_index("seq")
    long_len = long_cache.shape[1] * lax.axis_size("seq")
    heads = w_query.shape[1] // HD
    rows = tokens.shape[0] * lax.axis_size("head")
    starts = request_starts(new_len)
    token_index = seq_index * rows + jnp.arange(rows, dtype=jnp.int32)
    request, begin, position = token_facts(token_index, starts, cache_len, long_len)
    cosine, sine = rotate_tables(position)
    normed = normalize(tokens, norm_gain).reshape(2, LEAD, tokens.shape[1])
    queries, here, before, earlier_slots, earlier_owner, lead_queries = gather_project(
        normed, w_query, w_key, w_value, cosine, sine, short_cache, slot_owner[None, :]
    )
    lead_queries = jnp.pad(lead_queries.reshape(heads * LEAD, HD), ((0, LEAD), (0, 0)))
    long_mix, long_stat = long_part(lead_queries, long_cache)
    long_mix = long_mix[:, : heads * LEAD].reshape(HD, heads, LEAD).transpose(1, 2, 0)
    long_high = long_stat[0, : heads * LEAD].reshape(heads, LEAD)
    long_sum = long_stat[1, : heads * LEAD].reshape(heads, LEAD)

    shift = (seq_index - 1) * rows
    window_begin = jnp.maximum(begin - shift, 0)
    window_index = token_index - shift
    window_begin = jnp.where(request == starts.shape[0], -shift, window_begin)
    facts = jnp.stack([request, window_begin, window_index] + [window_index] * 5, axis=1)
    owner = jnp.concatenate([jnp.where(seq_index > 0, earlier_owner[0], -1), slot_owner])[None, :]
    first = window_begin[::TILE] // TILE
    attended, lead_mix, lead_top, lead_sum = local_attention(
        first, queries, before, here, earlier_slots, short_cache, owner, facts
    )
    lead_top = lead_top[:, :, 0]
    lead_sum = lead_sum[:, :, 0]
    highest = jnp.maximum(lead_top, long_high)
    scale_near = jnp.exp(lead_top - highest)
    scale_long = jnp.exp(long_high - highest)
    total = lead_sum * scale_near + long_sum * scale_long
    mixture = lead_mix * scale_near[..., None] + long_mix * scale_long[..., None]
    lead_out = (mixture / total[..., None]).astype(jnp.bfloat16)
    lead_out = jnp.transpose(lead_out, (1, 0, 2)).reshape(LEAD, heads * HD)
    lead_out = jnp.where(seq_index == 0, lead_out, attended[:LEAD])
    attended = lax.dynamic_update_slice(attended, lead_out, (0, 0))
    return lax.psum_scatter(
        dot32(attended, w_out).astype(jnp.bfloat16), "head", scatter_dimension=0, tiled=True
    )


def solution(mesh):
    placed = (
        P(("seq", "head"), None),
        P(),
        P(None, "head"),
        P(None, "head"),
        P(None, "head"),
        P("head", None),
        P(None, "seq", "head"),
        P(None, "seq", "head"),
        P("seq"),
        P(),
        P(),
    )
    return jax.shard_map(
        on_device, mesh=mesh, in_specs=placed, out_specs=P(("seq", "head"), None), check_vma=False
    )
```

```python
import math

import jax
import jax.numpy as jnp
from jax import lax
from jax.experimental import pallas as pl
from jax.experimental.pallas import tpu as pltpu
from jax.sharding import PartitionSpec as P

HD = 128
LEAD = 64
THETA_LOG = math.log(500000.0)
SCALE = 1.0 / math.sqrt(HD)
LOW = -1e30
TILE = 256


def from_behind(block, axis, distance):
    devices = range(lax.axis_size(axis))
    route = [(i - distance, i) for i in devices if i - distance in devices]
    return lax.ppermute(block, axis, route)


def request_starts(new_len):
    return LEAD + jnp.cumsum(new_len) - new_len


def token_facts(token_index, starts, cache_len, long_len):
    number = starts.shape[0]
    passed = (starts[None, :] <= token_index[:, None]).astype(jnp.int32)
    request = jnp.sum(passed, axis=1) - 1
    select = jnp.arange(number, dtype=jnp.int32)[None, :] == request[:, None]
    begin = jnp.sum(jnp.where(select, starts[None, :], 0), axis=1)
    cached = jnp.sum(jnp.where(select, cache_len[None, :], 0), axis=1)
    lead = request < 0
    position = jnp.where(lead, token_index + long_len, token_index - begin + cached)
    return jnp.where(lead, number, request), begin, position


def normalize(tokens, norm_gain):
    values = tokens.astype(jnp.float32)
    mean_square = jnp.mean(values * values, axis=-1, keepdims=True)
    return (values * lax.rsqrt(mean_square + 1e-05) * norm_gain).astype(jnp.bfloat16)


def rotate_tables(position):
    half = HD // 2
    frequency = jnp.exp(jnp.arange(half, dtype=jnp.float32) * (-2.0 * THETA_LOG / HD))
    angle = position.astype(jnp.float32)[:, None] * frequency[None, :]
    cosine = jnp.cos(angle)
    sine = jnp.sin(angle)
    return (
        jnp.concatenate([cosine, cosine], axis=1),
        jnp.concatenate([-sine, sine], axis=1),
    )


def dot32(a, b):
    return jnp.dot(a, b, preferred_element_type=jnp.float32)


def dot_t(a, b):
    return lax.dot_general(a, b, (((1,), (1,)), ((), ())), preferred_element_type=jnp.float32)


MESH = pl.DeviceIdType.MESH
LIMIT = 60 * 1024 * 1024
Z = 8
Y = 4
UNITS = [(0, 0), (0, 1), (1, 0), (3, 0), (1, 1), (2, 0), (2, 1), (3, 1)]
SLOT = {unit: number for number, unit in enumerate(UNITS)}


def place():
    seq = lax.axis_index("seq")
    head = lax.axis_index("head")
    return seq, head, head // 2, lax.rem(head, 2)


def pick(number, table):
    value = jnp.int32(table[0])
    for at, entry in enumerate(table):
        value = jnp.where(number == at, jnp.int32(entry), value)
    return value


def greet(device):
    pl.semaphore_signal(
        pltpu.get_barrier_semaphore(), inc=1, device_id=device, device_id_type=MESH
    )


def gather_kernel(
    normed_ref,
    wq_ref,
    wk_ref,
    wv_ref,
    cos_ref,
    sin_ref,
    slots_ref,
    owner_ref,
    q_ref,
    kv_ref,
    before_ref,
    slots_before_ref,
    owner_before_ref,
    lead_ref,
    held,
    ring_send,
    ring_recv,
    pair_send,
    pair_recv,
    kv_send,
    kv_recv,
    slot_send,
    slot_recv,
    lead_send,
    lead_recv,
):
    seq, head, y, core = place()
    n_seq = lax.axis_size("seq")
    x, z = seq // Z, lax.rem(seq, Z)
    way = 1 - 2 * core
    right = (seq, lax.rem(y + way + Y, Y) * 2 + core)
    left = (seq, lax.rem(y - way + Y, Y) * 2 + core)
    pair = (seq, head + way)
    following = (lax.rem(seq + 1, n_seq), head)
    previous = (lax.rem(seq + n_seq - 1, n_seq), head)
    heads = q_ref.shape[0]
    half = held.shape[2]

    for device in (right, left, pair, following, previous):
        greet(device)

    @pl.when(seq == 0)
    def _():
        for to in range(1, Z):
            greet((to, head))

    @pl.when(x == 0)
    def _():
        for to in range(1, n_seq // Z):
            greet((to * Z + z, head))

    @pl.when((x == 0) & (z > 0))
    def _():
        greet((0, head))

    @pl.when(x > 0)
    def _():
        greet((z, head))

    barrier = pltpu.get_barrier_semaphore()
    others = n_seq // Z - 1

    @pl.when(seq == 0)
    def _():
        pl.semaphore_wait(barrier, 5 + Z - 1 + others)

    @pl.when((x == 0) & (z > 0))
    def _():
        pl.semaphore_wait(barrier, 5 + 1 + others)

    @pl.when(x > 0)
    def _():
        pl.semaphore_wait(barrier, 5 + 1)

    def ring(number, source, to, unit):
        slot = SLOT[unit]
        return pltpu.make_async_remote_copy(
            src_ref=source,
            dst_ref=held.at[slot, core],
            send_sem=ring_send.at[number],
            recv_sem=ring_recv.at[slot],
            device_id=to,
            device_id_type=MESH,
        )

    def mine(unit):
        return held.at[SLOT[unit], core]

    def to_pair(unit):
        slot = SLOT[unit]
        return pltpu.make_async_remote_copy(
            src_ref=normed_ref.at[unit[1]] if unit[0] == 0 else mine(unit),
            dst_ref=held.at[slot, core],
            send_sem=pair_send.at[slot],
            recv_sem=pair_recv.at[slot],
            device_id=pair,
            device_id_type=MESH,
        )

    rings = [
        ring(0, normed_ref.at[0], right, (1, 0)),
        ring(1, normed_ref.at[0], left, (3, 0)),
        ring(2, normed_ref.at[1], right, (1, 1)),
        ring(3, mine((1, 0)), right, (2, 0)),
        ring(4, mine((1, 1)), right, (2, 1)),
        ring(5, mine((2, 1)), right, (3, 1)),
    ]
    pairs = {unit: to_pair(unit) for unit in UNITS}
    side = [
        pltpu.make_async_remote_copy(
            src_ref=source,
            dst_ref=target,
            send_sem=slot_send.at[number],
            recv_sem=slot_recv.at[number],
            device_id=following,
            device_id_type=MESH,
        )
        for number, (source, target) in enumerate(
            [(slots_ref, slots_before_ref), (owner_ref, owner_before_ref)]
        )
    ]

    def lead_copy(number, to):
        return pltpu.make_async_remote_copy(
            src_ref=lead_ref,
            dst_ref=lead_ref,
            send_sem=lead_send.at[number],
            recv_sem=lead_recv,
            device_id=(to, head),
            device_id_type=MESH,
        )

    along_z = [lead_copy(to - 1, jnp.int32(to)) for to in range(1, Z)]
    along_x = [lead_copy(Z - 2 + to, to * Z + z) for to in range(1, n_seq // Z)]

    def row_starts(number):
        distance = pick(number, [unit[0] for unit in UNITS])
        later = pick(number, [unit[1] for unit in UNITS])
        first = lax.rem(y - distance + Y, Y) * (4 * half) + later * half
        second = lax.rem(y + distance, Y) * (4 * half) + 2 * half + later * half
        return pl.multiple_of(first, half), pl.multiple_of(second, half)

    def kv_copies(number):
        return [
            pltpu.make_async_remote_copy(
                src_ref=kv_ref.at[:, pl.ds(start, half), :],
                dst_ref=before_ref.at[:, pl.ds(start, half), :],
                send_sem=kv_send.at[2 * number + part],
                recv_sem=kv_recv.at[2 * number + part],
                device_id=following,
                device_id_type=MESH,
            )
            for part, start in enumerate(row_starts(number))
        ]

    rings[0].start()
    pairs[(0, 0)].start()
    rings[1].start()
    rings[2].start()
    pairs[(0, 1)].start()
    for copy in side:
        copy.start()
    for later in range(2):
        held[SLOT[(0, later)], core] = normed_ref[later]

    def event_0():
        pairs[(0, 0)].wait_recv()

    def event_1():
        pairs[(0, 1)].wait_recv()

    def event_2():
        rings[0].wait_recv()
        rings[3].start()
        pairs[(1, 0)].start()
        pairs[(1, 0)].wait_recv()

    def event_3():
        rings[1].wait_recv()
        pairs[(3, 0)].start()
        rings[2].wait_recv()
        rings[4].start()
        pairs[(1, 1)].start()
        pairs[(3, 0)].wait_recv()

    def event_4():
        pairs[(1, 1)].wait_recv()

    def event_5():
        rings[3].wait_recv()
        pairs[(2, 0)].start()
        pairs[(2, 0)].wait_recv()

    def event_6():
        @pl.when(seq == 0)
        def _():
            lead_ref[...] = q_ref[:, pl.ds(0, LEAD), :]
            for copy in along_z:
                copy.start()
            for copy in along_x:
                copy.start()

        rings[4].wait_recv()
        rings[5].start()
        pairs[(2, 1)].start()
        pairs[(2, 1)].wait_recv()

    def event_7():
        rings[5].wait_recv()
        pairs[(3, 1)].start()

        @pl.when((x == 0) & (z > 0))
        def _():
            along_z[0].wait_recv()
            for copy in along_x:
                copy.start()

        pairs[(3, 1)].wait_recv()

    events = [event_0, event_1, event_2, event_3, event_4, event_5, event_6, event_7]

    @pl.loop(0, len(UNITS))
    def _(number):
        for at, event in enumerate(events):
            pl.when(number == at)(event)
        block = held[number].reshape(2 * half, held.shape[3])
        starts = row_starts(number)
        cosine = jnp.concatenate([cos_ref[pl.ds(start, half), :] for start in starts], axis=0)
        sine = jnp.concatenate([sin_ref[pl.ds(start, half), :] for start in starts], axis=0)

        def turned(product):
            return (product * cosine + pltpu.roll(product, HD // 2, 1) * sine).astype(jnp.bfloat16)

        def put(ref, at, rows):
            for part, start in enumerate(starts):
                ref[at, pl.ds(start, half), :] = rows[part * half : (part + 1) * half]

        both = dot32(block, jnp.concatenate([wk_ref[...], wv_ref[...]], axis=1))
        put(kv_ref, 0, turned(both[:, :HD]))
        put(kv_ref, 1, both[:, HD:].astype(jnp.bfloat16))
        product = dot32(block, wq_ref[...])
        for at in range(heads):
            put(q_ref, at, turned(product[:, at * HD : (at + 1) * HD]))
        for copy in kv_copies(number):
            copy.start()

    @pl.loop(0, len(UNITS))
    def _(number):
        for copy in kv_copies(number):
            copy.wait_recv()
            copy.wait_send()

    for copy in rings:
        copy.wait_send()
    for unit in UNITS:
        pairs[unit].wait_send()
    for copy in side:
        copy.wait_recv()
        copy.wait_send()

    @pl.when(seq == 0)
    def _():
        for copy in along_z:
            copy.wait_send()

    @pl.when(x == 0)
    def _():
        for copy in along_x:
            copy.wait_send()

    @pl.when(x > 0)
    def _():
        along_x[0].wait_recv()


def gather_project(normed, w_query, w_key, w_value, cosine, sine, slots, owner):
    rows, width = cosine.shape[0], normed.shape[-1]
    heads = w_query.shape[1] // HD
    half = normed.shape[1]
    vmem = pl.BlockSpec(memory_space=pltpu.VMEM)
    dma = pltpu.SemaphoreType.DMA
    shape = jax.ShapeDtypeStruct
    return pl.pallas_call(
        gather_kernel,
        in_specs=[vmem] * 8,
        out_specs=[vmem] * 6,
        out_shape=[
            shape((heads, rows, HD), jnp.bfloat16),
            shape((2, rows, HD), jnp.bfloat16),
            shape((2, rows, HD), jnp.bfloat16),
            shape(slots.shape, jnp.bfloat16),
            shape(owner.shape, jnp.int32),
            shape((heads, LEAD, HD), jnp.bfloat16),
        ],
        scratch_shapes=[
            pltpu.VMEM((len(UNITS), 2, half, width), jnp.bfloat16),
            dma((6,)),
            dma((len(UNITS),)),
            dma((len(UNITS),)),
            dma((len(UNITS),)),
            dma((2 * len(UNITS),)),
            dma((2 * len(UNITS),)),
            dma((2,)),
            dma((2,)),
            dma((Z + 2,)),
            dma,
        ],
        compiler_params=pltpu.CompilerParams(
            collective_id=0, has_side_effects=True, vmem_limit_bytes=LIMIT
        ),
        name="gather_project",
    )(normed, w_query, w_key, w_value, cosine, sine, slots, owner)


def local_kernel(
    first_ref,
    q_ref,
    before_ref,
    here_ref,
    slot_before_ref,
    slot_here_ref,
    owner_ref,
    facts_ref,
    out_ref,
    lead_mix_ref,
    lead_top_ref,
    lead_sum_ref,
    window,
    top_ref,
    sum_ref,
    mix_ref,
):
    step = pl.program_id(0)
    rows = here_ref.shape[1]
    slots = slot_here_ref.shape[1]
    heads, tile, _ = q_ref.shape

    @pl.when(step == 0)
    def _():
        window[:, pl.ds(0, rows)] = before_ref[...]
        window[:, pl.ds(rows, rows)] = here_ref[...]
        window[:, pl.ds(2 * rows, slots)] = slot_before_ref[...]
        window[:, pl.ds(2 * rows + slots, slots)] = slot_here_ref[...]

    request = facts_ref[:, 0:1]
    begin = facts_ref[:, 1:2]
    index = facts_ref[:, 2:3]

    def take(keys, values, valid, fresh):
        for head in range(heads):
            scores = jnp.where(valid, dot_t(q_ref[head], keys) * SCALE, LOW)
            top = jnp.max(scores, axis=1, keepdims=True)
            if not fresh:
                old = top_ref[head]
                top = jnp.maximum(top, old)
                keep = jnp.exp(old - top)
            weights = jnp.exp(scores - top)
            total = jnp.sum(weights, axis=1, keepdims=True)
            mixed = dot32(weights.astype(jnp.bfloat16), values)
            top_ref[head] = top
            if fresh:
                sum_ref[head] = total
                mix_ref[head] = mixed
            else:
                sum_ref[head] = sum_ref[head] * keep + total
                mix_ref[head] = mix_ref[head] * keep + mixed

    def new_chunk(number, fresh):
        at = pl.multiple_of(number * tile, tile)
        key_at = at + lax.broadcasted_iota(jnp.int32, (tile, tile), 1)
        valid = (key_at >= begin) & (key_at <= index)
        take(window[0, pl.ds(at, tile), :], window[1, pl.ds(at, tile), :], valid, fresh)

    last = rows // tile + step
    new_chunk(last, True)
    first = first_ref[step]

    @pl.loop(first, last)
    def _(number):
        new_chunk(number, False)

    valid = owner_ref[...] == request
    take(window[0, pl.ds(2 * rows, 2 * slots), :], window[1, pl.ds(2 * rows, 2 * slots), :], valid, False)
    for head in range(heads):
        out_ref[:, head * HD : (head + 1) * HD] = (mix_ref[head] / sum_ref[head]).astype(jnp.bfloat16)

    @pl.when(step == 0)
    def _():
        lead_mix_ref[...] = mix_ref[:, pl.ds(0, LEAD), :]
        lead_top_ref[...] = jnp.broadcast_to(top_ref[:, pl.ds(0, LEAD), :], lead_top_ref.shape)
        lead_sum_ref[...] = jnp.broadcast_to(sum_ref[:, pl.ds(0, LEAD), :], lead_sum_ref.shape)


def local_attention(first, queries, before, here, slot_before, slot_here, owner, facts):
    heads, rows, _ = queries.shape
    slots = slot_here.shape[1]
    tile = TILE

    def whole(array):
        return pl.BlockSpec(array.shape, lambda i, first: (0,) * array.ndim)

    lead_shape = jax.ShapeDtypeStruct((heads, LEAD, HD), jnp.float32)
    return pl.pallas_call(
        local_kernel,
        grid_spec=pltpu.PrefetchScalarGridSpec(
            num_scalar_prefetch=1,
            grid=(rows // tile,),
            in_specs=[
                pl.BlockSpec((heads, tile, HD), lambda i, first: (0, i, 0)),
                whole(before),
                whole(here),
                whole(slot_before),
                whole(slot_here),
                whole(owner),
                pl.BlockSpec((tile, facts.shape[1]), lambda i, first: (i, 0)),
            ],
            out_specs=[
                pl.BlockSpec((tile, heads * HD), lambda i, first: (i, 0)),
                whole(lead_shape),
                whole(lead_shape),
                whole(lead_shape),
            ],
            scratch_shapes=[
                pltpu.VMEM((2, 2 * rows + 2 * slots, HD), jnp.bfloat16),
                pltpu.VMEM((heads, tile, 1), jnp.float32),
                pltpu.VMEM((heads, tile, 1), jnp.float32),
                pltpu.VMEM((heads, tile, HD), jnp.float32),
            ],
        ),
        out_shape=[
            jax.ShapeDtypeStruct((rows, heads * HD), jnp.bfloat16),
            lead_shape,
            lead_shape,
            lead_shape,
        ],
        cost_estimate=pl.CostEstimate(
            flops=4 * heads * rows * (rows + 2 * slots) * HD,
            bytes_accessed=8 * rows * HD * heads,
            transcendentals=heads * rows * (rows + 2 * slots),
        ),
        name="local_attention",
    )(first, queries, before, here, slot_before, slot_here, owner, facts)


def merge(into, top, total, part, part_top, part_total):
    highest = jnp.maximum(top, part_top)
    keep, add = jnp.exp(top - highest), jnp.exp(part_top - highest)
    return into * keep + part * add, highest, total * keep + part_total * add


PIECES = 4


def scatter_kernel(
    attended_ref,
    w_ref,
    q_ref,
    cache_ref,
    near_mix_ref,
    near_top_ref,
    near_sum_ref,
    out_ref,
    pair_out,
    pair_in,
    own,
    ring_out,
    ring_in,
    mix_out,
    stat_out,
    mix_in,
    stat_in,
    pair_send,
    pair_recv,
    ring_send,
    ring_recv,
    sends,
    recvs,
):
    seq, head, y, core = place()
    n_x = lax.axis_size("seq") // Z
    x, z = seq // Z, lax.rem(seq, Z)
    way = 1 - 2 * core
    right = (seq, lax.rem(y + way + Y, Y) * 2 + core)
    left = (seq, lax.rem(y - way + Y, Y) * 2 + core)
    pair = (seq, head + way)
    half = ring_out.shape[2]
    heads = q_ref.shape[0]
    width = w_ref.shape[1] // PIECES
    barrier = pltpu.get_barrier_semaphore()

    for device in (right, left, pair):
        greet(device)

    @pl.when(z > 0)
    def _():
        greet((x * Z, head))
        pl.semaphore_wait(barrier, 3 + 1)

    @pl.when((z == 0) & (x > 0))
    def _():
        for at in range(1, Z):
            greet((x * Z + at, head))
        greet((0, head))
        pl.semaphore_wait(barrier, 3 + Z)

    @pl.when(seq == 0)
    def _():
        for at in range(1, Z):
            greet((at, head))
        for at in range(1, n_x):
            greet((at * Z, head))
        pl.semaphore_wait(barrier, 3 + Z - 1 + n_x - 1)

    def columns(piece):
        return pl.ds(piece * width, width)

    def rows_of(chip, of_core, later):
        return attended_ref[pl.ds(pl.multiple_of(chip * (4 * half) + of_core * (2 * half) + later * half, half), half), :]

    def stack(later):
        parts = [rows_of(lax.rem(y - k * way + 2 * Y * 2, Y), 1 - core, later) for k in range(Y)]
        parts += [rows_of(lax.rem(y + k * way + 2 * Y * 2, Y), core, later) for k in range(Y)]
        return jnp.concatenate(parts, axis=0)

    def pair_copy(later, piece):
        return pltpu.make_async_remote_copy(
            src_ref=pair_out.at[later, :, columns(piece)],
            dst_ref=pair_in.at[later, :, columns(piece)],
            send_sem=pair_send.at[later, piece],
            recv_sem=pair_recv.at[later, piece],
            device_id=pair,
            device_id_type=MESH,
        )

    def ring_copy(later, step, piece):
        return pltpu.make_async_remote_copy(
            src_ref=ring_out.at[later, step, :, columns(piece)],
            dst_ref=ring_in.at[later, step, :, columns(piece)],
            send_sem=ring_send.at[later, step, piece],
            recv_sem=ring_recv.at[later, step, piece],
            device_id=left if (later, step) == (0, 2) else right,
            device_id_type=MESH,
        )

    def project(rows, later, piece):
        product = dot32(rows, w_ref[:, columns(piece)]).astype(jnp.bfloat16)
        pair_out[later, :, columns(piece)] = product[: Y * half]
        own[later, :, columns(piece)] = product[Y * half :]

    def chip_sum(later, k, piece):
        rows = pl.ds(k * half, half)
        return own[later, rows, columns(piece)].astype(jnp.float32) + pair_in[
            later, rows, columns(piece)
        ].astype(jnp.float32)

    def arrived(later, step, piece):
        ring_copy(later, step, piece).wait_recv()
        return ring_in[later, step, :, columns(piece)].astype(jnp.float32)

    def pass_on(later, step, piece, value):
        ring_out[later, step, :, columns(piece)] = value.astype(jnp.bfloat16)
        ring_copy(later, step, piece).start()

    def first_hop(piece):
        pair_copy(1, piece).wait_recv()
        pass_on(1, 0, piece, chip_sum(1, 3, piece))

    rows = stack(1)
    for piece in range(PIECES):
        project(rows, 1, piece)
        pair_copy(1, piece).start()
        if piece:
            first_hop(piece - 1)
    first_hop(PIECES - 1)

    queries = jnp.concatenate([q_ref[at] for at in range(heads)] + [q_ref[heads - 1]], axis=0)
    scores = dot_t(cache_ref[0], queries) * SCALE
    top = jnp.max(scores, axis=0, keepdims=True)
    weights = jnp.exp(scores - top)
    mixed = lax.dot_general(
        cache_ref[1],
        weights.astype(jnp.bfloat16),
        (((0,), (0,)), ((), ())),
        preferred_element_type=jnp.float32,
    )

    def keep_state(mixed, top, total):
        mix_out[...] = mixed.astype(jnp.bfloat16)
        stat_out[0:1, :] = top
        stat_out[1:2, :] = total

    def state_copies(slot, to):
        return [
            pltpu.make_async_remote_copy(
                src_ref=source,
                dst_ref=target.at[slot],
                send_sem=sends.at[number],
                recv_sem=recvs.at[number, slot],
                device_id=(to, head),
                device_id_type=MESH,
            )
            for number, (source, target) in enumerate([(mix_out, mix_in), (stat_out, stat_in)])
        ]

    def collect(slots):
        state = (mix_out[...].astype(jnp.float32), stat_out[0:1, :], stat_out[1:2, :])
        for slot in slots:
            for copy in state_copies(slot, jnp.int32(0)):
                copy.wait_recv()
            state = merge(
                *state,
                mix_in[slot].astype(jnp.float32),
                stat_in[slot, 0:1, :],
                stat_in[slot, 1:2, :],
            )
            state = (state[0], state[1], state[2])
        return state

    stat_out[...] = jnp.zeros_like(stat_out)
    keep_state(mixed, top, jnp.sum(weights, axis=0, keepdims=True))
    for at in range(1, Z):
        @pl.when(z == at)
        def _():
            for copy in state_copies(at - 1, x * Z):
                copy.start()

    rows = stack(0)
    for piece in range(PIECES):
        project(rows, 0, piece)

    for piece in range(PIECES):
        pass_on(1, 1, piece, chip_sum(1, 2, piece) + arrived(1, 0, piece))

    @pl.when(z == 0)
    def _():
        keep_state(*collect(range(Z - 1)))

    for at in range(1, n_x):
        @pl.when((z == 0) & (x == at))
        def _():
            for copy in state_copies(Z - 2 + at, jnp.int32(0)):
                copy.start()

    for piece in range(PIECES):
        pass_on(1, 2, piece, chip_sum(1, 1, piece) + arrived(1, 1, piece))

    @pl.when(seq == 0)
    def _():
        mixed, top, total = collect(range(Z - 1, Z + n_x - 2))
        mixed = jnp.transpose(mixed)
        top = jnp.transpose(jnp.broadcast_to(top, mix_out.shape))
        total = jnp.transpose(jnp.broadcast_to(total, mix_out.shape))
        parts = []
        for at in range(heads):
            lead = slice(at * LEAD, (at + 1) * LEAD)
            joined = merge(
                near_mix_ref[at],
                near_top_ref[at],
                near_sum_ref[at],
                mixed[lead],
                top[lead],
                total[lead],
            )
            parts.append((joined[0] / joined[2]).astype(jnp.bfloat16))
        lead_rows = jnp.concatenate(parts, axis=1)
        for piece in range(PIECES):
            product = dot32(lead_rows, w_ref[:, columns(piece)]).astype(jnp.bfloat16)

            @pl.when(core == 0)
            def _():
                at = pl.multiple_of(lax.rem(Y - y, Y) * half, half)
                own[0, pl.ds(at, half), columns(piece)] = product

            @pl.when(core == 1)
            def _():
                at = pl.multiple_of(lax.rem(Y - y, Y) * half, half)
                pair_out[0, pl.ds(at, half), columns(piece)] = product

    for piece in range(PIECES):
        pair_copy(0, piece).start()
    for piece in range(PIECES):
        pair_copy(0, piece).wait_recv()
        pass_on(0, 0, piece, chip_sum(0, 2, piece))
        pass_on(0, 2, piece, chip_sum(0, 3, piece))
    for piece in range(PIECES):
        value = chip_sum(1, 0, piece) + arrived(1, 2, piece)
        out_ref[pl.ds(half, half), columns(piece)] = value.astype(jnp.bfloat16)
    for piece in range(PIECES):
        pass_on(0, 1, piece, chip_sum(0, 1, piece) + arrived(0, 0, piece))
    for piece in range(PIECES):
        value = chip_sum(0, 0, piece) + arrived(0, 2, piece) + arrived(0, 1, piece)
        out_ref[pl.ds(0, half), columns(piece)] = value.astype(jnp.bfloat16)

    for later in range(2):
        for piece in range(PIECES):
            pair_copy(later, piece).wait_send()
            for step in range(3):
                ring_copy(later, step, piece).wait_send()

    @pl.when(seq > 0)
    def _():
        for copy in state_copies(0, jnp.int32(0)):
            copy.wait_send()


def project_scatter(attended, w_out, lead_queries, cache, near_mix, near_top, near_sum):
    rows, inner = attended.shape
    width = w_out.shape[1]
    half = LEAD
    slots = Z - 1 + 3
    queries = (lead_queries.shape[0] + 1) * LEAD
    vmem = pl.BlockSpec(memory_space=pltpu.VMEM)
    dma = pltpu.SemaphoreType.DMA
    return pl.pallas_call(
        scatter_kernel,
        in_specs=[vmem] * 7,
        out_specs=vmem,
        out_shape=jax.ShapeDtypeStruct((2 * half, width), jnp.bfloat16),
        scratch_shapes=[
            pltpu.VMEM((2, Y * half, width), jnp.bfloat16),
            pltpu.VMEM((2, Y * half, width), jnp.bfloat16),
            pltpu.VMEM((2, Y * half, width), jnp.bfloat16),
            pltpu.VMEM((2, 3, half, width), jnp.bfloat16),
            pltpu.VMEM((2, 3, half, width), jnp.bfloat16),
            pltpu.VMEM((HD, queries), jnp.bfloat16),
            pltpu.VMEM((8, queries), jnp.float32),
            pltpu.VMEM((slots, HD, queries), jnp.bfloat16),
            pltpu.VMEM((slots, 8, queries), jnp.float32),
            dma((2, PIECES)),
            dma((2, PIECES)),
            dma((2, 3, PIECES)),
            dma((2, 3, PIECES)),
            dma((2,)),
            dma((2, slots)),
        ],
        compiler_params=pltpu.CompilerParams(
            collective_id=1, has_side_effects=True, vmem_limit_bytes=LIMIT
        ),
        name="project_scatter",
    )(attended, w_out, lead_queries, cache, near_mix, near_top, near_sum)


def on_device(
    tokens,
    norm_gain,
    w_query,
    w_key,
    w_value,
    w_out,
    long_cache,
    short_cache,
    slot_owner,
    new_len,
    cache_len,
):
    seq_index = lax.axis_index("seq")
    long_len = long_cache.shape[1] * lax.axis_size("seq")
    heads = w_query.shape[1] // HD
    rows = tokens.shape[0] * lax.axis_size("head")
    starts = request_starts(new_len)
    token_index = seq_index * rows + jnp.arange(rows, dtype=jnp.int32)
    request, begin, position = token_facts(token_index, starts, cache_len, long_len)
    cosine, sine = rotate_tables(position)
    normed = normalize(tokens, norm_gain).reshape(2, LEAD, tokens.shape[1])
    queries, here, before, earlier_slots, earlier_owner, lead_queries = gather_project(
        normed, w_query, w_key, w_value, cosine, sine, short_cache, slot_owner[None, :]
    )

    shift = (seq_index - 1) * rows
    window_begin = jnp.maximum(begin - shift, 0)
    window_index = token_index - shift
    window_begin = jnp.where(request == starts.shape[0], -shift, window_begin)
    facts = jnp.stack([request, window_begin, window_index] + [window_index] * 5, axis=1)
    owner = jnp.concatenate([jnp.where(seq_index > 0, earlier_owner[0], -1), slot_owner])[None, :]
    first = window_begin[::TILE] // TILE
    attended, lead_mix, lead_top, lead_sum = local_attention(
        first, queries, before, here, earlier_slots, short_cache, owner, facts
    )
    return project_scatter(
        attended, w_out, lead_queries, long_cache, lead_mix, lead_top, lead_sum
    )


def solution(mesh):
    placed = (
        P(("seq", "head"), None),
        P(),
        P(None, "head"),
        P(None, "head"),
        P(None, "head"),
        P("head", None),
        P(None, "seq", "head"),
        P(None, "seq", "head"),
        P("seq"),
        P(),
        P(),
    )
    return jax.shard_map(
        on_device, mesh=mesh, in_specs=placed, out_specs=P(("seq", "head"), None), check_vma=False
    )
```

```python
import math

import jax
import jax.numpy as jnp
from jax import lax
from jax.experimental import pallas as pl
from jax.experimental.pallas import tpu as pltpu
from jax.sharding import PartitionSpec as P

HD = 128
LEAD = 64
THETA_LOG = math.log(500000.0)
SCALE = 1.0 / math.sqrt(HD)
LOW = -1e30


def request_starts(new_len):
    return LEAD + jnp.cumsum(new_len) - new_len


def token_facts(token_index, starts, cache_len, long_len):
    number = starts.shape[0]
    passed = (starts[None, :] <= token_index[:, None]).astype(jnp.int32)
    request = jnp.sum(passed, axis=1) - 1
    select = jnp.arange(number, dtype=jnp.int32)[None, :] == request[:, None]
    begin = jnp.sum(jnp.where(select, starts[None, :], 0), axis=1)
    cached = jnp.sum(jnp.where(select, cache_len[None, :], 0), axis=1)
    lead = request < 0
    position = jnp.where(lead, token_index + long_len, token_index - begin + cached)
    return jnp.where(lead, number, request), begin, position


def normalize(tokens, norm_gain):
    values = tokens.astype(jnp.float32)
    mean_square = jnp.mean(values * values, axis=-1, keepdims=True)
    return (values * lax.rsqrt(mean_square + 1e-05) * norm_gain).astype(jnp.bfloat16)


def rotate_table(position):
    half = HD // 2
    frequency = jnp.exp(jnp.arange(half, dtype=jnp.float32) * (-2.0 * THETA_LOG / HD))
    angle = position.astype(jnp.float32)[:, None] * frequency[None, :]
    return jnp.concatenate([jnp.cos(angle), jnp.sin(angle)], axis=1)


def dot32(a, b):
    return jnp.dot(a, b, preferred_element_type=jnp.float32)


def dot_t(a, b):
    return lax.dot_general(a, b, (((1,), (1,)), ((), ())), preferred_element_type=jnp.float32)


MESH = pl.DeviceIdType.MESH
LIMIT = 60 * 1024 * 1024
Z = 8
Y = 4
UNITS = [(0, 0), (0, 1), (1, 0), (3, 0), (1, 1), (2, 0), (2, 1), (3, 1)]
SLOT = {unit: number for number, unit in enumerate(UNITS)}


def place():
    seq = lax.axis_index("seq")
    head = lax.axis_index("head")
    return seq, head, head // 2, lax.rem(head, 2)


def pick(number, table):
    value = jnp.int32(table[0])
    for at, entry in enumerate(table):
        value = jnp.where(number == at, jnp.int32(entry), value)
    return value


def greet(device):
    pl.semaphore_signal(
        pltpu.get_barrier_semaphore(), inc=1, device_id=device, device_id_type=MESH
    )


def gather_kernel(
    tokens_ref,
    gain_ref,
    wq_ref,
    wk_ref,
    wv_ref,
    table_ref,
    slots_ref,
    owner_ref,
    q_ref,
    kv_ref,
    before_ref,
    slots_before_ref,
    owner_before_ref,
    lead_ref,
    normed_ref,
    held,
    ring_send,
    ring_recv,
    pair_send,
    pair_recv,
    kv_send,
    kv_recv,
    slot_send,
    slot_recv,
    lead_send,
    lead_recv,
):
    seq, head, y, core = place()
    n_seq = lax.axis_size("seq")
    x, z = seq // Z, lax.rem(seq, Z)
    way = 1 - 2 * core
    right = (seq, lax.rem(y + way + Y, Y) * 2 + core)
    left = (seq, lax.rem(y - way + Y, Y) * 2 + core)
    pair = (seq, head + way)
    following = (lax.rem(seq + 1, n_seq), head)
    previous = (lax.rem(seq + n_seq - 1, n_seq), head)
    heads = q_ref.shape[0]
    half = held.shape[2]

    for device in (right, left, pair, following, previous):
        greet(device)

    @pl.when(seq == 0)
    def _():
        for to in range(1, Z):
            greet((to, head))

    @pl.when(x == 0)
    def _():
        for to in range(1, n_seq // Z):
            greet((to * Z + z, head))

    @pl.when((x == 0) & (z > 0))
    def _():
        greet((0, head))

    @pl.when(x > 0)
    def _():
        greet((z, head))

    for later in range(2):
        normed_ref[later] = normalize(tokens_ref[later], gain_ref[...])
        held[SLOT[(0, later)], core] = normed_ref[later]

    barrier = pltpu.get_barrier_semaphore()
    others = n_seq // Z - 1

    @pl.when(seq == 0)
    def _():
        pl.semaphore_wait(barrier, 5 + Z - 1 + others)

    @pl.when((x == 0) & (z > 0))
    def _():
        pl.semaphore_wait(barrier, 5 + 1 + others)

    @pl.when(x > 0)
    def _():
        pl.semaphore_wait(barrier, 5 + 1)

    def ring(number, source, to, unit):
        slot = SLOT[unit]
        return pltpu.make_async_remote_copy(
            src_ref=source,
            dst_ref=held.at[slot, core],
            send_sem=ring_send.at[number],
            recv_sem=ring_recv.at[slot],
            device_id=to,
            device_id_type=MESH,
        )

    def mine(unit):
        return held.at[SLOT[unit], core]

    def to_pair(unit):
        slot = SLOT[unit]
        return pltpu.make_async_remote_copy(
            src_ref=normed_ref.at[unit[1]] if unit[0] == 0 else mine(unit),
            dst_ref=held.at[slot, core],
            send_sem=pair_send.at[slot],
            recv_sem=pair_recv.at[slot],
            device_id=pair,
            device_id_type=MESH,
        )

    rings = [
        ring(0, normed_ref.at[0], right, (1, 0)),
        ring(1, normed_ref.at[0], left, (3, 0)),
        ring(2, normed_ref.at[1], right, (1, 1)),
        ring(3, mine((1, 0)), right, (2, 0)),
        ring(4, mine((1, 1)), right, (2, 1)),
        ring(5, mine((2, 1)), right, (3, 1)),
    ]
    pairs = {unit: to_pair(unit) for unit in UNITS}
    side = [
        pltpu.make_async_remote_copy(
            src_ref=source,
            dst_ref=target,
            send_sem=slot_send.at[number],
            recv_sem=slot_recv.at[number],
            device_id=following,
            device_id_type=MESH,
        )
        for number, (source, target) in enumerate(
            [(slots_ref, slots_before_ref), (owner_ref, owner_before_ref)]
        )
    ]

    def lead_copy(number, to):
        return pltpu.make_async_remote_copy(
            src_ref=lead_ref,
            dst_ref=lead_ref,
            send_sem=lead_send.at[number],
            recv_sem=lead_recv,
            device_id=(to, head),
            device_id_type=MESH,
        )

    along_z = [lead_copy(to - 1, jnp.int32(to)) for to in range(1, Z)]
    along_x = [lead_copy(Z - 2 + to, to * Z + z) for to in range(1, n_seq // Z)]

    def row_starts(number):
        distance = pick(number, [unit[0] for unit in UNITS])
        later = pick(number, [unit[1] for unit in UNITS])
        first = lax.rem(y - distance + Y, Y) * (4 * half) + later * half
        second = lax.rem(y + distance, Y) * (4 * half) + 2 * half + later * half
        return pl.multiple_of(first, half), pl.multiple_of(second, half)

    def kv_copies(number):
        return [
            pltpu.make_async_remote_copy(
                src_ref=kv_ref.at[:, pl.ds(start, half), :],
                dst_ref=before_ref.at[:, pl.ds(start, half), :],
                send_sem=kv_send.at[2 * number + part],
                recv_sem=kv_recv.at[2 * number + part],
                device_id=following,
                device_id_type=MESH,
            )
            for part, start in enumerate(row_starts(number))
        ]

    rings[0].start()
    pairs[(0, 0)].start()
    rings[1].start()
    rings[2].start()
    pairs[(0, 1)].start()
    for copy in side:
        copy.start()
    def event_0():
        pairs[(0, 0)].wait_recv()

    def event_1():
        pairs[(0, 1)].wait_recv()

    def event_2():
        rings[0].wait_recv()
        rings[3].start()
        pairs[(1, 0)].start()
        pairs[(1, 0)].wait_recv()

    def event_3():
        rings[1].wait_recv()
        pairs[(3, 0)].start()
        rings[2].wait_recv()
        rings[4].start()
        pairs[(1, 1)].start()
        pairs[(3, 0)].wait_recv()

    def event_4():
        pairs[(1, 1)].wait_recv()

    def event_5():
        rings[3].wait_recv()
        pairs[(2, 0)].start()
        pairs[(2, 0)].wait_recv()

    def event_6():
        @pl.when(seq == 0)
        def _():
            lead_ref[...] = q_ref[:, pl.ds(0, LEAD), :]
            for copy in along_z:
                copy.start()
            for copy in along_x:
                copy.start()

        rings[4].wait_recv()
        rings[5].start()
        pairs[(2, 1)].start()
        pairs[(2, 1)].wait_recv()

    def event_7():
        rings[5].wait_recv()
        pairs[(3, 1)].start()

        @pl.when((x == 0) & (z > 0))
        def _():
            along_z[0].wait_recv()
            for copy in along_x:
                copy.start()

        pairs[(3, 1)].wait_recv()

    events = [event_0, event_1, event_2, event_3, event_4, event_5, event_6, event_7]

    @pl.loop(0, len(UNITS))
    def _(number):
        for at, event in enumerate(events):
            pl.when(number == at)(event)
        block = held[number].reshape(2 * half, held.shape[3])
        starts = row_starts(number)
        table = jnp.concatenate([table_ref[pl.ds(start, half), :] for start in starts], axis=0)
        swapped = pltpu.roll(table, HD // 2, 1)
        low = lax.broadcasted_iota(jnp.int32, table.shape, 1) < HD // 2
        cosine = jnp.where(low, table, swapped)
        sine = jnp.where(low, -swapped, table)

        def turned(product):
            return (product * cosine + pltpu.roll(product, HD // 2, 1) * sine).astype(jnp.bfloat16)

        def put(ref, at, rows):
            for part, start in enumerate(starts):
                ref[at, pl.ds(start, half), :] = rows[part * half : (part + 1) * half]

        both = dot32(block, jnp.concatenate([wk_ref[...], wv_ref[...]], axis=1))
        put(kv_ref, 0, turned(both[:, :HD]))
        put(kv_ref, 1, both[:, HD:].astype(jnp.bfloat16))
        product = dot32(block, wq_ref[...])
        for at in range(heads):
            put(q_ref, at, turned(product[:, at * HD : (at + 1) * HD]))
        for copy in kv_copies(number):
            copy.start()

    @pl.loop(0, len(UNITS))
    def _(number):
        for copy in kv_copies(number):
            copy.wait_recv()
            copy.wait_send()

    for copy in rings:
        copy.wait_send()
    for unit in UNITS:
        pairs[unit].wait_send()
    for copy in side:
        copy.wait_recv()
        copy.wait_send()

    @pl.when(seq == 0)
    def _():
        for copy in along_z:
            copy.wait_send()

    @pl.when(x == 0)
    def _():
        for copy in along_x:
            copy.wait_send()

    @pl.when(x > 0)
    def _():
        along_x[0].wait_recv()


def gather_project(tokens, gain, w_query, w_key, w_value, table, slots, owner):
    rows, width = table.shape[0], tokens.shape[-1]
    heads = w_query.shape[1] // HD
    half = tokens.shape[1]
    vmem = pl.BlockSpec(memory_space=pltpu.VMEM)
    dma = pltpu.SemaphoreType.DMA
    shape = jax.ShapeDtypeStruct
    return pl.pallas_call(
        gather_kernel,
        in_specs=[vmem] * 8,
        out_specs=[vmem] * 6,
        out_shape=[
            shape((heads, rows, HD), jnp.bfloat16),
            shape((2, rows, HD), jnp.bfloat16),
            shape((2, rows, HD), jnp.bfloat16),
            shape(slots.shape, jnp.bfloat16),
            shape(owner.shape, jnp.int32),
            shape((heads, LEAD, HD), jnp.bfloat16),
        ],
        scratch_shapes=[
            pltpu.VMEM((2, half, width), jnp.bfloat16),
            pltpu.VMEM((len(UNITS), 2, half, width), jnp.bfloat16),
            dma((6,)),
            dma((len(UNITS),)),
            dma((len(UNITS),)),
            dma((len(UNITS),)),
            dma((2 * len(UNITS),)),
            dma((2 * len(UNITS),)),
            dma((2,)),
            dma((2,)),
            dma((Z + 2,)),
            dma,
        ],
        compiler_params=pltpu.CompilerParams(
            collective_id=0, has_side_effects=True, vmem_limit_bytes=LIMIT
        ),
        name="gather_project",
    )(tokens, gain, w_query, w_key, w_value, table, slots, owner)


def local_kernel(
    begin_smem,
    q_ref,
    before_ref,
    here_ref,
    slot_before_ref,
    slot_here_ref,
    owner_before_ref,
    owner_here_ref,
    request_ref,
    begin_ref,
    lead_ref,
    cache_ref,
    out_ref,
    near_mix_ref,
    near_top_ref,
    near_sum_ref,
    long_mix_ref,
    long_stat_ref,
    window,
    top_ref,
    sum_ref,
    mix_ref,
):
    step = pl.program_id(0)
    rows = here_ref.shape[1]
    heads, tile, _ = q_ref.shape
    chunk = 2 * tile

    @pl.when(step == 0)
    def _():
        window[:, pl.ds(0, tile)] = jnp.zeros((2, tile, HD), jnp.bfloat16)
        window[:, pl.ds(tile, rows)] = before_ref[...]
        window[:, pl.ds(tile + rows, rows)] = here_ref[...]
        long_state(lead_ref, cache_ref, long_mix_ref, long_stat_ref)

    def column(ref):
        spread = jnp.broadcast_to(ref[...].astype(jnp.float32), (tile, tile))
        return jnp.concatenate([jnp.transpose(spread).astype(jnp.int32)] * 2, axis=1)

    request = column(request_ref)
    begin = column(begin_ref)
    lanes = lax.broadcasted_iota(jnp.int32, (tile, chunk), 1)
    index = rows + step * tile + lax.broadcasted_iota(jnp.int32, (tile, chunk), 0)

    def take(keys, values, valid, fresh):
        scores = dot_t(q_ref[...].reshape(heads * tile, HD), keys) * SCALE
        scores = jnp.where(jnp.concatenate([valid] * heads, axis=0), scores, LOW)
        top = jnp.max(scores, axis=1, keepdims=True)
        if not fresh:
            old = top_ref[...]
            top = jnp.maximum(top, old)
            keep = jnp.exp(old - top)
        weights = jnp.exp(scores - top)
        total = jnp.sum(weights, axis=1, keepdims=True)
        mixed = dot32(weights.astype(jnp.bfloat16), values)
        top_ref[...] = top
        if fresh:
            sum_ref[...] = total
            mix_ref[...] = mixed
        else:
            sum_ref[...] = sum_ref[...] * keep + total
            mix_ref[...] = mix_ref[...] * keep + mixed

    end = rows + (step + 1) * tile

    def new_chunk(number, fresh):
        key = end - (number + 1) * chunk
        key_at = key + lanes
        valid = (key_at >= begin) & (key_at <= index)
        at = pl.multiple_of(key + tile, tile)
        take(window[0, pl.ds(at, chunk), :], window[1, pl.ds(at, chunk), :], valid, fresh)

    first = begin_smem[step * tile]
    last = begin_smem[step * tile + tile - 1]
    new_chunk(0, True)

    @pl.loop(1, (end - first + chunk - 1) // chunk)
    def _(number):
        new_chunk(number, False)

    @pl.when(first < rows)
    def _():
        take(slot_before_ref[0], slot_before_ref[1], owner_before_ref[...] == request, False)

    @pl.when(last >= rows)
    def _():
        take(slot_here_ref[0], slot_here_ref[1], owner_here_ref[...] == request, False)

    mixed = mix_ref[...] / sum_ref[...]
    for head in range(heads):
        out_ref[:, head * HD : (head + 1) * HD] = mixed[head * tile : (head + 1) * tile].astype(
            jnp.bfloat16
        )

    @pl.when(step == 0)
    def _():
        for head in range(heads):
            lead = pl.ds(head * tile, LEAD)
            near_mix_ref[head] = mix_ref[lead, :]
            near_top_ref[head] = jnp.broadcast_to(top_ref[lead, :], (LEAD, HD))
            near_sum_ref[head] = jnp.broadcast_to(sum_ref[lead, :], (LEAD, HD))


def long_state(q_ref, cache_ref, mix_ref, stat_ref):
    heads = q_ref.shape[0]
    queries = jnp.concatenate([q_ref[at] for at in range(heads)] + [q_ref[heads - 1]], axis=0)
    scores = dot_t(cache_ref[0], queries) * SCALE
    top = jnp.max(scores, axis=0, keepdims=True)
    weights = jnp.exp(scores - top)
    mixed = lax.dot_general(
        cache_ref[1],
        weights.astype(jnp.bfloat16),
        (((0,), (0,)), ((), ())),
        preferred_element_type=jnp.float32,
    )
    mix_ref[...] = mixed.astype(jnp.bfloat16)
    stat_ref[...] = jnp.zeros_like(stat_ref)
    stat_ref[0:1, :] = top
    stat_ref[1:2, :] = jnp.sum(weights, axis=0, keepdims=True)


def local_attention(
    begin, queries, before, here, slot_before, slot_here, owner_before, owner_here, request, lead, cache
):
    heads, rows, _ = queries.shape
    tile = HD
    columns = (heads + 1) * LEAD

    def whole(array):
        return pl.BlockSpec(array.shape, lambda i, first: (0,) * len(array.shape))

    shape = jax.ShapeDtypeStruct
    near = shape((heads, LEAD, HD), jnp.float32)
    long_mix = shape((HD, columns), jnp.bfloat16)
    long_stat = shape((8, columns), jnp.float32)
    row = pl.BlockSpec((1, tile), lambda i, first: (0, i))
    kept = [before, here, slot_before, slot_here, owner_before, owner_here]
    return pl.pallas_call(
        local_kernel,
        grid_spec=pltpu.PrefetchScalarGridSpec(
            num_scalar_prefetch=1,
            grid=(rows // tile,),
            in_specs=[pl.BlockSpec((heads, tile, HD), lambda i, first: (0, i, 0))]
            + [whole(array) for array in kept]
            + [row, row, whole(lead), whole(cache)],
            out_specs=[pl.BlockSpec((tile, heads * HD), lambda i, first: (i, 0))]
            + [whole(array) for array in (near, near, near, long_mix, long_stat)],
            scratch_shapes=[
                pltpu.VMEM((2, tile + 2 * rows, HD), jnp.bfloat16),
                pltpu.VMEM((heads * tile, 1), jnp.float32),
                pltpu.VMEM((heads * tile, 1), jnp.float32),
                pltpu.VMEM((heads * tile, HD), jnp.float32),
            ],
        ),
        out_shape=[shape((rows, heads * HD), jnp.bfloat16), near, near, near, long_mix, long_stat],
        name="local_attention",
    )(begin, queries, *kept, request[None, :], begin[None, :], lead, cache)


def merge(into, top, total, part, part_top, part_total):
    highest = jnp.maximum(top, part_top)
    keep, add = jnp.exp(top - highest), jnp.exp(part_top - highest)
    return into * keep + part * add, highest, total * keep + part_total * add


PIECES = 4


def scatter_kernel(
    attended_ref,
    w_ref,
    long_mix_ref,
    long_stat_ref,
    near_mix_ref,
    near_top_ref,
    near_sum_ref,
    out_ref,
    pair_out,
    pair_in,
    own,
    ring_out,
    ring_in,
    mix_out,
    stat_out,
    mix_in,
    stat_in,
    pair_send,
    pair_recv,
    ring_send,
    ring_recv,
    sends,
    recvs,
):
    seq, head, y, core = place()
    n_x = lax.axis_size("seq") // Z
    x, z = seq // Z, lax.rem(seq, Z)
    way = 1 - 2 * core
    right = (seq, lax.rem(y + way + Y, Y) * 2 + core)
    left = (seq, lax.rem(y - way + Y, Y) * 2 + core)
    pair = (seq, head + way)
    half = ring_out.shape[2]
    heads = near_mix_ref.shape[0]
    width = w_ref.shape[1] // PIECES
    barrier = pltpu.get_barrier_semaphore()

    for device in (right, left, pair):
        greet(device)

    @pl.when(z > 0)
    def _():
        greet((x * Z, head))
        pl.semaphore_wait(barrier, 3 + 1)

    @pl.when((z == 0) & (x > 0))
    def _():
        for at in range(1, Z):
            greet((x * Z + at, head))
        greet((0, head))
        pl.semaphore_wait(barrier, 3 + Z)

    @pl.when(seq == 0)
    def _():
        for at in range(1, Z):
            greet((at, head))
        for at in range(1, n_x):
            greet((at * Z, head))
        pl.semaphore_wait(barrier, 3 + Z - 1 + n_x - 1)

    def columns(piece):
        return pl.ds(piece * width, width)

    def rows_of(chip, of_core, later):
        return attended_ref[pl.ds(pl.multiple_of(chip * (4 * half) + of_core * (2 * half) + later * half, half), half), :]

    def stack(later):
        parts = [rows_of(lax.rem(y - k * way + 2 * Y * 2, Y), 1 - core, later) for k in range(Y)]
        parts += [rows_of(lax.rem(y + k * way + 2 * Y * 2, Y), core, later) for k in range(Y)]
        return jnp.concatenate(parts, axis=0)

    def pair_copy(later, piece):
        return pltpu.make_async_remote_copy(
            src_ref=pair_out.at[later, :, columns(piece)],
            dst_ref=pair_in.at[later, :, columns(piece)],
            send_sem=pair_send.at[later, piece],
            recv_sem=pair_recv.at[later, piece],
            device_id=pair,
            device_id_type=MESH,
        )

    def ring_copy(later, step, piece):
        return pltpu.make_async_remote_copy(
            src_ref=ring_out.at[later, step, :, columns(piece)],
            dst_ref=ring_in.at[later, step, :, columns(piece)],
            send_sem=ring_send.at[later, step, piece],
            recv_sem=ring_recv.at[later, step, piece],
            device_id=left if (later, step) == (0, 2) else right,
            device_id_type=MESH,
        )

    def project(rows, later, piece):
        product = dot32(rows, w_ref[:, columns(piece)]).astype(jnp.bfloat16)
        pair_out[later, :, columns(piece)] = product[: Y * half]
        own[later, :, columns(piece)] = product[Y * half :]

    def chip_sum(later, k, piece):
        rows = pl.ds(k * half, half)
        return own[later, rows, columns(piece)].astype(jnp.float32) + pair_in[
            later, rows, columns(piece)
        ].astype(jnp.float32)

    def arrived(later, step, piece):
        ring_copy(later, step, piece).wait_recv()
        return ring_in[later, step, :, columns(piece)].astype(jnp.float32)

    def pass_on(later, step, piece, value):
        ring_out[later, step, :, columns(piece)] = value.astype(jnp.bfloat16)
        ring_copy(later, step, piece).start()

    def first_hop(piece):
        pair_copy(1, piece).wait_recv()
        pass_on(1, 0, piece, chip_sum(1, 3, piece))

    def keep_state(mixed, top, total):
        mix_out[...] = mixed.astype(jnp.bfloat16)
        stat_out[0:1, :] = top
        stat_out[1:2, :] = total

    def state_copies(slot, to, sources):
        return [
            pltpu.make_async_remote_copy(
                src_ref=source,
                dst_ref=target.at[slot],
                send_sem=sends.at[number],
                recv_sem=recvs.at[number, slot],
                device_id=(to, head),
                device_id_type=MESH,
            )
            for number, (source, target) in enumerate(zip(sources, (mix_in, stat_in)))
        ]

    def collect(slots, sources):
        mix, stat = sources
        state = (mix[...].astype(jnp.float32), stat[0:1, :], stat[1:2, :])
        for slot in slots:
            for copy in state_copies(slot, jnp.int32(0), sources):
                copy.wait_recv()
            state = merge(
                *state,
                mix_in[slot].astype(jnp.float32),
                stat_in[slot, 0:1, :],
                stat_in[slot, 1:2, :],
            )
        return state

    computed = (long_mix_ref, long_stat_ref)
    merged = (mix_out, stat_out)
    for at in range(1, Z):
        @pl.when(z == at)
        def _():
            for copy in state_copies(at - 1, x * Z, computed):
                copy.start()

    rows = stack(1)
    for piece in range(PIECES):
        project(rows, 1, piece)
        pair_copy(1, piece).start()
        if piece:
            first_hop(piece - 1)
    first_hop(PIECES - 1)

    rows = stack(0)
    for piece in range(PIECES):
        project(rows, 0, piece)

    for piece in range(PIECES):
        pass_on(1, 1, piece, chip_sum(1, 2, piece) + arrived(1, 0, piece))

    @pl.when(z == 0)
    def _():
        stat_out[...] = jnp.zeros_like(stat_out)
        keep_state(*collect(range(Z - 1), computed))

    for at in range(1, n_x):
        @pl.when((z == 0) & (x == at))
        def _():
            for copy in state_copies(Z - 2 + at, jnp.int32(0), merged):
                copy.start()

    for piece in range(PIECES):
        pass_on(1, 2, piece, chip_sum(1, 1, piece) + arrived(1, 1, piece))

    @pl.when(seq == 0)
    def _():
        mixed, top, total = collect(range(Z - 1, Z + n_x - 2), merged)
        mixed = jnp.transpose(mixed)
        top = jnp.transpose(jnp.broadcast_to(top, mix_out.shape))
        total = jnp.transpose(jnp.broadcast_to(total, mix_out.shape))
        parts = []
        for at in range(heads):
            lead = slice(at * LEAD, (at + 1) * LEAD)
            joined = merge(
                near_mix_ref[at],
                near_top_ref[at],
                near_sum_ref[at],
                mixed[lead],
                top[lead],
                total[lead],
            )
            parts.append((joined[0] / joined[2]).astype(jnp.bfloat16))
        lead_rows = jnp.concatenate(parts, axis=1)
        for piece in range(PIECES):
            product = dot32(lead_rows, w_ref[:, columns(piece)]).astype(jnp.bfloat16)

            @pl.when(core == 0)
            def _():
                at = pl.multiple_of(lax.rem(Y - y, Y) * half, half)
                own[0, pl.ds(at, half), columns(piece)] = product

            @pl.when(core == 1)
            def _():
                at = pl.multiple_of(lax.rem(Y - y, Y) * half, half)
                pair_out[0, pl.ds(at, half), columns(piece)] = product

    for piece in range(PIECES):
        pair_copy(0, piece).start()
    for piece in range(PIECES):
        pair_copy(0, piece).wait_recv()
        pass_on(0, 0, piece, chip_sum(0, 2, piece))
        pass_on(0, 2, piece, chip_sum(0, 3, piece))
    for piece in range(PIECES):
        value = chip_sum(1, 0, piece) + arrived(1, 2, piece)
        out_ref[pl.ds(half, half), columns(piece)] = value.astype(jnp.bfloat16)
    for piece in range(PIECES):
        pass_on(0, 1, piece, chip_sum(0, 1, piece) + arrived(0, 0, piece))
    for piece in range(PIECES):
        value = chip_sum(0, 0, piece) + arrived(0, 2, piece) + arrived(0, 1, piece)
        out_ref[pl.ds(0, half), columns(piece)] = value.astype(jnp.bfloat16)

    for later in range(2):
        for piece in range(PIECES):
            pair_copy(later, piece).wait_send()
            for step in range(3):
                ring_copy(later, step, piece).wait_send()

    @pl.when(seq > 0)
    def _():
        for copy in state_copies(0, jnp.int32(0), merged):
            copy.wait_send()


def project_scatter(attended, w_out, long_mix, long_stat, near_mix, near_top, near_sum):
    rows, inner = attended.shape
    width = w_out.shape[1]
    half = LEAD
    slots = Z - 1 + 3
    queries = long_mix.shape[1]
    vmem = pl.BlockSpec(memory_space=pltpu.VMEM)
    dma = pltpu.SemaphoreType.DMA
    return pl.pallas_call(
        scatter_kernel,
        in_specs=[vmem] * 7,
        out_specs=vmem,
        out_shape=jax.ShapeDtypeStruct((2 * half, width), jnp.bfloat16),
        scratch_shapes=[
            pltpu.VMEM((2, Y * half, width), jnp.bfloat16),
            pltpu.VMEM((2, Y * half, width), jnp.bfloat16),
            pltpu.VMEM((2, Y * half, width), jnp.bfloat16),
            pltpu.VMEM((2, 3, half, width), jnp.bfloat16),
            pltpu.VMEM((2, 3, half, width), jnp.bfloat16),
            pltpu.VMEM((HD, queries), jnp.bfloat16),
            pltpu.VMEM((8, queries), jnp.float32),
            pltpu.VMEM((slots, HD, queries), jnp.bfloat16),
            pltpu.VMEM((slots, 8, queries), jnp.float32),
            dma((2, PIECES)),
            dma((2, PIECES)),
            dma((2, 3, PIECES)),
            dma((2, 3, PIECES)),
            dma((2,)),
            dma((2, slots)),
        ],
        compiler_params=pltpu.CompilerParams(
            collective_id=1, has_side_effects=True, vmem_limit_bytes=LIMIT
        ),
        name="project_scatter",
    )(attended, w_out, long_mix, long_stat, near_mix, near_top, near_sum)


def on_device(
    tokens,
    norm_gain,
    w_query,
    w_key,
    w_value,
    w_out,
    long_cache,
    short_cache,
    slot_owner,
    new_len,
    cache_len,
):
    seq_index = lax.axis_index("seq")
    long_len = long_cache.shape[1] * lax.axis_size("seq")
    rows = tokens.shape[0] * lax.axis_size("head")
    starts = request_starts(new_len)
    token_index = seq_index * rows + jnp.arange(rows, dtype=jnp.int32)
    request, begin, position = token_facts(token_index, starts, cache_len, long_len)
    table = rotate_table(position)
    queries, here, before, earlier_slots, earlier_owner, lead_queries = gather_project(
        tokens.reshape(2, LEAD, tokens.shape[1]),
        norm_gain[None, :],
        w_query,
        w_key,
        w_value,
        table,
        short_cache,
        slot_owner[None, :],
    )
    shift = (seq_index - 1) * rows
    window_begin = jnp.where(request == starts.shape[0], rows, jnp.maximum(begin - shift, 0))
    attended, near_mix, near_top, near_sum, long_mix, long_stat = local_attention(
        window_begin,
        queries,
        before,
        here,
        earlier_slots,
        short_cache,
        earlier_owner,
        slot_owner[None, :],
        request,
        lead_queries,
        long_cache,
    )
    return project_scatter(attended, w_out, long_mix, long_stat, near_mix, near_top, near_sum)


def solution(mesh):
    placed = (
        P(("seq", "head"), None),
        P(),
        P(None, "head"),
        P(None, "head"),
        P(None, "head"),
        P("head", None),
        P(None, "seq", "head"),
        P(None, "seq", "head"),
        P("seq"),
        P(),
        P(),
    )
    return jax.shard_map(
        on_device, mesh=mesh, in_specs=placed, out_specs=P(("seq", "head"), None), check_vma=False
    )
```

```python
import math

import jax
import jax.numpy as jnp
from jax import lax
from jax.experimental import pallas as pl
from jax.experimental.pallas import tpu as pltpu
from jax.sharding import PartitionSpec as P

HD = 128
LEAD = 64
THETA_LOG = math.log(500000.0)
SCALE = 1.0 / math.sqrt(HD)
LOW = -1e30


def request_starts(new_len):
    return LEAD + jnp.cumsum(new_len) - new_len


def token_facts(token_index, starts, cache_len, long_len):
    number = starts.shape[0]
    passed = (starts[None, :] <= token_index[:, None]).astype(jnp.int32)
    request = jnp.sum(passed, axis=1) - 1
    select = jnp.arange(number, dtype=jnp.int32)[None, :] == request[:, None]
    begin = jnp.sum(jnp.where(select, starts[None, :], 0), axis=1)
    cached = jnp.sum(jnp.where(select, cache_len[None, :], 0), axis=1)
    lead = request < 0
    position = jnp.where(lead, token_index + long_len, token_index - begin + cached)
    return jnp.where(lead, number, request), begin, position


def normalize(tokens, norm_gain):
    values = tokens.astype(jnp.float32)
    mean_square = jnp.mean(values * values, axis=-1, keepdims=True)
    return (values * lax.rsqrt(mean_square + 1e-05) * norm_gain).astype(jnp.bfloat16)


def rotate_table(position):
    half = HD // 2
    frequency = jnp.exp(jnp.arange(half, dtype=jnp.float32) * (-2.0 * THETA_LOG / HD))
    angle = position.astype(jnp.float32)[:, None] * frequency[None, :]
    return jnp.concatenate([jnp.cos(angle), jnp.sin(angle)], axis=1)


def dot32(a, b):
    return jnp.dot(a, b, preferred_element_type=jnp.float32)


def dot_t(a, b):
    return lax.dot_general(a, b, (((1,), (1,)), ((), ())), preferred_element_type=jnp.float32)


MESH = pl.DeviceIdType.MESH
LIMIT = 60 * 1024 * 1024
Z = 8
Y = 4
UNITS = [(0, 0), (0, 1), (1, 0), (3, 0), (1, 1), (2, 0), (2, 1), (3, 1)]
SLOT = {unit: number for number, unit in enumerate(UNITS)}


def place():
    seq = lax.axis_index("seq")
    head = lax.axis_index("head")
    return seq, head, head // 2, lax.rem(head, 2)


def pick(number, table):
    value = jnp.int32(table[0])
    for at, entry in enumerate(table):
        value = jnp.where(number == at, jnp.int32(entry), value)
    return value


def greet(device):
    pl.semaphore_signal(
        pltpu.get_barrier_semaphore(), inc=1, device_id=device, device_id_type=MESH
    )


def gather_kernel(
    tokens_ref,
    gain_ref,
    wq_ref,
    wk_ref,
    wv_ref,
    table_ref,
    slots_ref,
    owner_ref,
    q_ref,
    kv_ref,
    before_ref,
    slots_before_ref,
    owner_before_ref,
    lead_ref,
    normed_ref,
    held,
    ring_send,
    ring_recv,
    pair_send,
    pair_recv,
    kv_send,
    kv_recv,
    slot_send,
    slot_recv,
    lead_send,
    lead_recv,
):
    seq, head, y, core = place()
    n_seq = lax.axis_size("seq")
    x, z = seq // Z, lax.rem(seq, Z)
    way = 1 - 2 * core
    right = (seq, lax.rem(y + way + Y, Y) * 2 + core)
    left = (seq, lax.rem(y - way + Y, Y) * 2 + core)
    pair = (seq, head + way)
    following = (lax.rem(seq + 1, n_seq), head)
    previous = (lax.rem(seq + n_seq - 1, n_seq), head)
    heads = q_ref.shape[0]
    half = held.shape[2]

    for device in (right, left, pair, following, previous):
        greet(device)

    @pl.when(seq == 0)
    def _():
        for to in range(1, Z):
            greet((to, head))

    @pl.when(x == 0)
    def _():
        for to in range(1, n_seq // Z):
            greet((to * Z + z, head))

    @pl.when((x == 0) & (z > 0))
    def _():
        greet((0, head))

    @pl.when(x > 0)
    def _():
        greet((z, head))

    for later in range(2):
        normed_ref[later] = normalize(tokens_ref[later], gain_ref[...])
        held[SLOT[(0, later)], core] = normed_ref[later]

    barrier = pltpu.get_barrier_semaphore()
    others = n_seq // Z - 1

    @pl.when(seq == 0)
    def _():
        pl.semaphore_wait(barrier, 5 + Z - 1 + others)

    @pl.when((x == 0) & (z > 0))
    def _():
        pl.semaphore_wait(barrier, 5 + 1 + others)

    @pl.when(x > 0)
    def _():
        pl.semaphore_wait(barrier, 5 + 1)

    def ring(number, source, to, unit):
        slot = SLOT[unit]
        return pltpu.make_async_remote_copy(
            src_ref=source,
            dst_ref=held.at[slot, core],
            send_sem=ring_send.at[number],
            recv_sem=ring_recv.at[slot],
            device_id=to,
            device_id_type=MESH,
        )

    def mine(unit):
        return held.at[SLOT[unit], core]

    def to_pair(unit):
        slot = SLOT[unit]
        return pltpu.make_async_remote_copy(
            src_ref=normed_ref.at[unit[1]] if unit[0] == 0 else mine(unit),
            dst_ref=held.at[slot, core],
            send_sem=pair_send.at[slot],
            recv_sem=pair_recv.at[slot],
            device_id=pair,
            device_id_type=MESH,
        )

    rings = [
        ring(0, normed_ref.at[0], right, (1, 0)),
        ring(1, normed_ref.at[0], left, (3, 0)),
        ring(2, normed_ref.at[1], right, (1, 1)),
        ring(3, mine((1, 0)), right, (2, 0)),
        ring(4, mine((1, 1)), right, (2, 1)),
        ring(5, mine((2, 1)), right, (3, 1)),
    ]
    pairs = {unit: to_pair(unit) for unit in UNITS}
    side = [
        pltpu.make_async_remote_copy(
            src_ref=source,
            dst_ref=target,
            send_sem=slot_send.at[number],
            recv_sem=slot_recv.at[number],
            device_id=following,
            device_id_type=MESH,
        )
        for number, (source, target) in enumerate(
            [(slots_ref, slots_before_ref), (owner_ref, owner_before_ref)]
        )
    ]

    def lead_copy(number, to):
        return pltpu.make_async_remote_copy(
            src_ref=lead_ref,
            dst_ref=lead_ref,
            send_sem=lead_send.at[number],
            recv_sem=lead_recv,
            device_id=(to, head),
            device_id_type=MESH,
        )

    along_z = [lead_copy(to - 1, jnp.int32(to)) for to in range(1, Z)]
    along_x = [lead_copy(Z - 2 + to, to * Z + z) for to in range(1, n_seq // Z)]

    def row_starts(number):
        distance = pick(number, [unit[0] for unit in UNITS])
        later = pick(number, [unit[1] for unit in UNITS])
        first = lax.rem(y - distance + Y, Y) * (4 * half) + later * half
        second = lax.rem(y + distance, Y) * (4 * half) + 2 * half + later * half
        return pl.multiple_of(first, half), pl.multiple_of(second, half)

    def kv_copies(number):
        return [
            pltpu.make_async_remote_copy(
                src_ref=kv_ref.at[:, pl.ds(start, half), :],
                dst_ref=before_ref.at[:, pl.ds(start, half), :],
                send_sem=kv_send.at[2 * number + part],
                recv_sem=kv_recv.at[2 * number + part],
                device_id=following,
                device_id_type=MESH,
            )
            for part, start in enumerate(row_starts(number))
        ]

    rings[0].start()
    pairs[(0, 0)].start()
    rings[1].start()
    rings[2].start()
    pairs[(0, 1)].start()
    for copy in side:
        copy.start()
    def event_0():
        pairs[(0, 0)].wait_recv()

    def event_1():
        pairs[(0, 1)].wait_recv()

    def event_2():
        rings[0].wait_recv()
        rings[3].start()
        pairs[(1, 0)].start()
        pairs[(1, 0)].wait_recv()

    def event_3():
        rings[1].wait_recv()
        pairs[(3, 0)].start()
        rings[2].wait_recv()
        rings[4].start()
        pairs[(1, 1)].start()
        pairs[(3, 0)].wait_recv()

    def event_4():
        pairs[(1, 1)].wait_recv()

    def event_5():
        rings[3].wait_recv()
        pairs[(2, 0)].start()
        pairs[(2, 0)].wait_recv()

    def event_6():
        @pl.when(seq == 0)
        def _():
            lead_ref[...] = q_ref[:, pl.ds(0, LEAD), :]
            for copy in along_z:
                copy.start()
            for copy in along_x:
                copy.start()

        rings[4].wait_recv()
        rings[5].start()
        pairs[(2, 1)].start()
        pairs[(2, 1)].wait_recv()

    def event_7():
        rings[5].wait_recv()
        pairs[(3, 1)].start()

        @pl.when((x == 0) & (z > 0))
        def _():
            along_z[0].wait_recv()
            for copy in along_x:
                copy.start()

        pairs[(3, 1)].wait_recv()

    events = [event_0, event_1, event_2, event_3, event_4, event_5, event_6, event_7]

    @pl.loop(0, len(UNITS))
    def _(number):
        for at, event in enumerate(events):
            pl.when(number == at)(event)
        block = held[number].reshape(2 * half, held.shape[3])
        starts = row_starts(number)
        table = jnp.concatenate([table_ref[pl.ds(start, half), :] for start in starts], axis=0)
        swapped = pltpu.roll(table, HD // 2, 1)
        low = lax.broadcasted_iota(jnp.int32, table.shape, 1) < HD // 2
        cosine = jnp.where(low, table, swapped)
        sine = jnp.where(low, -swapped, table)

        def turned(product):
            return (product * cosine + pltpu.roll(product, HD // 2, 1) * sine).astype(jnp.bfloat16)

        def put(ref, at, rows):
            for part, start in enumerate(starts):
                ref[at, pl.ds(start, half), :] = rows[part * half : (part + 1) * half]

        both = dot32(block, jnp.concatenate([wk_ref[...], wv_ref[...]], axis=1))
        put(kv_ref, 0, turned(both[:, :HD]))
        put(kv_ref, 1, both[:, HD:].astype(jnp.bfloat16))
        product = dot32(block, wq_ref[...])
        for at in range(heads):
            put(q_ref, at, turned(product[:, at * HD : (at + 1) * HD]))
        for copy in kv_copies(number):
            copy.start()

    @pl.loop(0, len(UNITS))
    def _(number):
        for copy in kv_copies(number):
            copy.wait_recv()
            copy.wait_send()

    for copy in rings:
        copy.wait_send()
    for unit in UNITS:
        pairs[unit].wait_send()
    for copy in side:
        copy.wait_recv()
        copy.wait_send()

    @pl.when(seq == 0)
    def _():
        for copy in along_z:
            copy.wait_send()

    @pl.when(x == 0)
    def _():
        for copy in along_x:
            copy.wait_send()

    @pl.when(x > 0)
    def _():
        along_x[0].wait_recv()


def gather_project(tokens, gain, w_query, w_key, w_value, table, slots, owner):
    rows, width = table.shape[0], tokens.shape[-1]
    heads = w_query.shape[1] // HD
    half = tokens.shape[1]
    vmem = pl.BlockSpec(memory_space=pltpu.VMEM)
    dma = pltpu.SemaphoreType.DMA
    shape = jax.ShapeDtypeStruct
    return pl.pallas_call(
        gather_kernel,
        in_specs=[vmem] * 8,
        out_specs=[vmem] * 6,
        out_shape=[
            shape((heads, rows, HD), jnp.bfloat16),
            shape((2, rows, HD), jnp.bfloat16),
            shape((2, rows, HD), jnp.bfloat16),
            shape(slots.shape, jnp.bfloat16),
            shape(owner.shape, jnp.int32),
            shape((heads, LEAD, HD), jnp.bfloat16),
        ],
        scratch_shapes=[
            pltpu.VMEM((2, half, width), jnp.bfloat16),
            pltpu.VMEM((len(UNITS), 2, half, width), jnp.bfloat16),
            dma((6,)),
            dma((len(UNITS),)),
            dma((len(UNITS),)),
            dma((len(UNITS),)),
            dma((2 * len(UNITS),)),
            dma((2 * len(UNITS),)),
            dma((2,)),
            dma((2,)),
            dma((Z + 2,)),
            dma,
        ],
        compiler_params=pltpu.CompilerParams(
            collective_id=0, has_side_effects=True, vmem_limit_bytes=LIMIT
        ),
        name="gather_project",
    )(tokens, gain, w_query, w_key, w_value, table, slots, owner)


def local_kernel(
    begin_smem,
    q_ref,
    before_ref,
    here_ref,
    slot_before_ref,
    slot_here_ref,
    owner_before_ref,
    owner_here_ref,
    request_ref,
    begin_ref,
    lead_ref,
    cache_ref,
    out_ref,
    near_mix_ref,
    near_stat_ref,
    long_mix_ref,
    long_stat_ref,
    window,
    top_ref,
    sum_ref,
    mix_ref,
):
    step = pl.program_id(0)
    rows = here_ref.shape[1]
    heads, tile, _ = q_ref.shape
    chunk = 2 * tile

    @pl.when(step == 0)
    def _():
        window[:, pl.ds(0, tile)] = jnp.zeros((2, tile, HD), jnp.bfloat16)
        window[:, pl.ds(tile, rows)] = before_ref[...]
        window[:, pl.ds(tile + rows, rows)] = here_ref[...]
        long_state(lead_ref, cache_ref, long_mix_ref, long_stat_ref)

    request = request_ref[...]
    begin = begin_ref[...]
    down = lax.broadcasted_iota(jnp.int32, (chunk, tile), 0)
    index = rows + step * tile + lax.broadcasted_iota(jnp.int32, (1, tile), 1)
    queries = q_ref[...].reshape(heads * tile, HD)

    def take(keys, values, valid, fresh):
        scores = dot_t(keys, queries) * SCALE
        scores = jnp.where(jnp.concatenate([valid] * heads, axis=1), scores, LOW)
        top = jnp.max(scores, axis=0, keepdims=True)
        if not fresh:
            old = top_ref[...]
            top = jnp.maximum(top, old)
            keep = jnp.exp(old - top)
        weights = jnp.exp(scores - top)
        total = jnp.sum(weights, axis=0, keepdims=True)
        mixed = lax.dot_general(
            values,
            weights.astype(jnp.bfloat16),
            (((0,), (0,)), ((), ())),
            preferred_element_type=jnp.float32,
        )
        top_ref[...] = top
        if fresh:
            sum_ref[...] = total
            mix_ref[...] = mixed
        else:
            sum_ref[...] = sum_ref[...] * keep + total
            mix_ref[...] = mix_ref[...] * keep + mixed

    def owner_column(ref):
        spread = jnp.broadcast_to(ref[...].astype(jnp.float32), (tile, ref.shape[1]))
        return jnp.transpose(spread).astype(jnp.int32)

    end = rows + (step + 1) * tile

    def new_chunk(number, fresh):
        key = end - (number + 1) * chunk
        key_at = key + down
        valid = (key_at >= begin) & (key_at <= index)
        at = pl.multiple_of(key + tile, tile)
        take(window[0, pl.ds(at, chunk), :], window[1, pl.ds(at, chunk), :], valid, fresh)

    first = begin_smem[step * tile]
    last = begin_smem[step * tile + tile - 1]
    new_chunk(0, True)

    @pl.loop(1, (end - first + chunk - 1) // chunk)
    def _(number):
        new_chunk(number, False)

    @pl.when(first < rows)
    def _():
        take(slot_before_ref[0], slot_before_ref[1], owner_column(owner_before_ref) == request, False)

    @pl.when(last >= rows)
    def _():
        take(slot_here_ref[0], slot_here_ref[1], owner_column(owner_here_ref) == request, False)

    mixed = mix_ref[...] / sum_ref[...]
    for head in range(heads):
        span = slice(head * tile, (head + 1) * tile)
        out_ref[:, span] = jnp.transpose(mixed[:, span]).astype(jnp.bfloat16)

    @pl.when(step == 0)
    def _():
        def leads(ref):
            parts = [ref[:, head * tile : head * tile + LEAD] for head in range(heads)]
            return jnp.concatenate(parts + parts[-1:], axis=1)

        near_mix_ref[...] = leads(mix_ref)
        near_stat_ref[...] = jnp.zeros_like(near_stat_ref)
        near_stat_ref[0:1, :] = leads(top_ref)
        near_stat_ref[1:2, :] = leads(sum_ref)


def long_state(q_ref, cache_ref, mix_ref, stat_ref):
    heads = q_ref.shape[0]
    queries = jnp.concatenate([q_ref[at] for at in range(heads)] + [q_ref[heads - 1]], axis=0)
    scores = dot_t(cache_ref[0], queries) * SCALE
    top = jnp.max(scores, axis=0, keepdims=True)
    weights = jnp.exp(scores - top)
    mixed = lax.dot_general(
        cache_ref[1],
        weights.astype(jnp.bfloat16),
        (((0,), (0,)), ((), ())),
        preferred_element_type=jnp.float32,
    )
    mix_ref[...] = mixed.astype(jnp.bfloat16)
    stat_ref[...] = jnp.zeros_like(stat_ref)
    stat_ref[0:1, :] = top
    stat_ref[1:2, :] = jnp.sum(weights, axis=0, keepdims=True)


def local_attention(
    begin, queries, before, here, slot_before, slot_here, owner_before, owner_here, request, lead, cache
):
    heads, rows, _ = queries.shape
    tile = HD
    columns = (heads + 1) * LEAD

    def whole(array):
        return pl.BlockSpec(array.shape, lambda i, first: (0,) * len(array.shape))

    shape = jax.ShapeDtypeStruct
    near_mix = shape((HD, columns), jnp.float32)
    long_mix = shape((HD, columns), jnp.bfloat16)
    long_stat = shape((8, columns), jnp.float32)
    row = pl.BlockSpec((1, tile), lambda i, first: (0, i))
    kept = [before, here, slot_before, slot_here, owner_before, owner_here]
    return pl.pallas_call(
        local_kernel,
        grid_spec=pltpu.PrefetchScalarGridSpec(
            num_scalar_prefetch=1,
            grid=(rows // tile,),
            in_specs=[pl.BlockSpec((heads, tile, HD), lambda i, first: (0, i, 0))]
            + [whole(array) for array in kept]
            + [row, row, whole(lead), whole(cache)],
            out_specs=[pl.BlockSpec((tile, heads * HD), lambda i, first: (i, 0))]
            + [whole(array) for array in (near_mix, long_stat, long_mix, long_stat)],
            scratch_shapes=[
                pltpu.VMEM((2, tile + 2 * rows, HD), jnp.bfloat16),
                pltpu.VMEM((1, heads * tile), jnp.float32),
                pltpu.VMEM((1, heads * tile), jnp.float32),
                pltpu.VMEM((HD, heads * tile), jnp.float32),
            ],
        ),
        out_shape=[shape((rows, heads * HD), jnp.bfloat16), near_mix, long_stat, long_mix, long_stat],
        name="local_attention",
    )(begin, queries, *kept, request[None, :], begin[None, :], lead, cache)


def merge(into, top, total, part, part_top, part_total):
    highest = jnp.maximum(top, part_top)
    keep, add = jnp.exp(top - highest), jnp.exp(part_top - highest)
    return into * keep + part * add, highest, total * keep + part_total * add


PIECES = 4


def scatter_kernel(
    attended_ref,
    w_ref,
    long_mix_ref,
    long_stat_ref,
    near_mix_ref,
    near_stat_ref,
    out_ref,
    pair_out,
    pair_in,
    own,
    ring_out,
    ring_in,
    mix_out,
    stat_out,
    mix_in,
    stat_in,
    pair_send,
    pair_recv,
    ring_send,
    ring_recv,
    sends,
    recvs,
):
    seq, head, y, core = place()
    n_x = lax.axis_size("seq") // Z
    x, z = seq // Z, lax.rem(seq, Z)
    way = 1 - 2 * core
    right = (seq, lax.rem(y + way + Y, Y) * 2 + core)
    left = (seq, lax.rem(y - way + Y, Y) * 2 + core)
    pair = (seq, head + way)
    half = ring_out.shape[2]
    heads = w_ref.shape[0] // HD
    width = w_ref.shape[1] // PIECES
    barrier = pltpu.get_barrier_semaphore()

    for device in (right, left, pair):
        greet(device)

    @pl.when(z > 0)
    def _():
        greet((x * Z, head))
        pl.semaphore_wait(barrier, 3 + 1)

    @pl.when((z == 0) & (x > 0))
    def _():
        for at in range(1, Z):
            greet((x * Z + at, head))
        greet((0, head))
        pl.semaphore_wait(barrier, 3 + Z)

    @pl.when(seq == 0)
    def _():
        for at in range(1, Z):
            greet((at, head))
        for at in range(1, n_x):
            greet((at * Z, head))
        pl.semaphore_wait(barrier, 3 + Z - 1 + n_x - 1)

    def columns(piece):
        return pl.ds(piece * width, width)

    def rows_of(chip, of_core, later):
        return attended_ref[pl.ds(pl.multiple_of(chip * (4 * half) + of_core * (2 * half) + later * half, half), half), :]

    def stack(later):
        parts = [rows_of(lax.rem(y - k * way + 2 * Y * 2, Y), 1 - core, later) for k in range(Y)]
        parts += [rows_of(lax.rem(y + k * way + 2 * Y * 2, Y), core, later) for k in range(Y)]
        return jnp.concatenate(parts, axis=0)

    def pair_copy(later, piece):
        return pltpu.make_async_remote_copy(
            src_ref=pair_out.at[later, :, columns(piece)],
            dst_ref=pair_in.at[later, :, columns(piece)],
            send_sem=pair_send.at[later, piece],
            recv_sem=pair_recv.at[later, piece],
            device_id=pair,
            device_id_type=MESH,
        )

    def ring_copy(later, step, piece):
        return pltpu.make_async_remote_copy(
            src_ref=ring_out.at[later, step, :, columns(piece)],
            dst_ref=ring_in.at[later, step, :, columns(piece)],
            send_sem=ring_send.at[later, step, piece],
            recv_sem=ring_recv.at[later, step, piece],
            device_id=left if (later, step) == (0, 2) else right,
            device_id_type=MESH,
        )

    def project(rows, later, piece):
        product = dot32(rows, w_ref[:, columns(piece)]).astype(jnp.bfloat16)
        pair_out[later, :, columns(piece)] = product[: Y * half]
        own[later, :, columns(piece)] = product[Y * half :]

    def chip_sum(later, k, piece):
        rows = pl.ds(k * half, half)
        return own[later, rows, columns(piece)].astype(jnp.float32) + pair_in[
            later, rows, columns(piece)
        ].astype(jnp.float32)

    def arrived(later, step, piece):
        ring_copy(later, step, piece).wait_recv()
        return ring_in[later, step, :, columns(piece)].astype(jnp.float32)

    def pass_on(later, step, piece, value):
        ring_out[later, step, :, columns(piece)] = value.astype(jnp.bfloat16)
        ring_copy(later, step, piece).start()

    def first_hop(piece):
        pair_copy(1, piece).wait_recv()
        pass_on(1, 0, piece, chip_sum(1, 3, piece))

    def keep_state(mixed, top, total):
        mix_out[...] = mixed.astype(jnp.bfloat16)
        stat_out[0:1, :] = top
        stat_out[1:2, :] = total

    def state_copies(slot, to, sources):
        return [
            pltpu.make_async_remote_copy(
                src_ref=source,
                dst_ref=target.at[slot],
                send_sem=sends.at[number],
                recv_sem=recvs.at[number, slot],
                device_id=(to, head),
                device_id_type=MESH,
            )
            for number, (source, target) in enumerate(zip(sources, (mix_in, stat_in)))
        ]

    def collect(slots, sources):
        mix, stat = sources
        state = (mix[...].astype(jnp.float32), stat[0:1, :], stat[1:2, :])
        for slot in slots:
            for copy in state_copies(slot, jnp.int32(0), sources):
                copy.wait_recv()
            state = merge(
                *state,
                mix_in[slot].astype(jnp.float32),
                stat_in[slot, 0:1, :],
                stat_in[slot, 1:2, :],
            )
        return state

    computed = (long_mix_ref, long_stat_ref)
    merged = (mix_out, stat_out)
    for at in range(1, Z):
        @pl.when(z == at)
        def _():
            for copy in state_copies(at - 1, x * Z, computed):
                copy.start()

    rows = stack(1)
    for piece in range(PIECES):
        project(rows, 1, piece)
        pair_copy(1, piece).start()
        if piece:
            first_hop(piece - 1)
    first_hop(PIECES - 1)

    rows = stack(0)
    for piece in range(PIECES):
        project(rows, 0, piece)

    for piece in range(PIECES):
        pass_on(1, 1, piece, chip_sum(1, 2, piece) + arrived(1, 0, piece))

    @pl.when(z == 0)
    def _():
        stat_out[...] = jnp.zeros_like(stat_out)
        keep_state(*collect(range(Z - 1), computed))

    for at in range(1, n_x):
        @pl.when((z == 0) & (x == at))
        def _():
            for copy in state_copies(Z - 2 + at, jnp.int32(0), merged):
                copy.start()

    for piece in range(PIECES):
        pass_on(1, 2, piece, chip_sum(1, 1, piece) + arrived(1, 1, piece))

    @pl.when(seq == 0)
    def _():
        near = (near_mix_ref[...], near_stat_ref[0:1, :], near_stat_ref[1:2, :])
        mixed, _, total = merge(*near, *collect(range(Z - 1, Z + n_x - 2), merged))
        mixed = jnp.transpose(mixed / total).astype(jnp.bfloat16)
        parts = [mixed[at * LEAD : (at + 1) * LEAD] for at in range(heads)]
        lead_rows = jnp.concatenate(parts, axis=1)
        for piece in range(PIECES):
            product = dot32(lead_rows, w_ref[:, columns(piece)]).astype(jnp.bfloat16)

            @pl.when(core == 0)
            def _():
                at = pl.multiple_of(lax.rem(Y - y, Y) * half, half)
                own[0, pl.ds(at, half), columns(piece)] = product

            @pl.when(core == 1)
            def _():
                at = pl.multiple_of(lax.rem(Y - y, Y) * half, half)
                pair_out[0, pl.ds(at, half), columns(piece)] = product

    for piece in range(PIECES):
        pair_copy(0, piece).start()
    for piece in range(PIECES):
        pair_copy(0, piece).wait_recv()
        pass_on(0, 0, piece, chip_sum(0, 2, piece))
        pass_on(0, 2, piece, chip_sum(0, 3, piece))
    for piece in range(PIECES):
        value = chip_sum(1, 0, piece) + arrived(1, 2, piece)
        out_ref[pl.ds(half, half), columns(piece)] = value.astype(jnp.bfloat16)
    for piece in range(PIECES):
        pass_on(0, 1, piece, chip_sum(0, 1, piece) + arrived(0, 0, piece))
    for piece in range(PIECES):
        value = chip_sum(0, 0, piece) + arrived(0, 2, piece) + arrived(0, 1, piece)
        out_ref[pl.ds(0, half), columns(piece)] = value.astype(jnp.bfloat16)

    for later in range(2):
        for piece in range(PIECES):
            pair_copy(later, piece).wait_send()
            for step in range(3):
                ring_copy(later, step, piece).wait_send()

    @pl.when(seq > 0)
    def _():
        for copy in state_copies(0, jnp.int32(0), merged):
            copy.wait_send()


def project_scatter(attended, w_out, long_mix, long_stat, near_mix, near_stat):
    rows, inner = attended.shape
    width = w_out.shape[1]
    half = LEAD
    slots = Z - 1 + 3
    queries = long_mix.shape[1]
    vmem = pl.BlockSpec(memory_space=pltpu.VMEM)
    dma = pltpu.SemaphoreType.DMA
    return pl.pallas_call(
        scatter_kernel,
        in_specs=[vmem] * 6,
        out_specs=vmem,
        out_shape=jax.ShapeDtypeStruct((2 * half, width), jnp.bfloat16),
        scratch_shapes=[
            pltpu.VMEM((2, Y * half, width), jnp.bfloat16),
            pltpu.VMEM((2, Y * half, width), jnp.bfloat16),
            pltpu.VMEM((2, Y * half, width), jnp.bfloat16),
            pltpu.VMEM((2, 3, half, width), jnp.bfloat16),
            pltpu.VMEM((2, 3, half, width), jnp.bfloat16),
            pltpu.VMEM((HD, queries), jnp.bfloat16),
            pltpu.VMEM((8, queries), jnp.float32),
            pltpu.VMEM((slots, HD, queries), jnp.bfloat16),
            pltpu.VMEM((slots, 8, queries), jnp.float32),
            dma((2, PIECES)),
            dma((2, PIECES)),
            dma((2, 3, PIECES)),
            dma((2, 3, PIECES)),
            dma((2,)),
            dma((2, slots)),
        ],
        compiler_params=pltpu.CompilerParams(
            collective_id=1, has_side_effects=True, vmem_limit_bytes=LIMIT
        ),
        name="project_scatter",
    )(attended, w_out, long_mix, long_stat, near_mix, near_stat)


def on_device(
    tokens,
    norm_gain,
    w_query,
    w_key,
    w_value,
    w_out,
    long_cache,
    short_cache,
    slot_owner,
    new_len,
    cache_len,
):
    seq_index = lax.axis_index("seq")
    long_len = long_cache.shape[1] * lax.axis_size("seq")
    rows = tokens.shape[0] * lax.axis_size("head")
    starts = request_starts(new_len)
    token_index = seq_index * rows + jnp.arange(rows, dtype=jnp.int32)
    request, begin, position = token_facts(token_index, starts, cache_len, long_len)
    table = rotate_table(position)
    queries, here, before, earlier_slots, earlier_owner, lead_queries = gather_project(
        tokens.reshape(2, LEAD, tokens.shape[1]),
        norm_gain[None, :],
        w_query,
        w_key,
        w_value,
        table,
        short_cache,
        slot_owner[None, :],
    )
    shift = (seq_index - 1) * rows
    window_begin = jnp.where(request == starts.shape[0], rows, jnp.maximum(begin - shift, 0))
    attended, near_mix, near_stat, long_mix, long_stat = local_attention(
        window_begin,
        queries,
        before,
        here,
        earlier_slots,
        short_cache,
        earlier_owner,
        slot_owner[None, :],
        request,
        lead_queries,
        long_cache,
    )
    return project_scatter(attended, w_out, long_mix, long_stat, near_mix, near_stat)


def solution(mesh):
    placed = (
        P(("seq", "head"), None),
        P(),
        P(None, "head"),
        P(None, "head"),
        P(None, "head"),
        P("head", None),
        P(None, "seq", "head"),
        P(None, "seq", "head"),
        P("seq"),
        P(),
        P(),
    )
    return jax.shard_map(
        on_device, mesh=mesh, in_specs=placed, out_specs=P(("seq", "head"), None), check_vma=False
    )
```

```python
import math

import jax
import jax.numpy as jnp
from jax import lax
from jax.experimental import pallas as pl
from jax.experimental.pallas import tpu as pltpu
from jax.sharding import PartitionSpec as P

HD = 128
LEAD = 64
THETA_LOG = math.log(500000.0)
SCALE = 1.0 / math.sqrt(HD)
LOW = -1e30


def normalize(tokens, norm_gain):
    values = tokens.astype(jnp.float32)
    mean_square = jnp.mean(values * values, axis=-1, keepdims=True)
    return (values * lax.rsqrt(mean_square + 1e-05) * norm_gain).astype(jnp.bfloat16)


def dot32(a, b):
    return jnp.dot(a, b, preferred_element_type=jnp.float32)


def dot_t(a, b):
    return lax.dot_general(a, b, (((1,), (1,)), ((), ())), preferred_element_type=jnp.float32)


MESH = pl.DeviceIdType.MESH
LIMIT = 60 * 1024 * 1024
Z = 8
Y = 4
LONG_ROWS = 1024
UNITS = [(0, 0), (0, 1), (1, 0), (3, 0), (1, 1), (2, 0), (2, 1), (3, 1)]
SLOT = {unit: number for number, unit in enumerate(UNITS)}


def place():
    seq = lax.axis_index("seq")
    head = lax.axis_index("head")
    return seq, head, head // 2, lax.rem(head, 2)


def pick(number, table):
    value = jnp.int32(table[0])
    for at, entry in enumerate(table):
        value = jnp.where(number == at, jnp.int32(entry), value)
    return value


def greet(device):
    pl.semaphore_signal(
        pltpu.get_barrier_semaphore(), inc=1, device_id=device, device_id_type=MESH
    )


def token_facts(seq, new_len_ref, cache_len_ref, request_ref, begin_ref, place_ref):
    number = new_len_ref.shape[0]
    shape = request_ref.shape
    rows = shape[0] * shape[1]
    token = (
        seq * rows
        + lax.broadcasted_iota(jnp.int32, shape, 0) * shape[1]
        + lax.broadcasted_iota(jnp.int32, shape, 1)
    )

    def step(at, carry):
        start, request, begin, cached = carry
        passed = token >= start
        return (
            start + new_len_ref[at],
            jnp.where(passed, at, request),
            jnp.where(passed, start, begin),
            jnp.where(passed, cache_len_ref[at], cached),
        )

    zero = jnp.zeros(shape, jnp.int32)
    _, request, begin, cached = lax.fori_loop(
        0, number, step, (jnp.int32(LEAD), zero + number, zero, zero)
    )
    lead = request == number
    long_len = lax.axis_size("seq") * LONG_ROWS
    position = jnp.where(lead, token + long_len, token - begin + cached)
    place_ref[...] = position.astype(jnp.float32)
    request_ref[...] = request
    begin_ref[...] = jnp.where(lead, rows, jnp.maximum(begin - (seq - 1) * rows, 0))


def gather_kernel(
    tokens_ref,
    gain_ref,
    wq_hbm,
    wk_hbm,
    wv_hbm,
    new_len_ref,
    cache_len_ref,
    slots_ref,
    owner_ref,
    q_ref,
    kv_ref,
    before_ref,
    slots_before_ref,
    owner_before_ref,
    lead_ref,
    request_ref,
    begin_ref,
    normed_ref,
    wq_ref,
    wkv_ref,
    table_ref,
    place_ref,
    held,
    ring_send,
    ring_recv,
    pair_send,
    pair_recv,
    kv_send,
    kv_recv,
    slot_send,
    slot_recv,
    lead_send,
    lead_recv,
    weight_sem,
):
    seq, head, y, core = place()
    weights = [
        pltpu.make_async_copy(wk_hbm, wkv_ref.at[:, pl.ds(0, HD)], weight_sem.at[0]),
        pltpu.make_async_copy(wv_hbm, wkv_ref.at[:, pl.ds(HD, HD)], weight_sem.at[1]),
        pltpu.make_async_copy(wq_hbm, wq_ref, weight_sem.at[2]),
    ]
    for copy in weights:
        copy.start()
    n_seq = lax.axis_size("seq")
    x, z = seq // Z, lax.rem(seq, Z)
    way = 1 - 2 * core
    right = (seq, lax.rem(y + way + Y, Y) * 2 + core)
    left = (seq, lax.rem(y - way + Y, Y) * 2 + core)
    pair = (seq, head + way)
    following = (lax.rem(seq + 1, n_seq), head)
    previous = (lax.rem(seq + n_seq - 1, n_seq), head)
    heads = q_ref.shape[0]
    half = held.shape[2]

    for device in (right, left, pair, following, previous):
        greet(device)

    @pl.when(seq == 0)
    def _():
        for to in range(1, Z):
            greet((to, head))

    @pl.when(x == 0)
    def _():
        for to in range(1, n_seq // Z):
            greet((to * Z + z, head))

    @pl.when((x == 0) & (z > 0))
    def _():
        greet((0, head))

    @pl.when(x > 0)
    def _():
        greet((z, head))

    for later in range(2):
        normed_ref[later] = normalize(tokens_ref[later], gain_ref[...])
        held[SLOT[(0, later)], core] = normed_ref[later]

    barrier = pltpu.get_barrier_semaphore()
    others = n_seq // Z - 1

    @pl.when(seq == 0)
    def _():
        pl.semaphore_wait(barrier, 5 + Z - 1 + others)

    @pl.when((x == 0) & (z > 0))
    def _():
        pl.semaphore_wait(barrier, 5 + 1 + others)

    @pl.when(x > 0)
    def _():
        pl.semaphore_wait(barrier, 5 + 1)

    def ring(number, source, to, unit):
        slot = SLOT[unit]
        return pltpu.make_async_remote_copy(
            src_ref=source,
            dst_ref=held.at[slot, core],
            send_sem=ring_send.at[number],
            recv_sem=ring_recv.at[slot],
            device_id=to,
            device_id_type=MESH,
        )

    def mine(unit):
        return held.at[SLOT[unit], core]

    def to_pair(unit):
        slot = SLOT[unit]
        return pltpu.make_async_remote_copy(
            src_ref=normed_ref.at[unit[1]] if unit[0] == 0 else mine(unit),
            dst_ref=held.at[slot, core],
            send_sem=pair_send.at[slot],
            recv_sem=pair_recv.at[slot],
            device_id=pair,
            device_id_type=MESH,
        )

    rings = [
        ring(0, normed_ref.at[0], right, (1, 0)),
        ring(1, normed_ref.at[0], left, (3, 0)),
        ring(2, normed_ref.at[1], right, (1, 1)),
        ring(3, mine((1, 0)), right, (2, 0)),
        ring(4, mine((1, 1)), right, (2, 1)),
        ring(5, mine((2, 1)), right, (3, 1)),
    ]
    pairs = {unit: to_pair(unit) for unit in UNITS}
    side = [
        pltpu.make_async_remote_copy(
            src_ref=source,
            dst_ref=target,
            send_sem=slot_send.at[number],
            recv_sem=slot_recv.at[number],
            device_id=following,
            device_id_type=MESH,
        )
        for number, (source, target) in enumerate(
            [(slots_ref, slots_before_ref), (owner_ref, owner_before_ref)]
        )
    ]

    def lead_copy(number, to):
        return pltpu.make_async_remote_copy(
            src_ref=lead_ref,
            dst_ref=lead_ref,
            send_sem=lead_send.at[number],
            recv_sem=lead_recv,
            device_id=(to, head),
            device_id_type=MESH,
        )

    along_z = [lead_copy(to - 1, jnp.int32(to)) for to in range(1, Z)]
    along_x = [lead_copy(Z - 2 + to, to * Z + z) for to in range(1, n_seq // Z)]

    def row_starts(number):
        distance = pick(number, [unit[0] for unit in UNITS])
        later = pick(number, [unit[1] for unit in UNITS])
        first = lax.rem(y - distance + Y, Y) * (4 * half) + later * half
        second = lax.rem(y + distance, Y) * (4 * half) + 2 * half + later * half
        return pl.multiple_of(first, half), pl.multiple_of(second, half)

    def kv_copies(number):
        return [
            pltpu.make_async_remote_copy(
                src_ref=kv_ref.at[:, pl.ds(start, half), :],
                dst_ref=before_ref.at[:, pl.ds(start, half), :],
                send_sem=kv_send.at[2 * number + part],
                recv_sem=kv_recv.at[2 * number + part],
                device_id=following,
                device_id_type=MESH,
            )
            for part, start in enumerate(row_starts(number))
        ]

    rings[0].start()
    pairs[(0, 0)].start()
    rings[1].start()
    rings[2].start()
    pairs[(0, 1)].start()
    for copy in side:
        copy.start()

    token_facts(seq, new_len_ref, cache_len_ref, request_ref, begin_ref, place_ref)
    half_head = HD // 2
    lane = lax.broadcasted_iota(jnp.int32, (HD, HD), 1)
    entry = jnp.where(lane < half_head, lane, lane - half_head)
    frequency = jnp.exp(entry.astype(jnp.float32) * (-2.0 * THETA_LOG / HD))

    @pl.loop(0, place_ref.shape[0])
    def _(number):
        spread = jnp.broadcast_to(place_ref[pl.ds(number, 1), :], (HD, HD))
        angle = jnp.transpose(spread) * frequency
        at = pl.multiple_of(number * HD, HD)
        table_ref[pl.ds(at, HD), :] = jnp.where(lane < half_head, jnp.cos(angle), jnp.sin(angle))

    for copy in weights:
        copy.wait()
    def event_0():
        pairs[(0, 0)].wait_recv()

    def event_1():
        pairs[(0, 1)].wait_recv()

    def event_2():
        rings[0].wait_recv()
        rings[3].start()
        pairs[(1, 0)].start()
        pairs[(1, 0)].wait_recv()

    def event_3():
        rings[1].wait_recv()
        pairs[(3, 0)].start()
        rings[2].wait_recv()
        rings[4].start()
        pairs[(1, 1)].start()
        pairs[(3, 0)].wait_recv()

    def event_4():
        pairs[(1, 1)].wait_recv()

    def event_5():
        rings[3].wait_recv()
        pairs[(2, 0)].start()
        pairs[(2, 0)].wait_recv()

    def event_6():
        @pl.when(seq == 0)
        def _():
            lead_ref[...] = q_ref[:, pl.ds(0, LEAD), :]
            for copy in along_z:
                copy.start()
            for copy in along_x:
                copy.start()

        rings[4].wait_recv()
        rings[5].start()
        pairs[(2, 1)].start()
        pairs[(2, 1)].wait_recv()

    def event_7():
        rings[5].wait_recv()
        pairs[(3, 1)].start()

        @pl.when((x == 0) & (z > 0))
        def _():
            along_z[0].wait_recv()
            for copy in along_x:
                copy.start()

        pairs[(3, 1)].wait_recv()

    events = [event_0, event_1, event_2, event_3, event_4, event_5, event_6, event_7]

    @pl.loop(0, len(UNITS))
    def _(number):
        for at, event in enumerate(events):
            pl.when(number == at)(event)
        block = held[number].reshape(2 * half, held.shape[3])
        starts = row_starts(number)
        table = jnp.concatenate([table_ref[pl.ds(start, half), :] for start in starts], axis=0)
        swapped = pltpu.roll(table, HD // 2, 1)
        low = lax.broadcasted_iota(jnp.int32, table.shape, 1) < HD // 2
        cosine = jnp.where(low, table, swapped)
        sine = jnp.where(low, -swapped, table)

        def turned(product):
            return (product * cosine + pltpu.roll(product, HD // 2, 1) * sine).astype(jnp.bfloat16)

        def put(ref, at, rows):
            for part, start in enumerate(starts):
                ref[at, pl.ds(start, half), :] = rows[part * half : (part + 1) * half]

        both = dot32(block, wkv_ref[...])
        put(kv_ref, 0, turned(both[:, :HD]))
        put(kv_ref, 1, both[:, HD:].astype(jnp.bfloat16))
        product = dot32(block, wq_ref[...])
        for at in range(heads):
            put(q_ref, at, turned(product[:, at * HD : (at + 1) * HD]))
        for copy in kv_copies(number):
            copy.start()

    @pl.loop(0, len(UNITS))
    def _(number):
        for copy in kv_copies(number):
            copy.wait_recv()
            copy.wait_send()

    for copy in rings:
        copy.wait_send()
    for unit in UNITS:
        pairs[unit].wait_send()
    for copy in side:
        copy.wait_recv()
        copy.wait_send()

    @pl.when(seq == 0)
    def _():
        for copy in along_z:
            copy.wait_send()

    @pl.when(x == 0)
    def _():
        for copy in along_x:
            copy.wait_send()

    @pl.when(x > 0)
    def _():
        along_x[0].wait_recv()


def gather_project(tokens, gain, w_query, w_key, w_value, new_len, cache_len, slots, owner):
    half, width = tokens.shape[1:]
    rows = 2 * half * lax.axis_size("head")
    heads = w_query.shape[1] // HD
    vmem = pl.BlockSpec(memory_space=pltpu.VMEM)
    smem = pl.BlockSpec(memory_space=pltpu.SMEM)
    hbm = pl.BlockSpec(memory_space=pl.ANY)
    dma = pltpu.SemaphoreType.DMA
    shape = jax.ShapeDtypeStruct
    facts = (rows // HD, HD)
    return pl.pallas_call(
        gather_kernel,
        in_specs=[vmem, vmem, hbm, hbm, hbm, smem, smem, vmem, vmem],
        out_specs=[vmem] * 8,
        out_shape=[
            shape((heads, rows, HD), jnp.bfloat16),
            shape((2, rows, HD), jnp.bfloat16),
            shape((2, rows, HD), jnp.bfloat16),
            shape(slots.shape, jnp.bfloat16),
            shape(owner.shape, jnp.int32),
            shape((heads, LEAD, HD), jnp.bfloat16),
            shape(facts, jnp.int32),
            shape(facts, jnp.int32),
        ],
        scratch_shapes=[
            pltpu.VMEM((2, half, width), jnp.bfloat16),
            pltpu.VMEM(w_query.shape, jnp.bfloat16),
            pltpu.VMEM((width, 2 * HD), jnp.bfloat16),
            pltpu.VMEM((rows, HD), jnp.float32),
            pltpu.VMEM(facts, jnp.float32),
            pltpu.VMEM((len(UNITS), 2, half, width), jnp.bfloat16),
            dma((6,)),
            dma((len(UNITS),)),
            dma((len(UNITS),)),
            dma((len(UNITS),)),
            dma((2 * len(UNITS),)),
            dma((2 * len(UNITS),)),
            dma((2,)),
            dma((2,)),
            dma((Z + 2,)),
            dma,
            dma((3,)),
        ],
        compiler_params=pltpu.CompilerParams(
            collective_id=0, has_side_effects=True, vmem_limit_bytes=LIMIT
        ),
        name="gather_project",
    )(tokens, gain, w_query, w_key, w_value, new_len, cache_len, slots, owner)


def local_kernel(
    begin_smem,
    q_ref,
    before_ref,
    here_ref,
    slot_before_ref,
    slot_here_ref,
    owner_before_ref,
    owner_here_ref,
    request_ref,
    begin_ref,
    lead_ref,
    cache_ref,
    out_ref,
    near_mix_ref,
    near_stat_ref,
    long_mix_ref,
    long_stat_ref,
    window,
    owners,
    top_ref,
    sum_ref,
    mix_ref,
):
    step = pl.program_id(0)
    rows = here_ref.shape[1]
    heads, tile, _ = q_ref.shape
    chunk = 2 * tile

    @pl.when(step == 0)
    def _():
        window[:, pl.ds(0, tile)] = jnp.zeros((2, tile, HD), jnp.bfloat16)
        window[:, pl.ds(tile, rows)] = before_ref[...]
        window[:, pl.ds(tile + rows, rows)] = here_ref[...]
        for at, ref in enumerate((owner_before_ref, owner_here_ref)):
            spread = jnp.broadcast_to(ref[...].astype(jnp.float32), (tile, ref.shape[1]))
            owners[at] = jnp.transpose(spread).astype(jnp.int32)
        long_state(lead_ref, cache_ref, long_mix_ref, long_stat_ref)

    request = request_ref[pl.ds(step, 1), :]
    begin = begin_ref[pl.ds(step, 1), :]
    down = lax.broadcasted_iota(jnp.int32, (chunk, tile), 0)
    index = rows + step * tile + lax.broadcasted_iota(jnp.int32, (1, tile), 1)
    queries = q_ref[...].reshape(heads * tile, HD)

    def take(keys, values, valid, fresh):
        scores = dot_t(keys, queries) * SCALE
        scores = jnp.where(jnp.concatenate([valid] * heads, axis=1), scores, LOW)
        top = jnp.max(scores, axis=0, keepdims=True)
        if not fresh:
            old = top_ref[...]
            top = jnp.maximum(top, old)
            keep = jnp.exp(old - top)
        weights = jnp.exp(scores - top)
        total = jnp.sum(weights, axis=0, keepdims=True)
        mixed = lax.dot_general(
            values,
            weights.astype(jnp.bfloat16),
            (((0,), (0,)), ((), ())),
            preferred_element_type=jnp.float32,
        )
        top_ref[...] = top
        if fresh:
            sum_ref[...] = total
            mix_ref[...] = mixed
        else:
            sum_ref[...] = sum_ref[...] * keep + total
            mix_ref[...] = mix_ref[...] * keep + mixed

    end = rows + (step + 1) * tile

    def new_chunk(number):
        key = end - (number + 1) * chunk
        key_at = key + down
        valid = (key_at >= begin) & (key_at <= index)
        at = pl.multiple_of(key + tile, tile)
        return window[0, pl.ds(at, chunk), :], window[1, pl.ds(at, chunk), :], valid

    def join(*parts):
        return [jnp.concatenate(pair, axis=0) for pair in zip(*parts)]

    first = begin_smem[step, 0]
    take(*join(new_chunk(0), (slot_here_ref[0], slot_here_ref[1], owners[1] == request)), True)

    @pl.loop(1, (end - first + chunk - 1) // chunk)
    def _(number):
        take(*new_chunk(number), False)

    @pl.when(first < rows)
    def _():
        take(slot_before_ref[0], slot_before_ref[1], owners[0] == request, False)

    mixed = mix_ref[...] / sum_ref[...]
    for head in range(heads):
        span = slice(head * tile, (head + 1) * tile)
        out_ref[:, span] = jnp.transpose(mixed[:, span]).astype(jnp.bfloat16)

    @pl.when(step == 0)
    def _():
        def leads(ref):
            parts = [ref[:, head * tile : head * tile + LEAD] for head in range(heads)]
            return jnp.concatenate(parts + parts[-1:], axis=1)

        near_mix_ref[...] = leads(mix_ref)
        near_stat_ref[...] = jnp.zeros_like(near_stat_ref)
        near_stat_ref[0:1, :] = leads(top_ref)
        near_stat_ref[1:2, :] = leads(sum_ref)


def long_state(q_ref, cache_ref, mix_ref, stat_ref):
    heads = q_ref.shape[0]
    queries = jnp.concatenate([q_ref[at] for at in range(heads)] + [q_ref[heads - 1]], axis=0)
    scores = dot_t(cache_ref[0], queries) * SCALE
    top = jnp.max(scores, axis=0, keepdims=True)
    weights = jnp.exp(scores - top)
    mixed = lax.dot_general(
        cache_ref[1],
        weights.astype(jnp.bfloat16),
        (((0,), (0,)), ((), ())),
        preferred_element_type=jnp.float32,
    )
    mix_ref[...] = mixed.astype(jnp.bfloat16)
    stat_ref[...] = jnp.zeros_like(stat_ref)
    stat_ref[0:1, :] = top
    stat_ref[1:2, :] = jnp.sum(weights, axis=0, keepdims=True)


def local_attention(
    begin, queries, before, here, slot_before, slot_here, owner_before, owner_here, request, lead, cache
):
    heads, rows, _ = queries.shape
    tile = HD
    columns = (heads + 1) * LEAD

    def whole(array):
        return pl.BlockSpec(array.shape, lambda i, first: (0,) * len(array.shape))

    shape = jax.ShapeDtypeStruct
    near_mix = shape((HD, columns), jnp.float32)
    long_mix = shape((HD, columns), jnp.bfloat16)
    long_stat = shape((8, columns), jnp.float32)
    kept = [before, here, slot_before, slot_here, owner_before, owner_here, request, begin, lead, cache]
    return pl.pallas_call(
        local_kernel,
        grid_spec=pltpu.PrefetchScalarGridSpec(
            num_scalar_prefetch=1,
            grid=(rows // tile,),
            in_specs=[pl.BlockSpec((heads, tile, HD), lambda i, first: (0, i, 0))]
            + [whole(array) for array in kept],
            out_specs=[pl.BlockSpec((tile, heads * HD), lambda i, first: (i, 0))]
            + [whole(array) for array in (near_mix, long_stat, long_mix, long_stat)],
            scratch_shapes=[
                pltpu.VMEM((2, tile + 2 * rows, HD), jnp.bfloat16),
                pltpu.VMEM((2, slot_here.shape[1], tile), jnp.int32),
                pltpu.VMEM((1, heads * tile), jnp.float32),
                pltpu.VMEM((1, heads * tile), jnp.float32),
                pltpu.VMEM((HD, heads * tile), jnp.float32),
            ],
        ),
        out_shape=[shape((rows, heads * HD), jnp.bfloat16), near_mix, long_stat, long_mix, long_stat],
        name="local_attention",
    )(begin, queries, *kept)


def merge(into, top, total, part, part_top, part_total):
    highest = jnp.maximum(top, part_top)
    keep, add = jnp.exp(top - highest), jnp.exp(part_top - highest)
    return into * keep + part * add, highest, total * keep + part_total * add


PIECES = 4


def scatter_kernel(
    attended_ref,
    w_ref,
    long_mix_ref,
    long_stat_ref,
    near_mix_ref,
    near_stat_ref,
    out_ref,
    pair_out,
    pair_in,
    own,
    ring_out,
    ring_in,
    mix_out,
    stat_out,
    mix_in,
    stat_in,
    pair_send,
    pair_recv,
    ring_send,
    ring_recv,
    sends,
    recvs,
):
    seq, head, y, core = place()
    n_x = lax.axis_size("seq") // Z
    x, z = seq // Z, lax.rem(seq, Z)
    way = 1 - 2 * core
    right = (seq, lax.rem(y + way + Y, Y) * 2 + core)
    left = (seq, lax.rem(y - way + Y, Y) * 2 + core)
    pair = (seq, head + way)
    half = ring_out.shape[2]
    heads = w_ref.shape[0] // HD
    width = w_ref.shape[1] // PIECES
    barrier = pltpu.get_barrier_semaphore()

    for device in (right, left, pair):
        greet(device)

    @pl.when(z > 0)
    def _():
        greet((x * Z, head))
        pl.semaphore_wait(barrier, 3 + 1)

    @pl.when((z == 0) & (x > 0))
    def _():
        for at in range(1, Z):
            greet((x * Z + at, head))
        greet((0, head))
        pl.semaphore_wait(barrier, 3 + Z)

    @pl.when(seq == 0)
    def _():
        for at in range(1, Z):
            greet((at, head))
        for at in range(1, n_x):
            greet((at * Z, head))
        pl.semaphore_wait(barrier, 3 + Z - 1 + n_x - 1)

    def columns(piece):
        return pl.ds(piece * width, width)

    def rows_of(chip, of_core, later):
        return attended_ref[pl.ds(pl.multiple_of(chip * (4 * half) + of_core * (2 * half) + later * half, half), half), :]

    def stack(later):
        parts = [rows_of(lax.rem(y - k * way + 2 * Y * 2, Y), 1 - core, later) for k in range(Y)]
        parts += [rows_of(lax.rem(y + k * way + 2 * Y * 2, Y), core, later) for k in range(Y)]
        return jnp.concatenate(parts, axis=0)

    def pair_copy(later, piece):
        return pltpu.make_async_remote_copy(
            src_ref=pair_out.at[later, :, columns(piece)],
            dst_ref=pair_in.at[later, :, columns(piece)],
            send_sem=pair_send.at[later, piece],
            recv_sem=pair_recv.at[later, piece],
            device_id=pair,
            device_id_type=MESH,
        )

    def ring_copy(later, step, piece):
        return pltpu.make_async_remote_copy(
            src_ref=ring_out.at[later, step, :, columns(piece)],
            dst_ref=ring_in.at[later, step, :, columns(piece)],
            send_sem=ring_send.at[later, step, piece],
            recv_sem=ring_recv.at[later, step, piece],
            device_id=left if (later, step) == (0, 2) else right,
            device_id_type=MESH,
        )

    def project(rows, later, piece):
        product = dot32(rows, w_ref[:, columns(piece)]).astype(jnp.bfloat16)
        pair_out[later, :, columns(piece)] = product[: Y * half]
        own[later, :, columns(piece)] = product[Y * half :]

    def chip_sum(later, k, piece):
        rows = pl.ds(k * half, half)
        return own[later, rows, columns(piece)].astype(jnp.float32) + pair_in[
            later, rows, columns(piece)
        ].astype(jnp.float32)

    def arrived(later, step, piece):
        ring_copy(later, step, piece).wait_recv()
        return ring_in[later, step, :, columns(piece)].astype(jnp.float32)

    def pass_on(later, step, piece, value):
        ring_out[later, step, :, columns(piece)] = value.astype(jnp.bfloat16)
        ring_copy(later, step, piece).start()

    def first_hop(piece):
        pair_copy(1, piece).wait_recv()
        pass_on(1, 0, piece, chip_sum(1, 3, piece))

    def keep_state(mixed, top, total):
        mix_out[...] = mixed.astype(jnp.bfloat16)
        stat_out[0:1, :] = top
        stat_out[1:2, :] = total

    def state_copies(slot, to, sources):
        return [
            pltpu.make_async_remote_copy(
                src_ref=source,
                dst_ref=target.at[slot],
                send_sem=sends.at[number],
                recv_sem=recvs.at[number, slot],
                device_id=(to, head),
                device_id_type=MESH,
            )
            for number, (source, target) in enumerate(zip(sources, (mix_in, stat_in)))
        ]

    def collect(slots, sources):
        mix, stat = sources
        state = (mix[...].astype(jnp.float32), stat[0:1, :], stat[1:2, :])
        for slot in slots:
            for copy in state_copies(slot, jnp.int32(0), sources):
                copy.wait_recv()
            state = merge(
                *state,
                mix_in[slot].astype(jnp.float32),
                stat_in[slot, 0:1, :],
                stat_in[slot, 1:2, :],
            )
        return state

    computed = (long_mix_ref, long_stat_ref)
    merged = (mix_out, stat_out)
    for at in range(1, Z):
        @pl.when(z == at)
        def _():
            for copy in state_copies(at - 1, x * Z, computed):
                copy.start()

    rows = stack(1)
    for piece in range(PIECES):
        project(rows, 1, piece)
        pair_copy(1, piece).start()
        if piece:
            first_hop(piece - 1)
    first_hop(PIECES - 1)

    rows = stack(0)
    for piece in range(PIECES):
        project(rows, 0, piece)

    for piece in range(PIECES):
        pass_on(1, 1, piece, chip_sum(1, 2, piece) + arrived(1, 0, piece))

    @pl.when(z == 0)
    def _():
        stat_out[...] = jnp.zeros_like(stat_out)
        keep_state(*collect(range(Z - 1), computed))

    for at in range(1, n_x):
        @pl.when((z == 0) & (x == at))
        def _():
            for copy in state_copies(Z - 2 + at, jnp.int32(0), merged):
                copy.start()

    for piece in range(PIECES):
        pass_on(1, 2, piece, chip_sum(1, 1, piece) + arrived(1, 1, piece))

    @pl.when(seq == 0)
    def _():
        near = (near_mix_ref[...], near_stat_ref[0:1, :], near_stat_ref[1:2, :])
        mixed, _, total = merge(*near, *collect(range(Z - 1, Z + n_x - 2), merged))
        mixed = jnp.transpose(mixed / total).astype(jnp.bfloat16)
        parts = [mixed[at * LEAD : (at + 1) * LEAD] for at in range(heads)]
        lead_rows = jnp.concatenate(parts, axis=1)
        for piece in range(PIECES):
            product = dot32(lead_rows, w_ref[:, columns(piece)]).astype(jnp.bfloat16)

            @pl.when(core == 0)
            def _():
                at = pl.multiple_of(lax.rem(Y - y, Y) * half, half)
                own[0, pl.ds(at, half), columns(piece)] = product

            @pl.when(core == 1)
            def _():
                at = pl.multiple_of(lax.rem(Y - y, Y) * half, half)
                pair_out[0, pl.ds(at, half), columns(piece)] = product

    for piece in range(PIECES):
        pair_copy(0, piece).start()
    for piece in range(PIECES):
        pair_copy(0, piece).wait_recv()
        pass_on(0, 0, piece, chip_sum(0, 2, piece))
        pass_on(0, 2, piece, chip_sum(0, 3, piece))
    for piece in range(PIECES):
        value = chip_sum(1, 0, piece) + arrived(1, 2, piece)
        out_ref[pl.ds(half, half), columns(piece)] = value.astype(jnp.bfloat16)
    for piece in range(PIECES):
        pass_on(0, 1, piece, chip_sum(0, 1, piece) + arrived(0, 0, piece))
    for piece in range(PIECES):
        value = chip_sum(0, 0, piece) + arrived(0, 2, piece) + arrived(0, 1, piece)
        out_ref[pl.ds(0, half), columns(piece)] = value.astype(jnp.bfloat16)

    for later in range(2):
        for piece in range(PIECES):
            pair_copy(later, piece).wait_send()
            for step in range(3):
                ring_copy(later, step, piece).wait_send()

    @pl.when(seq > 0)
    def _():
        for copy in state_copies(0, jnp.int32(0), merged):
            copy.wait_send()


def project_scatter(attended, w_out, long_mix, long_stat, near_mix, near_stat):
    rows, inner = attended.shape
    width = w_out.shape[1]
    half = LEAD
    slots = Z - 1 + 3
    queries = long_mix.shape[1]
    vmem = pl.BlockSpec(memory_space=pltpu.VMEM)
    dma = pltpu.SemaphoreType.DMA
    return pl.pallas_call(
        scatter_kernel,
        in_specs=[vmem] * 6,
        out_specs=vmem,
        out_shape=jax.ShapeDtypeStruct((2 * half, width), jnp.bfloat16),
        scratch_shapes=[
            pltpu.VMEM((2, Y * half, width), jnp.bfloat16),
            pltpu.VMEM((2, Y * half, width), jnp.bfloat16),
            pltpu.VMEM((2, Y * half, width), jnp.bfloat16),
            pltpu.VMEM((2, 3, half, width), jnp.bfloat16),
            pltpu.VMEM((2, 3, half, width), jnp.bfloat16),
            pltpu.VMEM((HD, queries), jnp.bfloat16),
            pltpu.VMEM((8, queries), jnp.float32),
            pltpu.VMEM((slots, HD, queries), jnp.bfloat16),
            pltpu.VMEM((slots, 8, queries), jnp.float32),
            dma((2, PIECES)),
            dma((2, PIECES)),
            dma((2, 3, PIECES)),
            dma((2, 3, PIECES)),
            dma((2,)),
            dma((2, slots)),
        ],
        compiler_params=pltpu.CompilerParams(
            collective_id=1, has_side_effects=True, vmem_limit_bytes=LIMIT
        ),
        name="project_scatter",
    )(attended, w_out, long_mix, long_stat, near_mix, near_stat)


def on_device(
    tokens,
    norm_gain,
    w_query,
    w_key,
    w_value,
    w_out,
    long_cache,
    short_cache,
    slot_owner,
    new_len,
    cache_len,
):
    owner = slot_owner[None, :]
    queries, here, before, earlier_slots, earlier_owner, lead, request, begin = gather_project(
        tokens.reshape(2, LEAD, tokens.shape[1]),
        norm_gain[None, :],
        w_query,
        w_key,
        w_value,
        new_len,
        cache_len,
        short_cache,
        owner,
    )
    attended, near_mix, near_stat, long_mix, long_stat = local_attention(
        begin,
        queries,
        before,
        here,
        earlier_slots,
        short_cache,
        earlier_owner,
        owner,
        request,
        lead,
        long_cache,
    )
    return project_scatter(attended, w_out, long_mix, long_stat, near_mix, near_stat)


def solution(mesh):
    placed = (
        P(("seq", "head"), None),
        P(),
        P(None, "head"),
        P(None, "head"),
        P(None, "head"),
        P("head", None),
        P(None, "seq", "head"),
        P(None, "seq", "head"),
        P("seq"),
        P(),
        P(),
    )
    return jax.shard_map(
        on_device, mesh=mesh, in_specs=placed, out_specs=P(("seq", "head"), None), check_vma=False
    )
```

```python
import math

import jax
import jax.numpy as jnp
from jax import lax
from jax.experimental import pallas as pl
from jax.experimental.pallas import tpu as pltpu
from jax.sharding import PartitionSpec as P

HD = 128
LEAD = 64
THETA_LOG = math.log(500000.0)
SCALE = 1.0 / math.sqrt(HD)
LOW = -1e30


def normalize(tokens, norm_gain):
    values = tokens.astype(jnp.float32)
    mean_square = jnp.mean(values * values, axis=-1, keepdims=True)
    return (values * lax.rsqrt(mean_square + 1e-05) * norm_gain).astype(jnp.bfloat16)


def dot32(a, b):
    return jnp.dot(a, b, preferred_element_type=jnp.float32)


def dot_t(a, b):
    return lax.dot_general(a, b, (((1,), (1,)), ((), ())), preferred_element_type=jnp.float32)


MESH = pl.DeviceIdType.MESH
LIMIT = 60 * 1024 * 1024
Z = 8
Y = 4
LONG_ROWS = 1024
PARTS = 2
UNITS = [(0, 0), (0, 1), (1, 0), (3, 0), (1, 1), (2, 0), (2, 1), (3, 1)]
SLOT = {unit: number for number, unit in enumerate(UNITS)}


def place():
    seq = lax.axis_index("seq")
    head = lax.axis_index("head")
    return seq, head, head // 2, lax.rem(head, 2)


def pick(number, table):
    value = jnp.int32(table[0])
    for at, entry in enumerate(table):
        value = jnp.where(number == at, jnp.int32(entry), value)
    return value


def greet(device):
    pl.semaphore_signal(
        pltpu.get_barrier_semaphore(), inc=1, device_id=device, device_id_type=MESH
    )


def token_facts(seq, new_len_ref, cache_len_ref, request_ref, begin_ref, place_ref):
    number = new_len_ref.shape[0]
    shape = request_ref.shape
    rows = shape[0] * shape[1]
    token = (
        seq * rows
        + lax.broadcasted_iota(jnp.int32, shape, 0) * shape[1]
        + lax.broadcasted_iota(jnp.int32, shape, 1)
    )

    def step(at, carry):
        start, request, begin, cached = carry
        passed = token >= start
        return (
            start + new_len_ref[at],
            jnp.where(passed, at, request),
            jnp.where(passed, start, begin),
            jnp.where(passed, cache_len_ref[at], cached),
        )

    zero = jnp.zeros(shape, jnp.int32)
    _, request, begin, cached = lax.fori_loop(
        0, number, step, (jnp.int32(LEAD), zero + number, zero, zero)
    )
    lead = request == number
    long_len = lax.axis_size("seq") * LONG_ROWS
    position = jnp.where(lead, token + long_len, token - begin + cached)
    place_ref[...] = position.astype(jnp.float32)
    request_ref[...] = request
    begin_ref[...] = jnp.where(lead, rows, jnp.maximum(begin - (seq - 1) * rows, 0))


def gather_kernel(
    tokens_ref,
    gain_ref,
    wq_hbm,
    wk_hbm,
    wv_hbm,
    new_len_ref,
    cache_len_ref,
    slots_ref,
    owner_ref,
    q_ref,
    kv_ref,
    before_ref,
    slots_before_ref,
    owner_before_ref,
    lead_ref,
    request_ref,
    begin_ref,
    normed_ref,
    wq_ref,
    wkv_ref,
    table_ref,
    place_ref,
    held,
    ring_send,
    ring_recv,
    pair_send,
    pair_recv,
    kv_send,
    kv_recv,
    slot_send,
    slot_recv,
    lead_send,
    lead_recv,
    weight_sem,
):
    seq, head, y, core = place()
    weights = [
        pltpu.make_async_copy(wk_hbm, wkv_ref.at[:, pl.ds(0, HD)], weight_sem.at[0]),
        pltpu.make_async_copy(wv_hbm, wkv_ref.at[:, pl.ds(HD, HD)], weight_sem.at[1]),
        pltpu.make_async_copy(wq_hbm, wq_ref, weight_sem.at[2]),
    ]
    for copy in weights:
        copy.start()
    n_seq = lax.axis_size("seq")
    x, z = seq // Z, lax.rem(seq, Z)
    way = 1 - 2 * core
    right = (seq, lax.rem(y + way + Y, Y) * 2 + core)
    left = (seq, lax.rem(y - way + Y, Y) * 2 + core)
    pair = (seq, head + way)
    following = (lax.rem(seq + 1, n_seq), head)
    previous = (lax.rem(seq + n_seq - 1, n_seq), head)
    heads = q_ref.shape[0]
    half = held.shape[2]

    for device in (right, left, pair, following, previous):
        greet(device)

    @pl.when(seq == 0)
    def _():
        for to in range(1, Z):
            greet((to, head))

    @pl.when(x == 0)
    def _():
        for to in range(1, n_seq // Z):
            greet((to * Z + z, head))

    @pl.when((x == 0) & (z > 0))
    def _():
        greet((0, head))

    @pl.when(x > 0)
    def _():
        greet((z, head))

    for later in range(2):
        normed_ref[later] = normalize(tokens_ref[later], gain_ref[...])
        held[SLOT[(0, later)], core] = normed_ref[later]

    barrier = pltpu.get_barrier_semaphore()
    others = n_seq // Z - 1

    @pl.when(seq == 0)
    def _():
        pl.semaphore_wait(barrier, 5 + Z - 1 + others)

    @pl.when((x == 0) & (z > 0))
    def _():
        pl.semaphore_wait(barrier, 5 + 1 + others)

    @pl.when(x > 0)
    def _():
        pl.semaphore_wait(barrier, 5 + 1)

    def split(source):
        size = half // PARTS
        return [source.at[pl.ds(part * size, size), :] for part in range(PARTS)]

    def ring(number, source, to, unit):
        slot = SLOT[unit]
        return [
            pltpu.make_async_remote_copy(
                src_ref=here,
                dst_ref=there,
                send_sem=ring_send.at[number, part],
                recv_sem=ring_recv.at[slot, part],
                device_id=to,
                device_id_type=MESH,
            )
            for part, (here, there) in enumerate(zip(split(source), split(held.at[slot, core])))
        ]

    def mine(unit):
        return held.at[SLOT[unit], core]

    def to_pair(unit):
        slot = SLOT[unit]
        source = normed_ref.at[unit[1]] if unit[0] == 0 else mine(unit)
        return [
            pltpu.make_async_remote_copy(
                src_ref=here,
                dst_ref=there,
                send_sem=pair_send.at[slot, part],
                recv_sem=pair_recv.at[slot, part],
                device_id=pair,
                device_id_type=MESH,
            )
            for part, (here, there) in enumerate(zip(split(source), split(held.at[slot, core])))
        ]

    def start(copies):
        for copy in copies:
            copy.start()

    def await_pair(unit):
        for copy in pairs[unit]:
            copy.wait_recv()

    def take_on(number, unit, further=None):
        for part in range(PARTS):
            rings[number][part].wait_recv()
            if further is not None:
                rings[further][part].start()
            pairs[unit][part].start()

    rings = [
        ring(0, normed_ref.at[0], right, (1, 0)),
        ring(1, normed_ref.at[0], left, (3, 0)),
        ring(2, normed_ref.at[1], right, (1, 1)),
        ring(3, mine((1, 0)), right, (2, 0)),
        ring(4, mine((1, 1)), right, (2, 1)),
        ring(5, mine((2, 1)), right, (3, 1)),
    ]
    pairs = {unit: to_pair(unit) for unit in UNITS}
    side = [
        pltpu.make_async_remote_copy(
            src_ref=source,
            dst_ref=target,
            send_sem=slot_send.at[number],
            recv_sem=slot_recv.at[number],
            device_id=following,
            device_id_type=MESH,
        )
        for number, (source, target) in enumerate(
            [(slots_ref, slots_before_ref), (owner_ref, owner_before_ref)]
        )
    ]

    def lead_copy(number, to):
        return pltpu.make_async_remote_copy(
            src_ref=lead_ref,
            dst_ref=lead_ref,
            send_sem=lead_send.at[number],
            recv_sem=lead_recv,
            device_id=(to, head),
            device_id_type=MESH,
        )

    along_z = [lead_copy(to - 1, jnp.int32(to)) for to in range(1, Z)]
    along_x = [lead_copy(Z - 2 + to, to * Z + z) for to in range(1, n_seq // Z)]

    def row_starts(number):
        distance = pick(number, [unit[0] for unit in UNITS])
        later = pick(number, [unit[1] for unit in UNITS])
        first = lax.rem(y - distance + Y, Y) * (4 * half) + later * half
        second = lax.rem(y + distance, Y) * (4 * half) + 2 * half + later * half
        return pl.multiple_of(first, half), pl.multiple_of(second, half)

    def kv_copies(number):
        return [
            pltpu.make_async_remote_copy(
                src_ref=kv_ref.at[:, pl.ds(first, half), :],
                dst_ref=before_ref.at[:, pl.ds(first, half), :],
                send_sem=kv_send.at[2 * number + part],
                recv_sem=kv_recv.at[2 * number + part],
                device_id=following,
                device_id_type=MESH,
            )
            for part, first in enumerate(row_starts(number))
        ]

    start(rings[0])
    start(pairs[(0, 0)])
    start(rings[1])
    start(rings[2])
    start(pairs[(0, 1)])
    for copy in side:
        copy.start()

    token_facts(seq, new_len_ref, cache_len_ref, request_ref, begin_ref, place_ref)
    half_head = HD // 2
    lane = lax.broadcasted_iota(jnp.int32, (HD, HD), 1)
    entry = jnp.where(lane < half_head, lane, lane - half_head)
    frequency = jnp.exp(entry.astype(jnp.float32) * (-2.0 * THETA_LOG / HD))

    @pl.loop(0, place_ref.shape[0])
    def _(number):
        spread = jnp.broadcast_to(place_ref[pl.ds(number, 1), :], (HD, HD))
        angle = jnp.transpose(spread) * frequency
        at = pl.multiple_of(number * HD, HD)
        table_ref[pl.ds(at, HD), :] = jnp.where(lane < half_head, jnp.cos(angle), jnp.sin(angle))

    for copy in weights:
        copy.wait()
    def event_0():
        await_pair((0, 0))

    def event_1():
        await_pair((0, 1))

    def event_2():
        take_on(0, (1, 0), 3)
        await_pair((1, 0))

    def event_3():
        take_on(1, (3, 0))
        take_on(2, (1, 1), 4)
        await_pair((3, 0))

    def event_4():
        await_pair((1, 1))

    def event_5():
        take_on(3, (2, 0))
        await_pair((2, 0))

    def event_6():
        @pl.when(seq == 0)
        def _():
            lead_ref[...] = q_ref[:, pl.ds(0, LEAD), :]
            start(along_z)
            start(along_x)

        take_on(4, (2, 1), 5)
        await_pair((2, 1))

    def event_7():
        take_on(5, (3, 1))

        @pl.when((x == 0) & (z > 0))
        def _():
            along_z[0].wait_recv()
            start(along_x)

        await_pair((3, 1))

    events = [event_0, event_1, event_2, event_3, event_4, event_5, event_6, event_7]

    @pl.loop(0, len(UNITS))
    def _(number):
        for at, event in enumerate(events):
            pl.when(number == at)(event)
        block = held[number].reshape(2 * half, held.shape[3])
        starts = row_starts(number)
        table = jnp.concatenate([table_ref[pl.ds(first, half), :] for first in starts], axis=0)
        swapped = pltpu.roll(table, HD // 2, 1)
        low = lax.broadcasted_iota(jnp.int32, table.shape, 1) < HD // 2
        cosine = jnp.where(low, table, swapped)
        sine = jnp.where(low, -swapped, table)

        def turned(product):
            return (product * cosine + pltpu.roll(product, HD // 2, 1) * sine).astype(jnp.bfloat16)

        def put(ref, at, rows):
            for part, first in enumerate(starts):
                ref[at, pl.ds(first, half), :] = rows[part * half : (part + 1) * half]

        both = dot32(block, wkv_ref[...])
        put(kv_ref, 0, turned(both[:, :HD]))
        put(kv_ref, 1, both[:, HD:].astype(jnp.bfloat16))
        product = dot32(block, wq_ref[...])
        start(kv_copies(number))
        for at in range(heads):
            put(q_ref, at, turned(product[:, at * HD : (at + 1) * HD]))

    @pl.loop(0, len(UNITS))
    def _(number):
        for copy in kv_copies(number):
            copy.wait_recv()
            copy.wait_send()

    for copy in sum(rings, []) + sum(pairs.values(), []):
        copy.wait_send()
    for copy in side:
        copy.wait_recv()
        copy.wait_send()

    @pl.when(seq == 0)
    def _():
        for copy in along_z:
            copy.wait_send()

    @pl.when(x == 0)
    def _():
        for copy in along_x:
            copy.wait_send()

    @pl.when(x > 0)
    def _():
        along_x[0].wait_recv()


def gather_project(tokens, gain, w_query, w_key, w_value, new_len, cache_len, slots, owner):
    half, width = tokens.shape[1:]
    rows = 2 * half * lax.axis_size("head")
    heads = w_query.shape[1] // HD
    vmem = pl.BlockSpec(memory_space=pltpu.VMEM)
    smem = pl.BlockSpec(memory_space=pltpu.SMEM)
    hbm = pl.BlockSpec(memory_space=pl.ANY)
    dma = pltpu.SemaphoreType.DMA
    shape = jax.ShapeDtypeStruct
    facts = (rows // HD, HD)
    return pl.pallas_call(
        gather_kernel,
        in_specs=[vmem, vmem, hbm, hbm, hbm, smem, smem, vmem, vmem],
        out_specs=[vmem] * 8,
        out_shape=[
            shape((heads, rows, HD), jnp.bfloat16),
            shape((2, rows, HD), jnp.bfloat16),
            shape((2, rows, HD), jnp.bfloat16),
            shape(slots.shape, jnp.bfloat16),
            shape(owner.shape, jnp.int32),
            shape((heads, LEAD, HD), jnp.bfloat16),
            shape(facts, jnp.int32),
            shape(facts, jnp.int32),
        ],
        scratch_shapes=[
            pltpu.VMEM((2, half, width), jnp.bfloat16),
            pltpu.VMEM(w_query.shape, jnp.bfloat16),
            pltpu.VMEM((width, 2 * HD), jnp.bfloat16),
            pltpu.VMEM((rows, HD), jnp.float32),
            pltpu.VMEM(facts, jnp.float32),
            pltpu.VMEM((len(UNITS), 2, half, width), jnp.bfloat16),
            dma((6, PARTS)),
            dma((len(UNITS), PARTS)),
            dma((len(UNITS), PARTS)),
            dma((len(UNITS), PARTS)),
            dma((2 * len(UNITS),)),
            dma((2 * len(UNITS),)),
            dma((2,)),
            dma((2,)),
            dma((Z + 2,)),
            dma,
            dma((3,)),
        ],
        compiler_params=pltpu.CompilerParams(
            collective_id=0, has_side_effects=True, vmem_limit_bytes=LIMIT
        ),
        name="gather_project",
    )(tokens, gain, w_query, w_key, w_value, new_len, cache_len, slots, owner)


def local_kernel(
    begin_smem,
    q_ref,
    before_ref,
    here_ref,
    slot_before_ref,
    slot_here_ref,
    owner_before_ref,
    owner_here_ref,
    request_ref,
    begin_ref,
    lead_ref,
    cache_ref,
    out_ref,
    near_mix_ref,
    near_stat_ref,
    long_mix_ref,
    long_stat_ref,
    window,
    owners,
    top_ref,
    sum_ref,
    mix_ref,
):
    step = pl.program_id(0)
    rows = here_ref.shape[1]
    heads, tile, _ = q_ref.shape
    chunk = 2 * tile

    @pl.when(step == 0)
    def _():
        window[:, pl.ds(0, tile)] = jnp.zeros((2, tile, HD), jnp.bfloat16)
        window[:, pl.ds(tile, rows)] = before_ref[...]
        window[:, pl.ds(tile + rows, rows)] = here_ref[...]
        for at, ref in enumerate((owner_before_ref, owner_here_ref)):
            spread = jnp.broadcast_to(ref[...].astype(jnp.float32), (tile, ref.shape[1]))
            owners[at] = jnp.transpose(spread).astype(jnp.int32)
        long_state(lead_ref, cache_ref, long_mix_ref, long_stat_ref)

    request = request_ref[pl.ds(step, 1), :]
    begin = begin_ref[pl.ds(step, 1), :]
    down = lax.broadcasted_iota(jnp.int32, (chunk, tile), 0)
    index = rows + step * tile + lax.broadcasted_iota(jnp.int32, (1, tile), 1)
    queries = q_ref[...].reshape(heads * tile, HD)

    def take(keys, values, valid, fresh):
        scores = dot_t(keys, queries) * SCALE
        scores = jnp.where(jnp.concatenate([valid] * heads, axis=1), scores, LOW)
        top = jnp.max(scores, axis=0, keepdims=True)
        if not fresh:
            old = top_ref[...]
            top = jnp.maximum(top, old)
            keep = jnp.exp(old - top)
        weights = jnp.exp(scores - top)
        total = jnp.sum(weights, axis=0, keepdims=True)
        mixed = lax.dot_general(
            values,
            weights.astype(jnp.bfloat16),
            (((0,), (0,)), ((), ())),
            preferred_element_type=jnp.float32,
        )
        top_ref[...] = top
        if fresh:
            sum_ref[...] = total
            mix_ref[...] = mixed
        else:
            sum_ref[...] = sum_ref[...] * keep + total
            mix_ref[...] = mix_ref[...] * keep + mixed

    end = rows + (step + 1) * tile

    def new_chunk(number):
        key = end - (number + 1) * chunk
        key_at = key + down
        valid = (key_at >= begin) & (key_at <= index)
        at = pl.multiple_of(key + tile, tile)
        return window[0, pl.ds(at, chunk), :], window[1, pl.ds(at, chunk), :], valid

    def join(*parts):
        return [jnp.concatenate(pair, axis=0) for pair in zip(*parts)]

    first = begin_smem[step, 0]
    take(*join(new_chunk(0), (slot_here_ref[0], slot_here_ref[1], owners[1] == request)), True)

    @pl.loop(1, (end - first + chunk - 1) // chunk)
    def _(number):
        take(*new_chunk(number), False)

    @pl.when(first < rows)
    def _():
        take(slot_before_ref[0], slot_before_ref[1], owners[0] == request, False)

    mixed = mix_ref[...] / sum_ref[...]
    for head in range(heads):
        span = slice(head * tile, (head + 1) * tile)
        out_ref[:, span] = jnp.transpose(mixed[:, span]).astype(jnp.bfloat16)

    @pl.when(step == 0)
    def _():
        def leads(ref):
            parts = [ref[:, head * tile : head * tile + LEAD] for head in range(heads)]
            return jnp.concatenate(parts + parts[-1:], axis=1)

        near_mix_ref[...] = leads(mix_ref)
        near_stat_ref[...] = jnp.zeros_like(near_stat_ref)
        near_stat_ref[0:1, :] = leads(top_ref)
        near_stat_ref[1:2, :] = leads(sum_ref)


def long_state(q_ref, cache_ref, mix_ref, stat_ref):
    heads = q_ref.shape[0]
    queries = jnp.concatenate([q_ref[at] for at in range(heads)] + [q_ref[heads - 1]], axis=0)
    scores = dot_t(cache_ref[0], queries) * SCALE
    top = jnp.max(scores, axis=0, keepdims=True)
    weights = jnp.exp(scores - top)
    mixed = lax.dot_general(
        cache_ref[1],
        weights.astype(jnp.bfloat16),
        (((0,), (0,)), ((), ())),
        preferred_element_type=jnp.float32,
    )
    mix_ref[...] = mixed.astype(jnp.bfloat16)
    stat_ref[...] = jnp.zeros_like(stat_ref)
    stat_ref[0:1, :] = top
    stat_ref[1:2, :] = jnp.sum(weights, axis=0, keepdims=True)


def local_attention(
    begin, queries, before, here, slot_before, slot_here, owner_before, owner_here, request, lead, cache
):
    heads, rows, _ = queries.shape
    tile = HD
    columns = (heads + 1) * LEAD

    def whole(array):
        return pl.BlockSpec(array.shape, lambda i, first: (0,) * len(array.shape))

    shape = jax.ShapeDtypeStruct
    near_mix = shape((HD, columns), jnp.float32)
    long_mix = shape((HD, columns), jnp.bfloat16)
    long_stat = shape((8, columns), jnp.float32)
    kept = [before, here, slot_before, slot_here, owner_before, owner_here, request, begin, lead, cache]
    return pl.pallas_call(
        local_kernel,
        grid_spec=pltpu.PrefetchScalarGridSpec(
            num_scalar_prefetch=1,
            grid=(rows // tile,),
            in_specs=[pl.BlockSpec((heads, tile, HD), lambda i, first: (0, i, 0))]
            + [whole(array) for array in kept],
            out_specs=[pl.BlockSpec((tile, heads * HD), lambda i, first: (i, 0))]
            + [whole(array) for array in (near_mix, long_stat, long_mix, long_stat)],
            scratch_shapes=[
                pltpu.VMEM((2, tile + 2 * rows, HD), jnp.bfloat16),
                pltpu.VMEM((2, slot_here.shape[1], tile), jnp.int32),
                pltpu.VMEM((1, heads * tile), jnp.float32),
                pltpu.VMEM((1, heads * tile), jnp.float32),
                pltpu.VMEM((HD, heads * tile), jnp.float32),
            ],
        ),
        out_shape=[shape((rows, heads * HD), jnp.bfloat16), near_mix, long_stat, long_mix, long_stat],
        name="local_attention",
    )(begin, queries, *kept)


def merge(into, top, total, part, part_top, part_total):
    highest = jnp.maximum(top, part_top)
    keep, add = jnp.exp(top - highest), jnp.exp(part_top - highest)
    return into * keep + part * add, highest, total * keep + part_total * add


PIECES = 4


def scatter_kernel(
    attended_hbm,
    w_hbm,
    long_mix_ref,
    long_stat_ref,
    near_mix_ref,
    near_stat_ref,
    out_ref,
    pair_out,
    pair_in,
    own,
    ring_out,
    ring_in,
    mix_out,
    stat_out,
    mix_in,
    stat_in,
    pair_send,
    pair_recv,
    ring_send,
    ring_recv,
    sends,
    recvs,
    attended_ref,
    w_ref,
    load_sem,
):
    seq, head, y, core = place()
    loads = [
        pltpu.make_async_copy(attended_hbm, attended_ref, load_sem.at[0]),
        pltpu.make_async_copy(w_hbm, w_ref, load_sem.at[1]),
    ]
    for copy in loads:
        copy.start()
    n_x = lax.axis_size("seq") // Z
    x, z = seq // Z, lax.rem(seq, Z)
    way = 1 - 2 * core
    right = (seq, lax.rem(y + way + Y, Y) * 2 + core)
    left = (seq, lax.rem(y - way + Y, Y) * 2 + core)
    pair = (seq, head + way)
    half = ring_out.shape[2]
    heads = w_ref.shape[0] // HD
    width = w_ref.shape[1] // PIECES
    barrier = pltpu.get_barrier_semaphore()

    for device in (right, left, pair):
        greet(device)

    @pl.when(z > 0)
    def _():
        greet((x * Z, head))
        pl.semaphore_wait(barrier, 3 + 1)

    @pl.when((z == 0) & (x > 0))
    def _():
        for at in range(1, Z):
            greet((x * Z + at, head))
        greet((0, head))
        pl.semaphore_wait(barrier, 3 + Z)

    @pl.when(seq == 0)
    def _():
        for at in range(1, Z):
            greet((at, head))
        for at in range(1, n_x):
            greet((at * Z, head))
        pl.semaphore_wait(barrier, 3 + Z - 1 + n_x - 1)

    def columns(piece):
        return pl.ds(piece * width, width)

    def rows_of(chip, of_core, later):
        return attended_ref[pl.ds(pl.multiple_of(chip * (4 * half) + of_core * (2 * half) + later * half, half), half), :]

    def stack(later):
        parts = [rows_of(lax.rem(y - k * way + 2 * Y * 2, Y), 1 - core, later) for k in range(Y)]
        parts += [rows_of(lax.rem(y + k * way + 2 * Y * 2, Y), core, later) for k in range(Y)]
        return jnp.concatenate(parts, axis=0)

    def pair_copy(later, piece):
        return pltpu.make_async_remote_copy(
            src_ref=pair_out.at[later, :, columns(piece)],
            dst_ref=pair_in.at[later, :, columns(piece)],
            send_sem=pair_send.at[later, piece],
            recv_sem=pair_recv.at[later, piece],
            device_id=pair,
            device_id_type=MESH,
        )

    def ring_copy(later, step, piece):
        return pltpu.make_async_remote_copy(
            src_ref=ring_out.at[later, step, :, columns(piece)],
            dst_ref=ring_in.at[later, step, :, columns(piece)],
            send_sem=ring_send.at[later, step, piece],
            recv_sem=ring_recv.at[later, step, piece],
            device_id=left if (later, step) == (0, 2) else right,
            device_id_type=MESH,
        )

    def project(rows, later, piece):
        product = dot32(rows, w_ref[:, columns(piece)]).astype(jnp.bfloat16)
        pair_out[later, :, columns(piece)] = product[: Y * half]
        own[later, :, columns(piece)] = product[Y * half :]

    def chip_sum(later, k, piece):
        rows = pl.ds(k * half, half)
        return own[later, rows, columns(piece)].astype(jnp.float32) + pair_in[
            later, rows, columns(piece)
        ].astype(jnp.float32)

    def arrived(later, step, piece):
        ring_copy(later, step, piece).wait_recv()
        return ring_in[later, step, :, columns(piece)].astype(jnp.float32)

    def pass_on(later, step, piece, value):
        ring_out[later, step, :, columns(piece)] = value.astype(jnp.bfloat16)
        ring_copy(later, step, piece).start()

    def first_hop(piece):
        pair_copy(1, piece).wait_recv()
        pass_on(1, 0, piece, chip_sum(1, 3, piece))

    def keep_state(mixed, top, total):
        mix_out[...] = mixed.astype(jnp.bfloat16)
        stat_out[0:1, :] = top
        stat_out[1:2, :] = total

    def state_copies(slot, to, sources):
        return [
            pltpu.make_async_remote_copy(
                src_ref=source,
                dst_ref=target.at[slot],
                send_sem=sends.at[number],
                recv_sem=recvs.at[number, slot],
                device_id=(to, head),
                device_id_type=MESH,
            )
            for number, (source, target) in enumerate(zip(sources, (mix_in, stat_in)))
        ]

    def collect(slots, sources):
        mix, stat = sources
        state = (mix[...].astype(jnp.float32), stat[0:1, :], stat[1:2, :])
        for slot in slots:
            for copy in state_copies(slot, jnp.int32(0), sources):
                copy.wait_recv()
            state = merge(
                *state,
                mix_in[slot].astype(jnp.float32),
                stat_in[slot, 0:1, :],
                stat_in[slot, 1:2, :],
            )
        return state

    computed = (long_mix_ref, long_stat_ref)
    merged = (mix_out, stat_out)
    for at in range(1, Z):
        @pl.when(z == at)
        def _():
            for copy in state_copies(at - 1, x * Z, computed):
                copy.start()

    for copy in loads:
        copy.wait()
    rows = stack(1)
    for piece in range(PIECES):
        project(rows, 1, piece)
        pair_copy(1, piece).start()
        if piece:
            first_hop(piece - 1)
    first_hop(PIECES - 1)

    rows = stack(0)
    for piece in range(PIECES):
        project(rows, 0, piece)

    for piece in range(PIECES):
        pass_on(1, 1, piece, chip_sum(1, 2, piece) + arrived(1, 0, piece))

    @pl.when(z == 0)
    def _():
        stat_out[...] = jnp.zeros_like(stat_out)
        keep_state(*collect(range(Z - 1), computed))

    for at in range(1, n_x):
        @pl.when((z == 0) & (x == at))
        def _():
            for copy in state_copies(Z - 2 + at, jnp.int32(0), merged):
                copy.start()

    for piece in range(PIECES):
        pass_on(1, 2, piece, chip_sum(1, 1, piece) + arrived(1, 1, piece))

    @pl.when(seq == 0)
    def _():
        near = (near_mix_ref[...], near_stat_ref[0:1, :], near_stat_ref[1:2, :])
        mixed, _, total = merge(*near, *collect(range(Z - 1, Z + n_x - 2), merged))
        mixed = jnp.transpose(mixed / total).astype(jnp.bfloat16)
        parts = [mixed[at * LEAD : (at + 1) * LEAD] for at in range(heads)]
        lead_rows = jnp.concatenate(parts, axis=1)
        for piece in range(PIECES):
            product = dot32(lead_rows, w_ref[:, columns(piece)]).astype(jnp.bfloat16)

            @pl.when(core == 0)
            def _():
                at = pl.multiple_of(lax.rem(Y - y, Y) * half, half)
                own[0, pl.ds(at, half), columns(piece)] = product

            @pl.when(core == 1)
            def _():
                at = pl.multiple_of(lax.rem(Y - y, Y) * half, half)
                pair_out[0, pl.ds(at, half), columns(piece)] = product

    for piece in range(PIECES):
        pair_copy(0, piece).start()
    for piece in range(PIECES):
        pair_copy(0, piece).wait_recv()
        pass_on(0, 0, piece, chip_sum(0, 2, piece))
        pass_on(0, 2, piece, chip_sum(0, 3, piece))
    for piece in range(PIECES):
        value = chip_sum(1, 0, piece) + arrived(1, 2, piece)
        out_ref[pl.ds(half, half), columns(piece)] = value.astype(jnp.bfloat16)
    for piece in range(PIECES):
        pass_on(0, 1, piece, chip_sum(0, 1, piece) + arrived(0, 0, piece))
    for piece in range(PIECES):
        value = chip_sum(0, 0, piece) + arrived(0, 2, piece) + arrived(0, 1, piece)
        out_ref[pl.ds(0, half), columns(piece)] = value.astype(jnp.bfloat16)

    for later in range(2):
        for piece in range(PIECES):
            pair_copy(later, piece).wait_send()
            for step in range(3):
                ring_copy(later, step, piece).wait_send()

    @pl.when(seq > 0)
    def _():
        for copy in state_copies(0, jnp.int32(0), merged):
            copy.wait_send()


def project_scatter(attended, w_out, long_mix, long_stat, near_mix, near_stat):
    rows, inner = attended.shape
    width = w_out.shape[1]
    half = LEAD
    slots = Z - 1 + 3
    queries = long_mix.shape[1]
    vmem = pl.BlockSpec(memory_space=pltpu.VMEM)
    dma = pltpu.SemaphoreType.DMA
    return pl.pallas_call(
        scatter_kernel,
        in_specs=[pl.BlockSpec(memory_space=pl.ANY)] * 2 + [vmem] * 4,
        out_specs=vmem,
        out_shape=jax.ShapeDtypeStruct((2 * half, width), jnp.bfloat16),
        scratch_shapes=[
            pltpu.VMEM((2, Y * half, width), jnp.bfloat16),
            pltpu.VMEM((2, Y * half, width), jnp.bfloat16),
            pltpu.VMEM((2, Y * half, width), jnp.bfloat16),
            pltpu.VMEM((2, 3, half, width), jnp.bfloat16),
            pltpu.VMEM((2, 3, half, width), jnp.bfloat16),
            pltpu.VMEM((HD, queries), jnp.bfloat16),
            pltpu.VMEM((8, queries), jnp.float32),
            pltpu.VMEM((slots, HD, queries), jnp.bfloat16),
            pltpu.VMEM((slots, 8, queries), jnp.float32),
            dma((2, PIECES)),
            dma((2, PIECES)),
            dma((2, 3, PIECES)),
            dma((2, 3, PIECES)),
            dma((2,)),
            dma((2, slots)),
            pltpu.VMEM(attended.shape, jnp.bfloat16),
            pltpu.VMEM(w_out.shape, jnp.bfloat16),
            dma((2,)),
        ],
        compiler_params=pltpu.CompilerParams(
            collective_id=1, has_side_effects=True, vmem_limit_bytes=LIMIT
        ),
        name="project_scatter",
    )(attended, w_out, long_mix, long_stat, near_mix, near_stat)


def on_device(
    tokens,
    norm_gain,
    w_query,
    w_key,
    w_value,
    w_out,
    long_cache,
    short_cache,
    slot_owner,
    new_len,
    cache_len,
):
    owner = slot_owner[None, :]
    queries, here, before, earlier_slots, earlier_owner, lead, request, begin = gather_project(
        tokens.reshape(2, LEAD, tokens.shape[1]),
        norm_gain[None, :],
        w_query,
        w_key,
        w_value,
        new_len,
        cache_len,
        short_cache,
        owner,
    )
    attended, near_mix, near_stat, long_mix, long_stat = local_attention(
        begin,
        queries,
        before,
        here,
        earlier_slots,
        short_cache,
        earlier_owner,
        owner,
        request,
        lead,
        long_cache,
    )
    return project_scatter(attended, w_out, long_mix, long_stat, near_mix, near_stat)


def solution(mesh):
    placed = (
        P(("seq", "head"), None),
        P(),
        P(None, "head"),
        P(None, "head"),
        P(None, "head"),
        P("head", None),
        P(None, "seq", "head"),
        P(None, "seq", "head"),
        P("seq"),
        P(),
        P(),
    )
    return jax.shard_map(
        on_device, mesh=mesh, in_specs=placed, out_specs=P(("seq", "head"), None), check_vma=False
    )
```

```python
import math

import jax
import jax.numpy as jnp
from jax import lax
from jax.experimental import pallas as pl
from jax.experimental.pallas import tpu as pltpu
from jax.sharding import PartitionSpec as P

HD = 128
LEAD = 64
THETA_LOG = math.log(500000.0)
SCALE = 1.0 / math.sqrt(HD)
LOW = -1e30


def normalize(tokens, norm_gain):
    values = tokens.astype(jnp.float32)
    mean_square = jnp.mean(values * values, axis=-1, keepdims=True)
    return (values * lax.rsqrt(mean_square + 1e-05) * norm_gain).astype(jnp.bfloat16)


def dot32(a, b):
    return jnp.dot(a, b, preferred_element_type=jnp.float32)


def dot_t(a, b):
    return lax.dot_general(a, b, (((1,), (1,)), ((), ())), preferred_element_type=jnp.float32)


MESH = pl.DeviceIdType.MESH
LIMIT = 60 * 1024 * 1024
Z = 8
Y = 4
LONG_ROWS = 1024
PARTS = 2
UNITS = [(0, 0), (0, 1), (1, 0), (3, 0), (1, 1), (2, 0), (2, 1), (3, 1)]
SLOT = {unit: number for number, unit in enumerate(UNITS)}


def place():
    seq = lax.axis_index("seq")
    head = lax.axis_index("head")
    return seq, head, head // 2, lax.rem(head, 2)


def pick(number, table):
    value = jnp.int32(table[0])
    for at, entry in enumerate(table):
        value = jnp.where(number == at, jnp.int32(entry), value)
    return value


def greet(device):
    pl.semaphore_signal(
        pltpu.get_barrier_semaphore(), inc=1, device_id=device, device_id_type=MESH
    )


def token_facts(seq, new_len_ref, cache_len_ref, request_ref, begin_ref, place_ref):
    number = new_len_ref.shape[0]
    shape = request_ref.shape
    rows = shape[0] * shape[1]
    token = (
        seq * rows
        + lax.broadcasted_iota(jnp.int32, shape, 0) * shape[1]
        + lax.broadcasted_iota(jnp.int32, shape, 1)
    )

    def step(at, carry):
        start, request, begin, cached = carry
        passed = token >= start
        return (
            start + new_len_ref[at],
            jnp.where(passed, at, request),
            jnp.where(passed, start, begin),
            jnp.where(passed, cache_len_ref[at], cached),
        )

    zero = jnp.zeros(shape, jnp.int32)
    _, request, begin, cached = lax.fori_loop(
        0, number, step, (jnp.int32(LEAD), zero + number, zero, zero)
    )
    lead = request == number
    long_len = lax.axis_size("seq") * LONG_ROWS
    position = jnp.where(lead, token + long_len, token - begin + cached)
    place_ref[...] = position.astype(jnp.float32)
    request_ref[...] = request
    begin_ref[...] = jnp.where(lead, rows, jnp.maximum(begin - (seq - 1) * rows, 0))


def gather_kernel(
    tokens_ref,
    gain_ref,
    wq_hbm,
    wk_hbm,
    wv_hbm,
    new_len_ref,
    cache_len_ref,
    slots_ref,
    owner_ref,
    q_ref,
    kv_ref,
    before_ref,
    slots_before_ref,
    owner_before_ref,
    lead_ref,
    request_ref,
    begin_ref,
    normed_ref,
    wq_ref,
    wkv_ref,
    table_ref,
    place_ref,
    held,
    ring_send,
    ring_recv,
    pair_send,
    pair_recv,
    kv_send,
    kv_recv,
    slot_send,
    slot_recv,
    lead_send,
    lead_recv,
    weight_sem,
):
    seq, head, y, core = place()
    weights = [
        pltpu.make_async_copy(wk_hbm, wkv_ref.at[:, pl.ds(0, HD)], weight_sem.at[0]),
        pltpu.make_async_copy(wv_hbm, wkv_ref.at[:, pl.ds(HD, HD)], weight_sem.at[1]),
        pltpu.make_async_copy(wq_hbm, wq_ref, weight_sem.at[2]),
    ]
    for copy in weights:
        copy.start()
    n_seq = lax.axis_size("seq")
    x, z = seq // Z, lax.rem(seq, Z)
    way = 1 - 2 * core
    right = (seq, lax.rem(y + way + Y, Y) * 2 + core)
    left = (seq, lax.rem(y - way + Y, Y) * 2 + core)
    pair = (seq, head + way)
    following = (lax.rem(seq + 1, n_seq), head)
    previous = (lax.rem(seq + n_seq - 1, n_seq), head)
    heads = q_ref.shape[0]
    half = held.shape[2]

    for device in (right, left, pair, following, previous):
        greet(device)

    @pl.when(seq == 0)
    def _():
        for to in range(1, Z):
            greet((to, head))

    @pl.when(x == 0)
    def _():
        for to in range(1, n_seq // Z):
            greet((to * Z + z, head))

    @pl.when((x == 0) & (z > 0))
    def _():
        greet((0, head))

    @pl.when(x > 0)
    def _():
        greet((z, head))

    for later in range(2):
        normed_ref[later] = normalize(tokens_ref[later], gain_ref[...])
        held[SLOT[(0, later)], core] = normed_ref[later]

    barrier = pltpu.get_barrier_semaphore()
    others = n_seq // Z - 1

    @pl.when(seq == 0)
    def _():
        pl.semaphore_wait(barrier, 5 + Z - 1 + others)

    @pl.when((x == 0) & (z > 0))
    def _():
        pl.semaphore_wait(barrier, 5 + 1 + others)

    @pl.when(x > 0)
    def _():
        pl.semaphore_wait(barrier, 5 + 1)

    def split(source):
        size = half // PARTS
        return [source.at[pl.ds(part * size, size), :] for part in range(PARTS)]

    def ring(number, source, to, unit):
        slot = SLOT[unit]
        return [
            pltpu.make_async_remote_copy(
                src_ref=here,
                dst_ref=there,
                send_sem=ring_send.at[number, part],
                recv_sem=ring_recv.at[slot, part],
                device_id=to,
                device_id_type=MESH,
            )
            for part, (here, there) in enumerate(zip(split(source), split(held.at[slot, core])))
        ]

    def mine(unit):
        return held.at[SLOT[unit], core]

    def to_pair(unit):
        slot = SLOT[unit]
        source = normed_ref.at[unit[1]] if unit[0] == 0 else mine(unit)
        return [
            pltpu.make_async_remote_copy(
                src_ref=here,
                dst_ref=there,
                send_sem=pair_send.at[slot, part],
                recv_sem=pair_recv.at[slot, part],
                device_id=pair,
                device_id_type=MESH,
            )
            for part, (here, there) in enumerate(zip(split(source), split(held.at[slot, core])))
        ]

    def start(copies):
        for copy in copies:
            copy.start()

    def await_pair(unit):
        for copy in pairs[unit]:
            copy.wait_recv()

    def take_on(number, unit, further=None):
        for part in range(PARTS):
            rings[number][part].wait_recv()
            if further is not None:
                rings[further][part].start()
            pairs[unit][part].start()

    rings = [
        ring(0, normed_ref.at[0], right, (1, 0)),
        ring(1, normed_ref.at[0], left, (3, 0)),
        ring(2, normed_ref.at[1], right, (1, 1)),
        ring(3, mine((1, 0)), right, (2, 0)),
        ring(4, mine((1, 1)), right, (2, 1)),
        ring(5, mine((2, 1)), right, (3, 1)),
    ]
    pairs = {unit: to_pair(unit) for unit in UNITS}
    side = [
        pltpu.make_async_remote_copy(
            src_ref=source,
            dst_ref=target,
            send_sem=slot_send.at[number],
            recv_sem=slot_recv.at[number],
            device_id=following,
            device_id_type=MESH,
        )
        for number, (source, target) in enumerate(
            [(slots_ref, slots_before_ref), (owner_ref, owner_before_ref)]
        )
    ]

    def lead_copy(number, to):
        return pltpu.make_async_remote_copy(
            src_ref=lead_ref,
            dst_ref=lead_ref,
            send_sem=lead_send.at[number],
            recv_sem=lead_recv,
            device_id=(to, head),
            device_id_type=MESH,
        )

    along_z = [lead_copy(to - 1, jnp.int32(to)) for to in range(1, Z)]
    along_x = [lead_copy(Z - 2 + to, to * Z + z) for to in range(1, n_seq // Z)]

    def row_starts(number):
        distance = pick(number, [unit[0] for unit in UNITS])
        later = pick(number, [unit[1] for unit in UNITS])
        first = lax.rem(y - distance + Y, Y) * (4 * half) + later * half
        second = lax.rem(y + distance, Y) * (4 * half) + 2 * half + later * half
        return pl.multiple_of(first, half), pl.multiple_of(second, half)

    def kv_copies(number):
        return [
            pltpu.make_async_remote_copy(
                src_ref=kv_ref.at[:, pl.ds(first, half), :],
                dst_ref=before_ref.at[:, pl.ds(first, half), :],
                send_sem=kv_send.at[2 * number + part],
                recv_sem=kv_recv.at[2 * number + part],
                device_id=following,
                device_id_type=MESH,
            )
            for part, first in enumerate(row_starts(number))
        ]

    start(rings[0])
    start(pairs[(0, 0)])
    start(rings[1])
    start(rings[2])
    start(pairs[(0, 1)])
    for copy in side:
        copy.start()

    token_facts(seq, new_len_ref, cache_len_ref, request_ref, begin_ref, place_ref)
    half_head = HD // 2
    lane = lax.broadcasted_iota(jnp.int32, (HD, HD), 1)
    entry = jnp.where(lane < half_head, lane, lane - half_head)
    frequency = jnp.exp(entry.astype(jnp.float32) * (-2.0 * THETA_LOG / HD))

    @pl.loop(0, place_ref.shape[0])
    def _(number):
        spread = jnp.broadcast_to(place_ref[pl.ds(number, 1), :], (HD, HD))
        angle = jnp.transpose(spread) * frequency
        at = pl.multiple_of(number * HD, HD)
        table_ref[pl.ds(at, HD), :] = jnp.where(lane < half_head, jnp.cos(angle), jnp.sin(angle))

    for copy in weights:
        copy.wait()
    def event_0():
        await_pair((0, 0))

    def event_1():
        await_pair((0, 1))

    def event_2():
        take_on(0, (1, 0), 3)
        await_pair((1, 0))

    def event_3():
        take_on(1, (3, 0))
        take_on(2, (1, 1), 4)
        await_pair((3, 0))

    def event_4():
        await_pair((1, 1))

    def event_5():
        take_on(3, (2, 0))
        await_pair((2, 0))

    def event_6():
        @pl.when(seq == 0)
        def _():
            lead_ref[...] = q_ref[:, pl.ds(0, LEAD), :]
            start(along_z)
            start(along_x)

        take_on(4, (2, 1), 5)
        await_pair((2, 1))

    def event_7():
        take_on(5, (3, 1))

        @pl.when((x == 0) & (z > 0))
        def _():
            along_z[0].wait_recv()
            start(along_x)

        await_pair((3, 1))

    events = [event_0, event_1, event_2, event_3, event_4, event_5, event_6, event_7]

    @pl.loop(0, len(UNITS))
    def _(number):
        for at, event in enumerate(events):
            pl.when(number == at)(event)
        block = held[number].reshape(2 * half, held.shape[3])
        starts = row_starts(number)
        table = jnp.concatenate([table_ref[pl.ds(first, half), :] for first in starts], axis=0)
        swapped = pltpu.roll(table, HD // 2, 1)
        low = lax.broadcasted_iota(jnp.int32, table.shape, 1) < HD // 2
        cosine = jnp.where(low, table, swapped)
        sine = jnp.where(low, -swapped, table)

        def turned(product):
            return (product * cosine + pltpu.roll(product, HD // 2, 1) * sine).astype(jnp.bfloat16)

        def put(ref, at, rows):
            for part, first in enumerate(starts):
                ref[at, pl.ds(first, half), :] = rows[part * half : (part + 1) * half]

        both = dot32(block, wkv_ref[...])
        put(kv_ref, 0, turned(both[:, :HD]))
        put(kv_ref, 1, both[:, HD:].astype(jnp.bfloat16))
        product = dot32(block, wq_ref[...])
        start(kv_copies(number))
        for at in range(heads):
            put(q_ref, at, turned(product[:, at * HD : (at + 1) * HD]))

    @pl.loop(0, len(UNITS))
    def _(number):
        for copy in kv_copies(number):
            copy.wait_recv()
            copy.wait_send()

    for copy in sum(rings, []) + sum(pairs.values(), []):
        copy.wait_send()
    for copy in side:
        copy.wait_recv()
        copy.wait_send()

    @pl.when(seq == 0)
    def _():
        for copy in along_z:
            copy.wait_send()

    @pl.when(x == 0)
    def _():
        for copy in along_x:
            copy.wait_send()

    @pl.when(x > 0)
    def _():
        along_x[0].wait_recv()


def gather_project(tokens, gain, w_query, w_key, w_value, new_len, cache_len, slots, owner):
    half, width = tokens.shape[1:]
    rows = 2 * half * lax.axis_size("head")
    heads = w_query.shape[1] // HD
    vmem = pl.BlockSpec(memory_space=pltpu.VMEM)
    smem = pl.BlockSpec(memory_space=pltpu.SMEM)
    hbm = pl.BlockSpec(memory_space=pl.ANY)
    dma = pltpu.SemaphoreType.DMA
    shape = jax.ShapeDtypeStruct
    facts = (rows // HD, HD)
    return pl.pallas_call(
        gather_kernel,
        in_specs=[vmem, vmem, hbm, hbm, hbm, smem, smem, vmem, vmem],
        out_specs=[vmem] * 8,
        out_shape=[
            shape((heads, rows, HD), jnp.bfloat16),
            shape((2, rows, HD), jnp.bfloat16),
            shape((2, rows, HD), jnp.bfloat16),
            shape(slots.shape, jnp.bfloat16),
            shape(owner.shape, jnp.int32),
            shape((heads, LEAD, HD), jnp.bfloat16),
            shape(facts, jnp.int32),
            shape(facts, jnp.int32),
        ],
        scratch_shapes=[
            pltpu.VMEM((2, half, width), jnp.bfloat16),
            pltpu.VMEM(w_query.shape, jnp.bfloat16),
            pltpu.VMEM((width, 2 * HD), jnp.bfloat16),
            pltpu.VMEM((rows, HD), jnp.float32),
            pltpu.VMEM(facts, jnp.float32),
            pltpu.VMEM((len(UNITS), 2, half, width), jnp.bfloat16),
            dma((6, PARTS)),
            dma((len(UNITS), PARTS)),
            dma((len(UNITS), PARTS)),
            dma((len(UNITS), PARTS)),
            dma((2 * len(UNITS),)),
            dma((2 * len(UNITS),)),
            dma((2,)),
            dma((2,)),
            dma((Z + 2,)),
            dma,
            dma((3,)),
        ],
        compiler_params=pltpu.CompilerParams(
            collective_id=0, has_side_effects=True, vmem_limit_bytes=LIMIT
        ),
        name="gather_project",
    )(tokens, gain, w_query, w_key, w_value, new_len, cache_len, slots, owner)


def local_kernel(
    begin_smem,
    q_ref,
    before_ref,
    here_ref,
    slot_before_ref,
    slot_here_ref,
    owner_before_ref,
    owner_here_ref,
    request_ref,
    begin_ref,
    lead_ref,
    cache_ref,
    out_ref,
    near_mix_ref,
    near_stat_ref,
    long_mix_ref,
    long_stat_ref,
    window,
    owners,
    top_ref,
    sum_ref,
    mix_ref,
):
    step = pl.program_id(0)
    rows = here_ref.shape[1]
    heads, tile, _ = q_ref.shape
    chunk = 2 * tile

    @pl.when(step == 0)
    def _():
        window[:, pl.ds(0, tile)] = jnp.zeros((2, tile, HD), jnp.bfloat16)
        window[:, pl.ds(tile, rows)] = before_ref[...]
        window[:, pl.ds(tile + rows, rows)] = here_ref[...]
        for at, ref in enumerate((owner_before_ref, owner_here_ref)):
            spread = jnp.broadcast_to(ref[...].astype(jnp.float32), (tile, ref.shape[1]))
            owners[at] = jnp.transpose(spread).astype(jnp.int32)
        long_state(lead_ref, cache_ref, long_mix_ref, long_stat_ref)

    request = request_ref[pl.ds(step, 1), :]
    begin = begin_ref[pl.ds(step, 1), :]
    down = lax.broadcasted_iota(jnp.int32, (chunk, tile), 0)
    index = rows + step * tile + lax.broadcasted_iota(jnp.int32, (1, tile), 1)
    queries = q_ref[...].reshape(heads * tile, HD)

    def take(keys, values, valid, fresh):
        scores = dot_t(keys, queries) * SCALE
        scores = jnp.where(jnp.concatenate([valid] * heads, axis=1), scores, LOW)
        top = jnp.max(scores, axis=0, keepdims=True)
        if not fresh:
            old = top_ref[...]
            top = jnp.maximum(top, old)
            keep = jnp.exp(old - top)
        weights = jnp.exp(scores - top)
        total = jnp.sum(weights, axis=0, keepdims=True)
        mixed = lax.dot_general(
            values,
            weights.astype(jnp.bfloat16),
            (((0,), (0,)), ((), ())),
            preferred_element_type=jnp.float32,
        )
        top_ref[...] = top
        if fresh:
            sum_ref[...] = total
            mix_ref[...] = mixed
        else:
            sum_ref[...] = sum_ref[...] * keep + total
            mix_ref[...] = mix_ref[...] * keep + mixed

    end = rows + (step + 1) * tile

    def new_chunk(number):
        key = end - (number + 1) * chunk
        key_at = key + down
        valid = (key_at >= begin) & (key_at <= index)
        at = pl.multiple_of(key + tile, tile)
        return window[0, pl.ds(at, chunk), :], window[1, pl.ds(at, chunk), :], valid

    def join(*parts):
        return [jnp.concatenate(pair, axis=0) for pair in zip(*parts)]

    first = begin_smem[step, 0]
    take(*join(new_chunk(0), (slot_here_ref[0], slot_here_ref[1], owners[1] == request)), True)

    @pl.loop(1, (end - first + chunk - 1) // chunk)
    def _(number):
        take(*new_chunk(number), False)

    @pl.when(first < rows)
    def _():
        take(slot_before_ref[0], slot_before_ref[1], owners[0] == request, False)

    mixed = mix_ref[...] / sum_ref[...]
    for head in range(heads):
        span = slice(head * tile, (head + 1) * tile)
        out_ref[:, span] = jnp.transpose(mixed[:, span]).astype(jnp.bfloat16)

    @pl.when(step == 0)
    def _():
        def leads(ref):
            parts = [ref[:, head * tile : head * tile + LEAD] for head in range(heads)]
            return jnp.concatenate(parts + parts[-1:], axis=1)

        near_mix_ref[...] = leads(mix_ref)
        near_stat_ref[...] = jnp.zeros_like(near_stat_ref)
        near_stat_ref[0:1, :] = leads(top_ref)
        near_stat_ref[1:2, :] = leads(sum_ref)


def long_state(q_ref, cache_ref, mix_ref, stat_ref):
    heads = q_ref.shape[0]
    queries = jnp.concatenate([q_ref[at] for at in range(heads)] + [q_ref[heads - 1]], axis=0)
    scores = dot_t(cache_ref[0], queries) * SCALE
    top = jnp.max(scores, axis=0, keepdims=True)
    weights = jnp.exp(scores - top)
    mixed = lax.dot_general(
        cache_ref[1],
        weights.astype(jnp.bfloat16),
        (((0,), (0,)), ((), ())),
        preferred_element_type=jnp.float32,
    )
    mix_ref[...] = mixed.astype(jnp.bfloat16)
    stat_ref[...] = jnp.zeros_like(stat_ref)
    stat_ref[0:1, :] = top
    stat_ref[1:2, :] = jnp.sum(weights, axis=0, keepdims=True)


def local_attention(
    begin, queries, before, here, slot_before, slot_here, owner_before, owner_here, request, lead, cache
):
    heads, rows, _ = queries.shape
    tile = HD
    columns = (heads + 1) * LEAD

    def whole(array):
        return pl.BlockSpec(array.shape, lambda i, first: (0,) * len(array.shape))

    shape = jax.ShapeDtypeStruct
    near_mix = shape((HD, columns), jnp.float32)
    long_mix = shape((HD, columns), jnp.bfloat16)
    long_stat = shape((8, columns), jnp.float32)
    kept = [before, here, slot_before, slot_here, owner_before, owner_here, request, begin, lead, cache]
    return pl.pallas_call(
        local_kernel,
        grid_spec=pltpu.PrefetchScalarGridSpec(
            num_scalar_prefetch=1,
            grid=(rows // tile,),
            in_specs=[pl.BlockSpec((heads, tile, HD), lambda i, first: (0, i, 0))]
            + [whole(array) for array in kept],
            out_specs=[pl.BlockSpec((tile, heads * HD), lambda i, first: (i, 0))]
            + [whole(array) for array in (near_mix, long_stat, long_mix, long_stat)],
            scratch_shapes=[
                pltpu.VMEM((2, tile + 2 * rows, HD), jnp.bfloat16),
                pltpu.VMEM((2, slot_here.shape[1], tile), jnp.int32),
                pltpu.VMEM((1, heads * tile), jnp.float32),
                pltpu.VMEM((1, heads * tile), jnp.float32),
                pltpu.VMEM((HD, heads * tile), jnp.float32),
            ],
        ),
        out_shape=[shape((rows, heads * HD), jnp.bfloat16), near_mix, long_stat, long_mix, long_stat],
        name="local_attention",
    )(begin, queries, *kept)


def merge(into, top, total, part, part_top, part_total):
    highest = jnp.maximum(top, part_top)
    keep, add = jnp.exp(top - highest), jnp.exp(part_top - highest)
    return into * keep + part * add, highest, total * keep + part_total * add


PIECES = 4


def scatter_kernel(
    attended_hbm,
    w_hbm,
    long_mix_ref,
    long_stat_ref,
    near_mix_ref,
    near_stat_ref,
    out_ref,
    pair_out,
    pair_in,
    own,
    ring_out,
    ring_in,
    mix_out,
    stat_out,
    mix_in,
    stat_in,
    pair_send,
    pair_recv,
    ring_send,
    ring_recv,
    sends,
    recvs,
    attended_ref,
    w_ref,
    load_sem,
):
    seq, head, y, core = place()
    loads = [
        pltpu.make_async_copy(attended_hbm, attended_ref, load_sem.at[0]),
        pltpu.make_async_copy(w_hbm, w_ref, load_sem.at[1]),
    ]
    for copy in loads:
        copy.start()
    n_x = lax.axis_size("seq") // Z
    x, z = seq // Z, lax.rem(seq, Z)
    way = 1 - 2 * core
    right = (seq, lax.rem(y + way + Y, Y) * 2 + core)
    left = (seq, lax.rem(y - way + Y, Y) * 2 + core)
    pair = (seq, head + way)
    half = ring_out.shape[2]
    heads = w_ref.shape[0] // HD
    width = w_ref.shape[1] // PIECES
    barrier = pltpu.get_barrier_semaphore()

    for device in (right, left, pair):
        greet(device)

    @pl.when(z > 0)
    def _():
        greet((x * Z, head))
        pl.semaphore_wait(barrier, 3 + 1)

    @pl.when((z == 0) & (x > 0))
    def _():
        for at in range(1, Z):
            greet((x * Z + at, head))
        greet((0, head))
        pl.semaphore_wait(barrier, 3 + Z)

    @pl.when(seq == 0)
    def _():
        for at in range(1, Z):
            greet((at, head))
        for at in range(1, n_x):
            greet((at * Z, head))
        pl.semaphore_wait(barrier, 3 + Z - 1 + n_x - 1)

    def columns(piece):
        return pl.ds(piece * width, width)

    def rows_of(chip, of_core, later):
        return attended_ref[pl.ds(pl.multiple_of(chip * (4 * half) + of_core * (2 * half) + later * half, half), half), :]

    def stack(later):
        parts = [rows_of(lax.rem(y - k * way + 2 * Y * 2, Y), 1 - core, later) for k in range(Y)]
        parts += [rows_of(lax.rem(y + k * way + 2 * Y * 2, Y), core, later) for k in range(Y)]
        return jnp.concatenate(parts, axis=0)

    def pair_copy(later, number):
        if later:
            at = (later, slice(None), columns(number))
        else:
            at = (later, pl.ds(number * half, half), slice(None))
        return pltpu.make_async_remote_copy(
            src_ref=pair_out.at[at],
            dst_ref=pair_in.at[at],
            send_sem=pair_send.at[later, number],
            recv_sem=pair_recv.at[later, number],
            device_id=pair,
            device_id_type=MESH,
        )

    def ring_copy(later, step, piece):
        return pltpu.make_async_remote_copy(
            src_ref=ring_out.at[later, step, :, columns(piece)],
            dst_ref=ring_in.at[later, step, :, columns(piece)],
            send_sem=ring_send.at[later, step, piece],
            recv_sem=ring_recv.at[later, step, piece],
            device_id=left if (later, step) == (0, 2) else right,
            device_id_type=MESH,
        )

    def project(rows, later, piece):
        product = dot32(rows, w_ref[:, columns(piece)]).astype(jnp.bfloat16)
        pair_out[later, :, columns(piece)] = product[: Y * half]
        own[later, :, columns(piece)] = product[Y * half :]

    def chip_sum(later, k, piece):
        rows = pl.ds(k * half, half)
        return own[later, rows, columns(piece)].astype(jnp.float32) + pair_in[
            later, rows, columns(piece)
        ].astype(jnp.float32)

    def arrived(later, step, piece):
        ring_copy(later, step, piece).wait_recv()
        return ring_in[later, step, :, columns(piece)].astype(jnp.float32)

    def pass_on(later, step, piece, value):
        ring_out[later, step, :, columns(piece)] = value.astype(jnp.bfloat16)
        ring_copy(later, step, piece).start()

    def first_hop(piece):
        pair_copy(1, piece).wait_recv()
        pass_on(1, 0, piece, chip_sum(1, 3, piece))

    def keep_state(mixed, top, total):
        mix_out[...] = mixed.astype(jnp.bfloat16)
        stat_out[0:1, :] = top
        stat_out[1:2, :] = total

    def state_copies(slot, to, sources):
        return [
            pltpu.make_async_remote_copy(
                src_ref=source,
                dst_ref=target.at[slot],
                send_sem=sends.at[number],
                recv_sem=recvs.at[number, slot],
                device_id=(to, head),
                device_id_type=MESH,
            )
            for number, (source, target) in enumerate(zip(sources, (mix_in, stat_in)))
        ]

    def collect(slots, sources):
        mix, stat = sources
        state = (mix[...].astype(jnp.float32), stat[0:1, :], stat[1:2, :])
        for slot in slots:
            for copy in state_copies(slot, jnp.int32(0), sources):
                copy.wait_recv()
            state = merge(
                *state,
                mix_in[slot].astype(jnp.float32),
                stat_in[slot, 0:1, :],
                stat_in[slot, 1:2, :],
            )
        return state

    computed = (long_mix_ref, long_stat_ref)
    merged = (mix_out, stat_out)
    for at in range(1, Z):
        @pl.when(z == at)
        def _():
            for copy in state_copies(at - 1, x * Z, computed):
                copy.start()

    for copy in loads:
        copy.wait()
    rows = stack(1)
    for piece in range(PIECES):
        project(rows, 1, piece)
        pair_copy(1, piece).start()
        if piece:
            first_hop(piece - 1)
    first_hop(PIECES - 1)

    rows = stack(0)
    for piece in range(PIECES):
        project(rows, 0, piece)

    lead_block = jnp.where(seq == 0, lax.rem(Y - y, Y), -1)
    for k in range(Y):
        @pl.when((core == 0) | (lead_block != k))
        def _():
            pair_copy(0, k).start()

    for piece in range(PIECES):
        pass_on(1, 1, piece, chip_sum(1, 2, piece) + arrived(1, 0, piece))

    @pl.when(z == 0)
    def _():
        stat_out[...] = jnp.zeros_like(stat_out)
        keep_state(*collect(range(Z - 1), computed))

    for at in range(1, n_x):
        @pl.when((z == 0) & (x == at))
        def _():
            for copy in state_copies(Z - 2 + at, jnp.int32(0), merged):
                copy.start()

    for piece in range(PIECES):
        pass_on(1, 2, piece, chip_sum(1, 1, piece) + arrived(1, 1, piece))

    def early_hop(step, k):
        pair_copy(0, k).wait_recv()
        for piece in range(PIECES):
            pass_on(0, step, piece, chip_sum(0, k, piece))

    for step, k in ((0, 2), (2, 3)):
        @pl.when((core == 1) | (lead_block != k))
        def _():
            early_hop(step, k)

    @pl.when(seq == 0)
    def _():
        near = (near_mix_ref[...], near_stat_ref[0:1, :], near_stat_ref[1:2, :])
        mixed, _, total = merge(*near, *collect(range(Z - 1, Z + n_x - 2), merged))
        mixed = jnp.transpose(mixed / total).astype(jnp.bfloat16)
        parts = [mixed[at * LEAD : (at + 1) * LEAD] for at in range(heads)]
        lead_rows = jnp.concatenate(parts, axis=1)
        for piece in range(PIECES):
            product = dot32(lead_rows, w_ref[:, columns(piece)]).astype(jnp.bfloat16)

            @pl.when(core == 0)
            def _():
                at = pl.multiple_of(lax.rem(Y - y, Y) * half, half)
                own[0, pl.ds(at, half), columns(piece)] = product

            @pl.when(core == 1)
            def _():
                at = pl.multiple_of(lax.rem(Y - y, Y) * half, half)
                pair_out[0, pl.ds(at, half), columns(piece)] = product

    for k in range(Y):
        @pl.when((core == 1) & (lead_block == k))
        def _():
            pair_copy(0, k).start()

    for step, k in ((0, 2), (2, 3)):
        @pl.when((core == 0) & (lead_block == k))
        def _():
            early_hop(step, k)

    for piece in range(PIECES):
        value = chip_sum(1, 0, piece) + arrived(1, 2, piece)
        out_ref[pl.ds(half, half), columns(piece)] = value.astype(jnp.bfloat16)
    pair_copy(0, 1).wait_recv()
    for piece in range(PIECES):
        pass_on(0, 1, piece, chip_sum(0, 1, piece) + arrived(0, 0, piece))
    pair_copy(0, 0).wait_recv()
    for piece in range(PIECES):
        value = chip_sum(0, 0, piece) + arrived(0, 2, piece) + arrived(0, 1, piece)
        out_ref[pl.ds(0, half), columns(piece)] = value.astype(jnp.bfloat16)

    for later in range(2):
        for piece in range(PIECES):
            pair_copy(later, piece).wait_send()
            for step in range(3):
                ring_copy(later, step, piece).wait_send()

    @pl.when(seq > 0)
    def _():
        for copy in state_copies(0, jnp.int32(0), merged):
            copy.wait_send()


def project_scatter(attended, w_out, long_mix, long_stat, near_mix, near_stat):
    rows, inner = attended.shape
    width = w_out.shape[1]
    half = LEAD
    slots = Z - 1 + 3
    queries = long_mix.shape[1]
    vmem = pl.BlockSpec(memory_space=pltpu.VMEM)
    dma = pltpu.SemaphoreType.DMA
    return pl.pallas_call(
        scatter_kernel,
        in_specs=[pl.BlockSpec(memory_space=pl.ANY)] * 2 + [vmem] * 4,
        out_specs=vmem,
        out_shape=jax.ShapeDtypeStruct((2 * half, width), jnp.bfloat16),
        scratch_shapes=[
            pltpu.VMEM((2, Y * half, width), jnp.bfloat16),
            pltpu.VMEM((2, Y * half, width), jnp.bfloat16),
            pltpu.VMEM((2, Y * half, width), jnp.bfloat16),
            pltpu.VMEM((2, 3, half, width), jnp.bfloat16),
            pltpu.VMEM((2, 3, half, width), jnp.bfloat16),
            pltpu.VMEM((HD, queries), jnp.bfloat16),
            pltpu.VMEM((8, queries), jnp.float32),
            pltpu.VMEM((slots, HD, queries), jnp.bfloat16),
            pltpu.VMEM((slots, 8, queries), jnp.float32),
            dma((2, PIECES)),
            dma((2, PIECES)),
            dma((2, 3, PIECES)),
            dma((2, 3, PIECES)),
            dma((2,)),
            dma((2, slots)),
            pltpu.VMEM(attended.shape, jnp.bfloat16),
            pltpu.VMEM(w_out.shape, jnp.bfloat16),
            dma((2,)),
        ],
        compiler_params=pltpu.CompilerParams(
            collective_id=1, has_side_effects=True, vmem_limit_bytes=LIMIT
        ),
        name="project_scatter",
    )(attended, w_out, long_mix, long_stat, near_mix, near_stat)


def on_device(
    tokens,
    norm_gain,
    w_query,
    w_key,
    w_value,
    w_out,
    long_cache,
    short_cache,
    slot_owner,
    new_len,
    cache_len,
):
    owner = slot_owner[None, :]
    queries, here, before, earlier_slots, earlier_owner, lead, request, begin = gather_project(
        tokens.reshape(2, LEAD, tokens.shape[1]),
        norm_gain[None, :],
        w_query,
        w_key,
        w_value,
        new_len,
        cache_len,
        short_cache,
        owner,
    )
    attended, near_mix, near_stat, long_mix, long_stat = local_attention(
        begin,
        queries,
        before,
        here,
        earlier_slots,
        short_cache,
        earlier_owner,
        owner,
        request,
        lead,
        long_cache,
    )
    return project_scatter(attended, w_out, long_mix, long_stat, near_mix, near_stat)


def solution(mesh):
    placed = (
        P(("seq", "head"), None),
        P(),
        P(None, "head"),
        P(None, "head"),
        P(None, "head"),
        P("head", None),
        P(None, "seq", "head"),
        P(None, "seq", "head"),
        P("seq"),
        P(),
        P(),
    )
    return jax.shard_map(
        on_device, mesh=mesh, in_specs=placed, out_specs=P(("seq", "head"), None), check_vma=False
    )
```

```python
import math

import jax
import jax.numpy as jnp
from jax import lax
from jax.experimental import pallas as pl
from jax.experimental.pallas import tpu as pltpu
from jax.sharding import PartitionSpec as P

HD = 128
LEAD = 64
THETA_LOG = math.log(500000.0)
SCALE = 1.0 / math.sqrt(HD)
LOW = -1e30


def normalize(tokens, norm_gain):
    values = tokens.astype(jnp.float32)
    mean_square = jnp.mean(values * values, axis=-1, keepdims=True)
    return (values * lax.rsqrt(mean_square + 1e-05) * norm_gain).astype(jnp.bfloat16)


def dot32(a, b):
    return jnp.dot(a, b, preferred_element_type=jnp.float32)


def dot_t(a, b):
    return lax.dot_general(a, b, (((1,), (1,)), ((), ())), preferred_element_type=jnp.float32)


MESH = pl.DeviceIdType.MESH
LIMIT = 60 * 1024 * 1024
Z = 8
Y = 4
LONG_ROWS = 1024
PARTS = 4
UNITS = [(0, 0), (0, 1), (1, 0), (3, 0), (1, 1), (2, 0), (2, 1), (3, 1)]
SLOT = {unit: number for number, unit in enumerate(UNITS)}


def place():
    seq = lax.axis_index("seq")
    head = lax.axis_index("head")
    return seq, head, head // 2, lax.rem(head, 2)


def pick(number, table):
    value = jnp.int32(table[0])
    for at, entry in enumerate(table):
        value = jnp.where(number == at, jnp.int32(entry), value)
    return value


def greet(device):
    pl.semaphore_signal(
        pltpu.get_barrier_semaphore(), inc=1, device_id=device, device_id_type=MESH
    )


def token_facts(seq, new_len_ref, cache_len_ref, request_ref, begin_ref, place_ref):
    number = new_len_ref.shape[0]
    shape = request_ref.shape
    rows = shape[0] * shape[1]
    token = (
        seq * rows
        + lax.broadcasted_iota(jnp.int32, shape, 0) * shape[1]
        + lax.broadcasted_iota(jnp.int32, shape, 1)
    )

    def step(at, carry):
        start, request, begin, cached = carry
        passed = token >= start
        return (
            start + new_len_ref[at],
            jnp.where(passed, at, request),
            jnp.where(passed, start, begin),
            jnp.where(passed, cache_len_ref[at], cached),
        )

    zero = jnp.zeros(shape, jnp.int32)
    _, request, begin, cached = lax.fori_loop(
        0, number, step, (jnp.int32(LEAD), zero + number, zero, zero)
    )
    lead = request == number
    long_len = lax.axis_size("seq") * LONG_ROWS
    position = jnp.where(lead, token + long_len, token - begin + cached)
    place_ref[...] = position.astype(jnp.float32)
    request_ref[...] = request
    begin_ref[...] = jnp.where(lead, rows, jnp.maximum(begin - (seq - 1) * rows, 0))


def gather_kernel(
    tokens_ref,
    gain_ref,
    wq_hbm,
    wk_hbm,
    wv_hbm,
    new_len_ref,
    cache_len_ref,
    slots_ref,
    owner_ref,
    q_ref,
    kv_ref,
    before_ref,
    slots_before_ref,
    owner_before_ref,
    lead_ref,
    request_ref,
    begin_ref,
    normed_ref,
    wq_ref,
    wkv_ref,
    table_ref,
    place_ref,
    held,
    ring_send,
    ring_recv,
    pair_send,
    pair_recv,
    kv_send,
    kv_recv,
    slot_send,
    slot_recv,
    lead_send,
    lead_recv,
    weight_sem,
):
    seq, head, y, core = place()
    weights = [
        pltpu.make_async_copy(wk_hbm, wkv_ref.at[:, pl.ds(0, HD)], weight_sem.at[0]),
        pltpu.make_async_copy(wv_hbm, wkv_ref.at[:, pl.ds(HD, HD)], weight_sem.at[1]),
        pltpu.make_async_copy(wq_hbm, wq_ref, weight_sem.at[2]),
    ]
    for copy in weights:
        copy.start()
    n_seq = lax.axis_size("seq")
    x, z = seq // Z, lax.rem(seq, Z)
    way = 1 - 2 * core
    right = (seq, lax.rem(y + way + Y, Y) * 2 + core)
    left = (seq, lax.rem(y - way + Y, Y) * 2 + core)
    pair = (seq, head + way)
    following = (lax.rem(seq + 1, n_seq), head)
    previous = (lax.rem(seq + n_seq - 1, n_seq), head)
    heads = q_ref.shape[0]
    half = held.shape[2]

    for device in (right, left, pair, following, previous):
        greet(device)

    @pl.when(seq == 0)
    def _():
        for to in range(1, Z):
            greet((to, head))

    @pl.when(x == 0)
    def _():
        for to in range(1, n_seq // Z):
            greet((to * Z + z, head))

    @pl.when((x == 0) & (z > 0))
    def _():
        greet((0, head))

    @pl.when(x > 0)
    def _():
        greet((z, head))

    for later in range(2):
        normed_ref[later] = normalize(tokens_ref[later], gain_ref[...])
        held[SLOT[(0, later)], core] = normed_ref[later]

    barrier = pltpu.get_barrier_semaphore()
    others = n_seq // Z - 1

    @pl.when(seq == 0)
    def _():
        pl.semaphore_wait(barrier, 5 + Z - 1 + others)

    @pl.when((x == 0) & (z > 0))
    def _():
        pl.semaphore_wait(barrier, 5 + 1 + others)

    @pl.when(x > 0)
    def _():
        pl.semaphore_wait(barrier, 5 + 1)

    def split(source):
        size = half // PARTS
        return [source.at[pl.ds(part * size, size), :] for part in range(PARTS)]

    def ring(number, source, to, unit):
        slot = SLOT[unit]
        return [
            pltpu.make_async_remote_copy(
                src_ref=here,
                dst_ref=there,
                send_sem=ring_send.at[number, part],
                recv_sem=ring_recv.at[slot, part],
                device_id=to,
                device_id_type=MESH,
            )
            for part, (here, there) in enumerate(zip(split(source), split(held.at[slot, core])))
        ]

    def mine(unit):
        return held.at[SLOT[unit], core]

    def to_pair(unit):
        slot = SLOT[unit]
        source = normed_ref.at[unit[1]] if unit[0] == 0 else mine(unit)
        return [
            pltpu.make_async_remote_copy(
                src_ref=here,
                dst_ref=there,
                send_sem=pair_send.at[slot, part],
                recv_sem=pair_recv.at[slot, part],
                device_id=pair,
                device_id_type=MESH,
            )
            for part, (here, there) in enumerate(zip(split(source), split(held.at[slot, core])))
        ]

    def start(copies):
        for copy in copies:
            copy.start()

    def await_pair(unit):
        for copy in pairs[unit]:
            copy.wait_recv()

    def take_on(number, unit, further=None):
        for part in range(PARTS):
            rings[number][part].wait_recv()
            if further is not None:
                rings[further][part].start()
            pairs[unit][part].start()

    rings = [
        ring(0, normed_ref.at[0], right, (1, 0)),
        ring(1, normed_ref.at[0], left, (3, 0)),
        ring(2, normed_ref.at[1], right, (1, 1)),
        ring(3, mine((1, 0)), right, (2, 0)),
        ring(4, mine((1, 1)), right, (2, 1)),
        ring(5, mine((2, 1)), right, (3, 1)),
    ]
    pairs = {unit: to_pair(unit) for unit in UNITS}
    side = [
        pltpu.make_async_remote_copy(
            src_ref=source,
            dst_ref=target,
            send_sem=slot_send.at[number],
            recv_sem=slot_recv.at[number],
            device_id=following,
            device_id_type=MESH,
        )
        for number, (source, target) in enumerate(
            [(slots_ref, slots_before_ref), (owner_ref, owner_before_ref)]
        )
    ]

    def lead_copy(number, to):
        return pltpu.make_async_remote_copy(
            src_ref=lead_ref,
            dst_ref=lead_ref,
            send_sem=lead_send.at[number],
            recv_sem=lead_recv,
            device_id=(to, head),
            device_id_type=MESH,
        )

    along_z = [lead_copy(to - 1, jnp.int32(to)) for to in range(1, Z)]
    along_x = [lead_copy(Z - 2 + to, to * Z + z) for to in range(1, n_seq // Z)]

    def row_starts(number):
        distance = pick(number, [unit[0] for unit in UNITS])
        later = pick(number, [unit[1] for unit in UNITS])
        first = lax.rem(y - distance + Y, Y) * (4 * half) + later * half
        second = lax.rem(y + distance, Y) * (4 * half) + 2 * half + later * half
        return pl.multiple_of(first, half), pl.multiple_of(second, half)

    def kv_copies(number):
        return [
            pltpu.make_async_remote_copy(
                src_ref=kv_ref.at[:, pl.ds(first, half), :],
                dst_ref=before_ref.at[:, pl.ds(first, half), :],
                send_sem=kv_send.at[2 * number + part],
                recv_sem=kv_recv.at[2 * number + part],
                device_id=following,
                device_id_type=MESH,
            )
            for part, first in enumerate(row_starts(number))
        ]

    start(rings[0])
    start(pairs[(0, 0)])
    start(rings[1])
    start(rings[2])
    start(pairs[(0, 1)])
    for copy in side:
        copy.start()

    token_facts(seq, new_len_ref, cache_len_ref, request_ref, begin_ref, place_ref)
    half_head = HD // 2
    lane = lax.broadcasted_iota(jnp.int32, (HD, HD), 1)
    entry = jnp.where(lane < half_head, lane, lane - half_head)
    frequency = jnp.exp(entry.astype(jnp.float32) * (-2.0 * THETA_LOG / HD))

    @pl.loop(0, place_ref.shape[0])
    def _(number):
        spread = jnp.broadcast_to(place_ref[pl.ds(number, 1), :], (HD, HD))
        angle = jnp.transpose(spread) * frequency
        at = pl.multiple_of(number * HD, HD)
        table_ref[pl.ds(at, HD), :] = jnp.where(lane < half_head, jnp.cos(angle), jnp.sin(angle))

    for copy in weights:
        copy.wait()
    def event_0():
        await_pair((0, 0))

    def event_1():
        await_pair((0, 1))

    def event_2():
        take_on(0, (1, 0), 3)
        await_pair((1, 0))

    def event_3():
        take_on(1, (3, 0))
        take_on(2, (1, 1), 4)
        await_pair((3, 0))

    def event_4():
        await_pair((1, 1))

    def event_5():
        take_on(3, (2, 0))
        await_pair((2, 0))

    def event_6():
        @pl.when(seq == 0)
        def _():
            lead_ref[...] = q_ref[:, pl.ds(0, LEAD), :]
            start(along_z)
            start(along_x)

        take_on(4, (2, 1), 5)
        await_pair((2, 1))

    def event_7():
        take_on(5, (3, 1))

        @pl.when((x == 0) & (z > 0))
        def _():
            along_z[0].wait_recv()
            start(along_x)

        await_pair((3, 1))

    events = [event_0, event_1, event_2, event_3, event_4, event_5, event_6, event_7]

    @pl.loop(0, len(UNITS))
    def _(number):
        for at, event in enumerate(events):
            pl.when(number == at)(event)
        block = held[number].reshape(2 * half, held.shape[3])
        starts = row_starts(number)
        table = jnp.concatenate([table_ref[pl.ds(first, half), :] for first in starts], axis=0)
        swapped = pltpu.roll(table, HD // 2, 1)
        low = lax.broadcasted_iota(jnp.int32, table.shape, 1) < HD // 2
        cosine = jnp.where(low, table, swapped)
        sine = jnp.where(low, -swapped, table)

        def turned(product):
            return (product * cosine + pltpu.roll(product, HD // 2, 1) * sine).astype(jnp.bfloat16)

        def put(ref, at, rows):
            for part, first in enumerate(starts):
                ref[at, pl.ds(first, half), :] = rows[part * half : (part + 1) * half]

        both = dot32(block, wkv_ref[...])
        put(kv_ref, 0, turned(both[:, :HD]))
        put(kv_ref, 1, both[:, HD:].astype(jnp.bfloat16))
        product = dot32(block, wq_ref[...])
        start(kv_copies(number))
        for at in range(heads):
            put(q_ref, at, turned(product[:, at * HD : (at + 1) * HD]))

    @pl.loop(0, len(UNITS))
    def _(number):
        for copy in kv_copies(number):
            copy.wait_recv()
            copy.wait_send()

    for copy in sum(rings, []) + sum(pairs.values(), []):
        copy.wait_send()
    for copy in side:
        copy.wait_recv()
        copy.wait_send()

    @pl.when(seq == 0)
    def _():
        for copy in along_z:
            copy.wait_send()

    @pl.when(x == 0)
    def _():
        for copy in along_x:
            copy.wait_send()

    @pl.when(x > 0)
    def _():
        along_x[0].wait_recv()


def gather_project(tokens, gain, w_query, w_key, w_value, new_len, cache_len, slots, owner):
    half, width = tokens.shape[1:]
    rows = 2 * half * lax.axis_size("head")
    heads = w_query.shape[1] // HD
    vmem = pl.BlockSpec(memory_space=pltpu.VMEM)
    smem = pl.BlockSpec(memory_space=pltpu.SMEM)
    hbm = pl.BlockSpec(memory_space=pl.ANY)
    dma = pltpu.SemaphoreType.DMA
    shape = jax.ShapeDtypeStruct
    facts = (rows // HD, HD)
    return pl.pallas_call(
        gather_kernel,
        in_specs=[vmem, vmem, hbm, hbm, hbm, smem, smem, vmem, vmem],
        out_specs=[vmem] * 8,
        out_shape=[
            shape((heads, rows, HD), jnp.bfloat16),
            shape((2, rows, HD), jnp.bfloat16),
            shape((2, rows, HD), jnp.bfloat16),
            shape(slots.shape, jnp.bfloat16),
            shape(owner.shape, jnp.int32),
            shape((heads, LEAD, HD), jnp.bfloat16),
            shape(facts, jnp.int32),
            shape(facts, jnp.int32),
        ],
        scratch_shapes=[
            pltpu.VMEM((2, half, width), jnp.bfloat16),
            pltpu.VMEM(w_query.shape, jnp.bfloat16),
            pltpu.VMEM((width, 2 * HD), jnp.bfloat16),
            pltpu.VMEM((rows, HD), jnp.float32),
            pltpu.VMEM(facts, jnp.float32),
            pltpu.VMEM((len(UNITS), 2, half, width), jnp.bfloat16),
            dma((6, PARTS)),
            dma((len(UNITS), PARTS)),
            dma((len(UNITS), PARTS)),
            dma((len(UNITS), PARTS)),
            dma((2 * len(UNITS),)),
            dma((2 * len(UNITS),)),
            dma((2,)),
            dma((2,)),
            dma((Z + 2,)),
            dma,
            dma((3,)),
        ],
        compiler_params=pltpu.CompilerParams(
            collective_id=0, has_side_effects=True, vmem_limit_bytes=LIMIT
        ),
        name="gather_project",
    )(tokens, gain, w_query, w_key, w_value, new_len, cache_len, slots, owner)


def local_kernel(
    begin_smem,
    q_ref,
    before_ref,
    here_ref,
    slot_before_ref,
    slot_here_ref,
    owner_before_ref,
    owner_here_ref,
    request_ref,
    begin_ref,
    lead_ref,
    cache_ref,
    out_ref,
    near_mix_ref,
    near_stat_ref,
    long_mix_ref,
    long_stat_ref,
    window,
    owners,
    top_ref,
    sum_ref,
    mix_ref,
):
    step = pl.program_id(0)
    rows = here_ref.shape[1]
    heads, tile, _ = q_ref.shape
    chunk = 2 * tile

    @pl.when(step == 0)
    def _():
        window[:, pl.ds(0, tile)] = jnp.zeros((2, tile, HD), jnp.bfloat16)
        window[:, pl.ds(tile, rows)] = before_ref[...]
        window[:, pl.ds(tile + rows, rows)] = here_ref[...]
        for at, ref in enumerate((owner_before_ref, owner_here_ref)):
            spread = jnp.broadcast_to(ref[...].astype(jnp.float32), (tile, ref.shape[1]))
            owners[at] = jnp.transpose(spread).astype(jnp.int32)
        long_state(lead_ref, cache_ref, long_mix_ref, long_stat_ref)

    request = request_ref[pl.ds(step, 1), :]
    begin = begin_ref[pl.ds(step, 1), :]
    down = lax.broadcasted_iota(jnp.int32, (chunk, tile), 0)
    index = rows + step * tile + lax.broadcasted_iota(jnp.int32, (1, tile), 1)
    queries = q_ref[...].reshape(heads * tile, HD)

    def take(keys, values, valid, fresh):
        scores = dot_t(keys, queries) * SCALE
        scores = jnp.where(jnp.concatenate([valid] * heads, axis=1), scores, LOW)
        top = jnp.max(scores, axis=0, keepdims=True)
        if not fresh:
            old = top_ref[...]
            top = jnp.maximum(top, old)
            keep = jnp.exp(old - top)
        weights = jnp.exp(scores - top)
        total = jnp.sum(weights, axis=0, keepdims=True)
        mixed = lax.dot_general(
            values,
            weights.astype(jnp.bfloat16),
            (((0,), (0,)), ((), ())),
            preferred_element_type=jnp.float32,
        )
        top_ref[...] = top
        if fresh:
            sum_ref[...] = total
            mix_ref[...] = mixed
        else:
            sum_ref[...] = sum_ref[...] * keep + total
            mix_ref[...] = mix_ref[...] * keep + mixed

    end = rows + (step + 1) * tile

    def new_chunk(number):
        key = end - (number + 1) * chunk
        key_at = key + down
        valid = (key_at >= begin) & (key_at <= index)
        at = pl.multiple_of(key + tile, tile)
        return window[0, pl.ds(at, chunk), :], window[1, pl.ds(at, chunk), :], valid

    def join(*parts):
        return [jnp.concatenate(pair, axis=0) for pair in zip(*parts)]

    first = begin_smem[step, 0]
    take(*join(new_chunk(0), (slot_here_ref[0], slot_here_ref[1], owners[1] == request)), True)

    @pl.loop(1, (end - first + chunk - 1) // chunk)
    def _(number):
        take(*new_chunk(number), False)

    @pl.when(first < rows)
    def _():
        take(slot_before_ref[0], slot_before_ref[1], owners[0] == request, False)

    mixed = mix_ref[...] / sum_ref[...]
    for head in range(heads):
        span = slice(head * tile, (head + 1) * tile)
        out_ref[:, span] = jnp.transpose(mixed[:, span]).astype(jnp.bfloat16)

    @pl.when(step == 0)
    def _():
        def leads(ref):
            parts = [ref[:, head * tile : head * tile + LEAD] for head in range(heads)]
            return jnp.concatenate(parts + parts[-1:], axis=1)

        near_mix_ref[...] = leads(mix_ref)
        near_stat_ref[...] = jnp.zeros_like(near_stat_ref)
        near_stat_ref[0:1, :] = leads(top_ref)
        near_stat_ref[1:2, :] = leads(sum_ref)


def long_state(q_ref, cache_ref, mix_ref, stat_ref):
    heads = q_ref.shape[0]
    queries = jnp.concatenate([q_ref[at] for at in range(heads)] + [q_ref[heads - 1]], axis=0)
    scores = dot_t(cache_ref[0], queries) * SCALE
    top = jnp.max(scores, axis=0, keepdims=True)
    weights = jnp.exp(scores - top)
    mixed = lax.dot_general(
        cache_ref[1],
        weights.astype(jnp.bfloat16),
        (((0,), (0,)), ((), ())),
        preferred_element_type=jnp.float32,
    )
    mix_ref[...] = mixed.astype(jnp.bfloat16)
    stat_ref[...] = jnp.zeros_like(stat_ref)
    stat_ref[0:1, :] = top
    stat_ref[1:2, :] = jnp.sum(weights, axis=0, keepdims=True)


def local_attention(
    begin, queries, before, here, slot_before, slot_here, owner_before, owner_here, request, lead, cache
):
    heads, rows, _ = queries.shape
    tile = HD
    columns = (heads + 1) * LEAD

    def whole(array):
        return pl.BlockSpec(array.shape, lambda i, first: (0,) * len(array.shape))

    shape = jax.ShapeDtypeStruct
    near_mix = shape((HD, columns), jnp.float32)
    long_mix = shape((HD, columns), jnp.bfloat16)
    long_stat = shape((8, columns), jnp.float32)
    kept = [before, here, slot_before, slot_here, owner_before, owner_here, request, begin, lead, cache]
    return pl.pallas_call(
        local_kernel,
        grid_spec=pltpu.PrefetchScalarGridSpec(
            num_scalar_prefetch=1,
            grid=(rows // tile,),
            in_specs=[pl.BlockSpec((heads, tile, HD), lambda i, first: (0, i, 0))]
            + [whole(array) for array in kept],
            out_specs=[pl.BlockSpec((tile, heads * HD), lambda i, first: (i, 0))]
            + [whole(array) for array in (near_mix, long_stat, long_mix, long_stat)],
            scratch_shapes=[
                pltpu.VMEM((2, tile + 2 * rows, HD), jnp.bfloat16),
                pltpu.VMEM((2, slot_here.shape[1], tile), jnp.int32),
                pltpu.VMEM((1, heads * tile), jnp.float32),
                pltpu.VMEM((1, heads * tile), jnp.float32),
                pltpu.VMEM((HD, heads * tile), jnp.float32),
            ],
        ),
        out_shape=[shape((rows, heads * HD), jnp.bfloat16), near_mix, long_stat, long_mix, long_stat],
        name="local_attention",
    )(begin, queries, *kept)


def merge(into, top, total, part, part_top, part_total):
    highest = jnp.maximum(top, part_top)
    keep, add = jnp.exp(top - highest), jnp.exp(part_top - highest)
    return into * keep + part * add, highest, total * keep + part_total * add


PIECES = 4


def scatter_kernel(
    attended_hbm,
    w_hbm,
    long_mix_ref,
    long_stat_ref,
    near_mix_ref,
    near_stat_ref,
    out_ref,
    pair_out,
    pair_in,
    own,
    ring_out,
    ring_in,
    mix_out,
    stat_out,
    mix_in,
    stat_in,
    pair_send,
    pair_recv,
    ring_send,
    ring_recv,
    sends,
    recvs,
    attended_ref,
    w_ref,
    load_sem,
):
    seq, head, y, core = place()
    loads = [
        pltpu.make_async_copy(attended_hbm, attended_ref, load_sem.at[0]),
        pltpu.make_async_copy(w_hbm, w_ref, load_sem.at[1]),
    ]
    for copy in loads:
        copy.start()
    n_x = lax.axis_size("seq") // Z
    x, z = seq // Z, lax.rem(seq, Z)
    way = 1 - 2 * core
    right = (seq, lax.rem(y + way + Y, Y) * 2 + core)
    left = (seq, lax.rem(y - way + Y, Y) * 2 + core)
    pair = (seq, head + way)
    half = ring_out.shape[2]
    heads = w_ref.shape[0] // HD
    width = w_ref.shape[1] // PIECES
    barrier = pltpu.get_barrier_semaphore()

    for device in (right, left, pair):
        greet(device)

    @pl.when(z > 0)
    def _():
        greet((x * Z, head))
        pl.semaphore_wait(barrier, 3 + 1)

    @pl.when((z == 0) & (x > 0))
    def _():
        for at in range(1, Z):
            greet((x * Z + at, head))
        greet((0, head))
        pl.semaphore_wait(barrier, 3 + Z)

    @pl.when(seq == 0)
    def _():
        for at in range(1, Z):
            greet((at, head))
        for at in range(1, n_x):
            greet((at * Z, head))
        pl.semaphore_wait(barrier, 3 + Z - 1 + n_x - 1)

    def columns(piece):
        return pl.ds(piece * width, width)

    def rows_of(chip, of_core, later):
        return attended_ref[pl.ds(pl.multiple_of(chip * (4 * half) + of_core * (2 * half) + later * half, half), half), :]

    def stack(later):
        parts = [rows_of(lax.rem(y - k * way + 2 * Y * 2, Y), 1 - core, later) for k in range(Y)]
        parts += [rows_of(lax.rem(y + k * way + 2 * Y * 2, Y), core, later) for k in range(Y)]
        return jnp.concatenate(parts, axis=0)

    def pair_copy(later, number):
        if later:
            at = (later, slice(None), columns(number))
        else:
            at = (later, pl.ds(number * half, half), slice(None))
        return pltpu.make_async_remote_copy(
            src_ref=pair_out.at[at],
            dst_ref=pair_in.at[at],
            send_sem=pair_send.at[later, number],
            recv_sem=pair_recv.at[later, number],
            device_id=pair,
            device_id_type=MESH,
        )

    def ring_copy(later, step, piece):
        return pltpu.make_async_remote_copy(
            src_ref=ring_out.at[later, step, :, columns(piece)],
            dst_ref=ring_in.at[later, step, :, columns(piece)],
            send_sem=ring_send.at[later, step, piece],
            recv_sem=ring_recv.at[later, step, piece],
            device_id=left if (later, step) == (0, 2) else right,
            device_id_type=MESH,
        )

    def project(rows, later, piece):
        product = dot32(rows, w_ref[:, columns(piece)]).astype(jnp.bfloat16)
        pair_out[later, :, columns(piece)] = product[: Y * half]
        own[later, :, columns(piece)] = product[Y * half :]

    def chip_sum(later, k, piece):
        rows = pl.ds(k * half, half)
        return own[later, rows, columns(piece)].astype(jnp.float32) + pair_in[
            later, rows, columns(piece)
        ].astype(jnp.float32)

    def arrived(later, step, piece):
        ring_copy(later, step, piece).wait_recv()
        return ring_in[later, step, :, columns(piece)].astype(jnp.float32)

    def pass_on(later, step, piece, value):
        ring_out[later, step, :, columns(piece)] = value.astype(jnp.bfloat16)
        ring_copy(later, step, piece).start()

    def first_hop(piece):
        pair_copy(1, piece).wait_recv()
        pass_on(1, 0, piece, chip_sum(1, 3, piece))

    def keep_state(mixed, top, total):
        mix_out[...] = mixed.astype(jnp.bfloat16)
        stat_out[0:1, :] = top
        stat_out[1:2, :] = total

    def state_copies(slot, to, sources):
        return [
            pltpu.make_async_remote_copy(
                src_ref=source,
                dst_ref=target.at[slot],
                send_sem=sends.at[number],
                recv_sem=recvs.at[number, slot],
                device_id=(to, head),
                device_id_type=MESH,
            )
            for number, (source, target) in enumerate(zip(sources, (mix_in, stat_in)))
        ]

    def collect(slots, sources):
        mix, stat = sources
        state = (mix[...].astype(jnp.float32), stat[0:1, :], stat[1:2, :])
        for slot in slots:
            for copy in state_copies(slot, jnp.int32(0), sources):
                copy.wait_recv()
            state = merge(
                *state,
                mix_in[slot].astype(jnp.float32),
                stat_in[slot, 0:1, :],
                stat_in[slot, 1:2, :],
            )
        return state

    computed = (long_mix_ref, long_stat_ref)
    merged = (mix_out, stat_out)
    for at in range(1, Z):
        @pl.when(z == at)
        def _():
            for copy in state_copies(at - 1, x * Z, computed):
                copy.start()

    for copy in loads:
        copy.wait()
    rows = stack(1)
    for piece in range(PIECES):
        project(rows, 1, piece)
        pair_copy(1, piece).start()
        if piece:
            first_hop(piece - 1)
    first_hop(PIECES - 1)

    rows = stack(0)
    for piece in range(PIECES):
        project(rows, 0, piece)

    lead_block = jnp.where(seq == 0, lax.rem(Y - y, Y), -1)
    for k in range(Y):
        @pl.when((core == 0) | (lead_block != k))
        def _():
            pair_copy(0, k).start()

    for piece in range(PIECES):
        pass_on(1, 1, piece, chip_sum(1, 2, piece) + arrived(1, 0, piece))

    @pl.when(z == 0)
    def _():
        stat_out[...] = jnp.zeros_like(stat_out)
        keep_state(*collect(range(Z - 1), computed))

    for at in range(1, n_x):
        @pl.when((z == 0) & (x == at))
        def _():
            for copy in state_copies(Z - 2 + at, jnp.int32(0), merged):
                copy.start()

    for piece in range(PIECES):
        pass_on(1, 2, piece, chip_sum(1, 1, piece) + arrived(1, 1, piece))

    def early_hop(step, k):
        pair_copy(0, k).wait_recv()
        for piece in range(PIECES):
            pass_on(0, step, piece, chip_sum(0, k, piece))

    for step, k in ((0, 2), (2, 3)):
        @pl.when((core == 1) | (lead_block != k))
        def _():
            early_hop(step, k)

    @pl.when(seq == 0)
    def _():
        near = (near_mix_ref[...], near_stat_ref[0:1, :], near_stat_ref[1:2, :])
        mixed, _, total = merge(*near, *collect(range(Z - 1, Z + n_x - 2), merged))
        mixed = jnp.transpose(mixed / total).astype(jnp.bfloat16)
        parts = [mixed[at * LEAD : (at + 1) * LEAD] for at in range(heads)]
        lead_rows = jnp.concatenate(parts, axis=1)
        for piece in range(PIECES):
            product = dot32(lead_rows, w_ref[:, columns(piece)]).astype(jnp.bfloat16)

            @pl.when(core == 0)
            def _():
                at = pl.multiple_of(lax.rem(Y - y, Y) * half, half)
                own[0, pl.ds(at, half), columns(piece)] = product

            @pl.when(core == 1)
            def _():
                at = pl.multiple_of(lax.rem(Y - y, Y) * half, half)
                pair_out[0, pl.ds(at, half), columns(piece)] = product

    for k in range(Y):
        @pl.when((core == 1) & (lead_block == k))
        def _():
            pair_copy(0, k).start()

    for step, k in ((0, 2), (2, 3)):
        @pl.when((core == 0) & (lead_block == k))
        def _():
            early_hop(step, k)

    for piece in range(PIECES):
        value = chip_sum(1, 0, piece) + arrived(1, 2, piece)
        out_ref[pl.ds(half, half), columns(piece)] = value.astype(jnp.bfloat16)
    pair_copy(0, 1).wait_recv()
    for piece in range(PIECES):
        pass_on(0, 1, piece, chip_sum(0, 1, piece) + arrived(0, 0, piece))
    pair_copy(0, 0).wait_recv()
    for piece in range(PIECES):
        value = chip_sum(0, 0, piece) + arrived(0, 2, piece) + arrived(0, 1, piece)
        out_ref[pl.ds(0, half), columns(piece)] = value.astype(jnp.bfloat16)

    for later in range(2):
        for piece in range(PIECES):
            pair_copy(later, piece).wait_send()
            for step in range(3):
                ring_copy(later, step, piece).wait_send()

    @pl.when(seq > 0)
    def _():
        for copy in state_copies(0, jnp.int32(0), merged):
            copy.wait_send()


def project_scatter(attended, w_out, long_mix, long_stat, near_mix, near_stat):
    rows, inner = attended.shape
    width = w_out.shape[1]
    half = LEAD
    slots = Z - 1 + 3
    queries = long_mix.shape[1]
    vmem = pl.BlockSpec(memory_space=pltpu.VMEM)
    dma = pltpu.SemaphoreType.DMA
    return pl.pallas_call(
        scatter_kernel,
        in_specs=[pl.BlockSpec(memory_space=pl.ANY)] * 2 + [vmem] * 4,
        out_specs=vmem,
        out_shape=jax.ShapeDtypeStruct((2 * half, width), jnp.bfloat16),
        scratch_shapes=[
            pltpu.VMEM((2, Y * half, width), jnp.bfloat16),
            pltpu.VMEM((2, Y * half, width), jnp.bfloat16),
            pltpu.VMEM((2, Y * half, width), jnp.bfloat16),
            pltpu.VMEM((2, 3, half, width), jnp.bfloat16),
            pltpu.VMEM((2, 3, half, width), jnp.bfloat16),
            pltpu.VMEM((HD, queries), jnp.bfloat16),
            pltpu.VMEM((8, queries), jnp.float32),
            pltpu.VMEM((slots, HD, queries), jnp.bfloat16),
            pltpu.VMEM((slots, 8, queries), jnp.float32),
            dma((2, PIECES)),
            dma((2, PIECES)),
            dma((2, 3, PIECES)),
            dma((2, 3, PIECES)),
            dma((2,)),
            dma((2, slots)),
            pltpu.VMEM(attended.shape, jnp.bfloat16),
            pltpu.VMEM(w_out.shape, jnp.bfloat16),
            dma((2,)),
        ],
        compiler_params=pltpu.CompilerParams(
            collective_id=1, has_side_effects=True, vmem_limit_bytes=LIMIT
        ),
        name="project_scatter",
    )(attended, w_out, long_mix, long_stat, near_mix, near_stat)


def on_device(
    tokens,
    norm_gain,
    w_query,
    w_key,
    w_value,
    w_out,
    long_cache,
    short_cache,
    slot_owner,
    new_len,
    cache_len,
):
    owner = slot_owner[None, :]
    queries, here, before, earlier_slots, earlier_owner, lead, request, begin = gather_project(
        tokens.reshape(2, LEAD, tokens.shape[1]),
        norm_gain[None, :],
        w_query,
        w_key,
        w_value,
        new_len,
        cache_len,
        short_cache,
        owner,
    )
    attended, near_mix, near_stat, long_mix, long_stat = local_attention(
        begin,
        queries,
        before,
        here,
        earlier_slots,
        short_cache,
        earlier_owner,
        owner,
        request,
        lead,
        long_cache,
    )
    return project_scatter(attended, w_out, long_mix, long_stat, near_mix, near_stat)


def solution(mesh):
    placed = (
        P(("seq", "head"), None),
        P(),
        P(None, "head"),
        P(None, "head"),
        P(None, "head"),
        P("head", None),
        P(None, "seq", "head"),
        P(None, "seq", "head"),
        P("seq"),
        P(),
        P(),
    )
    return jax.shard_map(
        on_device, mesh=mesh, in_specs=placed, out_specs=P(("seq", "head"), None), check_vma=False
    )
```
